256 devices in a mesh: case: 4 (over x), tile: 64 (over z, y, core).
Axes of the slice: x: 4, y: 4, z: 8, core: 2. Of those that a mesh axis runs over, the one named last changes fastest.
Arguments:
- forcing: bfloat16 [4, 1024, 512, 128], P('case', 'tile'), may hold values from -6 to 6
- permeability: float32 [4, 1024, 512], P('case', 'tile'), may hold values from 0.05 to 1
- merge_weights: int32 [4], P('case'), may hold values from 4 to 6
- start_codes: int32 [2, 256, 128], replicated, may hold values from -7 to 7
Outputs:
- basis: bfloat16 [4, 524288, 128], P('case', 'tile')
The draws below stay inside these ranges and needn't reach their ends.
All inputs are finite; a program needn't handle non-finite values.
Results may differ from the reference program's by a relative error of at most 0.018.
Values may be sent and summed in bfloat16 or wider, within the bound.
No kernel may reach another device: no remote copies, remote signals or barrier semaphores. Data moves between devices by JAX's collectives and lax.ppermute only.
A program may use at most 64 MiB of HBM per device.

```python
import math
import jax
import jax.numpy as jnp
from jax import lax

NY = 512
K = 128
STEPS = 3
LEVELS = 2
NCASE = 4
NX = 1024


def draw_forcing(key, part):
    shape = (NCASE, NX, NY, K)
    values = jax.random.truncated_normal(jax.random.fold_in(key, 13), -6.0, 6.0, shape, jnp.float32)
    return values.astype(jnp.bfloat16)


def with_ends(drawn, key, smallest, high):
    longest = drawn.shape.index(max(drawn.shape))
    spots = []
    for shift in (0, 1):
        where = [jax.random.randint(jax.random.fold_in(key, axis), (), 0, length) for axis, length in enumerate(drawn.shape)]
        where[longest] = (where[longest] + shift) % drawn.shape[longest]
        spots.append(tuple(where))
    return drawn.at[spots[0]].set(smallest).at[spots[1]].set(high)


def shard_levels(key, shape, cuts, least, top_value):
    def one(axis_at, parts):
        heights = jax.random.uniform(jax.random.fold_in(jax.random.fold_in(key, 6), axis_at), (parts,), jnp.float32, least / len(cuts), top_value / len(cuts))
        return jnp.repeat(jnp.exp(heights), shape[axis_at] // parts).reshape((-1,) + (1,) * (len(shape) - axis_at - 1))

    factor_of = one(*cuts[0])
    for cut in cuts[1:]:
        factor_of = factor_of * one(*cut)
    return factor_of


def setup_inputs(seed: int = 0) -> dict:
    seeds = jax.random.split(jax.random.key(seed), 5)
    return {
        "forcing": draw_forcing(jax.random.fold_in(seeds[4], 71), 0),
        "permeability": jnp.clip(jnp.exp(math.log(1.0) - 2.9957323 * jax.random.uniform(seeds[1], (NCASE, NX, NY), jnp.float32) ** shard_levels(seeds[1], (NCASE, NX, NY), ((0, 4), (1, 64)), -0.2, 0.2)), 0.05, 1.0),
        "merge_weights": with_ends(jax.random.randint(seeds[2], (NCASE,), 4, 7), jax.random.fold_in(seeds[2], 1), 4, 6).astype(jnp.int32),
        "start_codes": with_ends(jax.random.randint(seeds[3], (LEVELS, 2 * K, K), -7, 8), jax.random.fold_in(seeds[3], 1), -7, 7).astype(jnp.int32),
    }


def stencil_step(ext_field, ext_perm):
    wide_field = jnp.pad(ext_field, ((0, 0), (1, 1), (0, 0)))
    wide_perm = jnp.pad(ext_perm, ((0, 0), (1, 1)))
    center = ext_field[1:-1]
    perm_mid = ext_perm[1:-1]
    t_north = 0.5 * (perm_mid + ext_perm[2:])
    t_south = 0.5 * (perm_mid + ext_perm[:-2])
    t_east = 0.5 * (perm_mid + wide_perm[1:-1, 2:])
    t_west = 0.5 * (perm_mid + wide_perm[1:-1, :-2])
    flux = t_north[:, :, None] * (ext_field[2:] - center)
    flux = flux + t_south[:, :, None] * (ext_field[:-2] - center)
    flux = flux + t_east[:, :, None] * (wide_field[1:-1, 2:] - center)
    flux = flux + t_west[:, :, None] * (wide_field[1:-1, :-2] - center)
    return center + 0.24 * flux

def merge(own, other, start_code):
    cells = NX * NY
    stacked = jnp.concatenate([own, other], 1)
    gram = jnp.dot(stacked.T.astype(jnp.float32), stacked.astype(jnp.float32), preferred_element_type=jnp.float32)
    start = start_code.astype(jnp.float32)
    first = jnp.dot(gram, start, precision=lax.Precision.HIGHEST) / cells
    second = jnp.dot(gram, first, precision=lax.Precision.HIGHEST) / cells
    coeff = second.astype(jnp.bfloat16)
    compressed = jnp.dot(stacked.astype(jnp.float32), coeff.astype(jnp.float32), preferred_element_type=jnp.float32)
    inner = jnp.dot(compressed.T, compressed, precision=lax.Precision.HIGHEST)
    factor = jnp.linalg.cholesky(inner)
    solved = lax.linalg.triangular_solve(factor, compressed, left_side=False, lower=True, transpose_a=True)
    return (math.sqrt(cells) * solved).astype(jnp.bfloat16)

def reference(forcing, permeability, merge_weights, start_codes):
    bases = []
    for group in range(NCASE):
        field = forcing[group].astype(jnp.float32)
        ext_perm = jnp.pad(permeability[group], ((1, 1), (0, 0)))
        for step in range(STEPS):
            field = stencil_step(jnp.pad(field, ((1, 1), (0, 0), (0, 0))), ext_perm)
        weight = jnp.sqrt(merge_weights[group].astype(jnp.float32))
        bases.append((field * weight).astype(jnp.bfloat16).reshape(NX * NY, K))
    for level in range(LEVELS):
        updated = []
        for group in range(NCASE):
            other = group ^ 1 << level
            updated.append(merge(bases[group], bases[other], start_codes[level]))
        bases = updated
    return jnp.stack(bases)
```

```python
import math

import jax
import jax.numpy as jnp
from jax import lax
from jax.sharding import PartitionSpec as P

STEPS = 3
HI = lax.Precision.HIGHEST
BAR = lax.optimization_barrier


def place(index):
    return index // 8, (index // 2) % 4, index % 2


def at(z, y, core):
    return ((z % 8) * 4 + (y % 4)) * 2 + core


def tile_pairs(dz, dy, dcore, xor=False):
    pairs = []
    for source in range(64):
        z, y, core = place(source)
        where = at(z ^ dz, y ^ dy, core ^ dcore)
        pairs.append((source, where))
    return pairs


Y_GROUPS = [[at(z, y, core) for y in range(4)] for z in range(8) for core in range(2)]


def case_swap(value, apart):
    return lax.ppermute(value, "case", [(source, source ^ apart) for source in range(4)])


def tile_swap(value, dz, dy, dcore):
    return lax.ppermute(value, "tile", tile_pairs(dz, dy, dcore))


def extended(cells, width):
    head, tail = cells[:width], cells[cells.shape[0] - width :]
    up = [(i, i + 1) for i in range(63)]
    down = [(i + 1, i) for i in range(63)]
    return jnp.concatenate([lax.ppermute(tail, "tile", up), cells, lax.ppermute(head, "tile", down)], 0)


def stencil_step(field, perm):
    wide_field = jnp.pad(field, ((0, 0), (1, 1), (0, 0)))
    wide_perm = jnp.pad(perm, ((0, 0), (1, 1)))
    center = field[1:-1]
    mid = perm[1:-1]
    north = 0.5 * (mid + perm[2:])
    south = 0.5 * (mid + perm[:-2])
    east = 0.5 * (mid + wide_perm[1:-1, 2:])
    west = 0.5 * (mid + wide_perm[1:-1, :-2])
    flux = north[:, :, None] * (field[2:] - center)
    flux = flux + south[:, :, None] * (field[:-2] - center)
    flux = flux + east[:, :, None] * (wide_field[1:-1, 2:] - center)
    flux = flux + west[:, :, None] * (wide_field[1:-1, :-2] - center)
    return center + 0.24 * flux


def total(gram):
    core = lax.axis_index("tile") % 2
    halves = gram.reshape(2, -1, 128)
    own = lax.dynamic_index_in_dim(halves, core, 0, False)
    other = lax.dynamic_index_in_dim(halves, 1 - core, 0, False)
    part = own + tile_swap(other, 0, 0, 1)
    split = lax.all_to_all(part.reshape(4, -1, 128), "tile", 0, 0, axis_index_groups=Y_GROUPS)
    part = split.sum(0)
    for dz in (1, 2, 4):
        part = part + tile_swap(part, dz, 0, 0)
    for dx in (1, 2):
        part = part + case_swap(part, dx)
    whole = jnp.broadcast_to(part, (4,) + part.shape)
    whole = lax.all_to_all(whole, "tile", 0, 0, axis_index_groups=Y_GROUPS)
    own = whole.reshape(-1, 128)
    other = tile_swap(own, 0, 0, 1)
    first = jnp.where(core == 0, own, other)
    second = jnp.where(core == 0, other, own)
    return jnp.concatenate([first, second], 0).reshape(gram.shape)


def whitened(coeff, inner):
    factor = jnp.linalg.cholesky(inner)
    return lax.linalg.triangular_solve(factor, coeff, left_side=False, lower=True, transpose_a=True)


def dot(a, b):
    return jnp.dot(a, b, precision=HI)


PAIRS = [(0, 0), (1, 1), (2, 2), (3, 3), (0, 1), (2, 3), (0, 2), (0, 3), (1, 2), (1, 3)]


def per_device(forcing, permeability, merge_weights, start_codes):
    me = lax.axis_index("case")
    tile = lax.axis_index("tile")
    count = lax.axis_size("tile")
    rows = forcing.shape[1]
    ny = forcing.shape[2]
    cells = rows * count * ny
    field = extended(forcing[0], STEPS).astype(jnp.float32)
    perm = extended(permeability[0], STEPS)
    for step in range(STEPS):
        skip = STEPS - step
        field = stencil_step(field, perm[step : perm.shape[0] - step])
        row = tile * rows + jnp.arange(field.shape[0]) - (skip - 1)
        inside = (row >= 0) & (row < rows * count)
        field = jnp.where(inside[:, None, None], field, 0.0)
    weight = jnp.sqrt(merge_weights[0].astype(jnp.float32))
    snap = (field * weight).astype(jnp.bfloat16).reshape(4, -1, 128)
    snap = jnp.stack([lax.dynamic_index_in_dim(snap, me ^ j, 0, False) for j in range(4)])
    got = {(0, j): snap[j] for j in range(4)}
    for e in (2, 1, 3):
        got[e, 0] = case_swap(snap[e], e)
    quarter = jnp.stack([got[e, 0] for e in range(4)])
    late, quarter = BAR((snap, quarter))
    for j in (1, 2, 3):
        for e in (1, 2, 3):
            got[e, j] = case_swap(late[e ^ j], e)
    groups = jnp.stack([lax.dynamic_index_in_dim(quarter, me ^ k, 0, False) for k in range(4)])
    wide = jnp.concatenate([groups[k] for k in range(4)], 1)
    gram = lax.dot_general(wide, wide, (((0,), (0,)), ((), ())), preferred_element_type=jnp.float32)
    packed = jnp.stack([gram[a * 128 : a * 128 + 128, b * 128 : b * 128 + 128] for a, b in PAIRS])
    packed = total(packed)
    full = [[None] * 4 for _ in range(4)]
    for i, (a, b) in enumerate(PAIRS):
        full[a][b] = packed[i]
        full[b][a] = packed[i].T
    full = jnp.stack([jnp.stack(r) for r in full])
    near = jnp.stack([lax.dynamic_index_in_dim(full, me ^ e, 0, False) for e in range(4)])
    near = jnp.stack([lax.dynamic_index_in_dim(near, me ^ e, 1, False) for e in range(4)], 1)

    def joined(first, second):
        return jnp.concatenate(
            [jnp.concatenate([near[i, j] for j in second], 1) for i in first], 0
        )

    start = start_codes[0].astype(jnp.float32)
    maps = []
    for ids in ((0, 1), (2, 3)):
        part = joined(ids, ids)
        first = dot(part, start) / cells
        coeff = (dot(part, first) / cells).astype(jnp.bfloat16).astype(jnp.float32)
        inner = dot(coeff.T, dot(part, coeff))
        maps.append(math.sqrt(cells) * whitened(coeff, inner))
    cross = dot(maps[0].T, dot(joined((0, 1), (2, 3)), maps[1]))
    eye = cells * jnp.eye(128, dtype=jnp.float32)
    part = jnp.concatenate(
        [jnp.concatenate([eye, cross], 1), jnp.concatenate([cross.T, eye], 1)], 0
    )
    start = start_codes[1].astype(jnp.float32)
    first = dot(part, start) / cells
    coeff = (dot(part, first) / cells).astype(jnp.bfloat16).astype(jnp.float32)
    inner = dot(coeff.T, dot(part, coeff))
    last = math.sqrt(cells) * whitened(coeff, inner)
    mix = jnp.concatenate([dot(maps[0], last[:128]), dot(maps[1], last[128:])], 0)
    high = mix.astype(jnp.bfloat16)
    low = (mix - high.astype(jnp.float32)).astype(jnp.bfloat16)
    outs = []
    for j in range(4):
        stack = jnp.concatenate([got[e, j] for e in range(4)], 1)
        outs.append(
            jnp.dot(stack, high, preferred_element_type=jnp.float32)
            + jnp.dot(stack, low, preferred_element_type=jnp.float32)
        )
    outs = jnp.stack(outs).astype(jnp.bfloat16)
    outs = jnp.stack([lax.dynamic_index_in_dim(outs, me ^ q, 0, False) for q in range(4)])
    return outs.reshape(1, -1, 128)


def solution(mesh):
    placed = (P("case", "tile", None, None), P("case", "tile", None), P("case"), P())
    return jax.shard_map(
        per_device, mesh=mesh, in_specs=placed, out_specs=P("case", "tile", None), check_vma=False
    )
```

```python
import functools
import math

import jax
import jax.numpy as jnp
from jax import lax
from jax.experimental import pallas as pl
from jax.experimental.pallas import tpu as pltpu
from jax.sharding import PartitionSpec as P

STEPS = 3
BAR = lax.optimization_barrier


def place(index):
    return index // 8, (index // 2) % 4, index % 2


def at(z, y, core):
    return ((z % 8) * 4 + (y % 4)) * 2 + core


def tile_pairs(dz, dy, dcore, xor=False):
    pairs = []
    for source in range(64):
        z, y, core = place(source)
        where = at(z ^ dz, y ^ dy, core ^ dcore)
        pairs.append((source, where))
    return pairs


Y_GROUPS = [[at(z, y, core) for y in range(4)] for z in range(8) for core in range(2)]


def case_swap(value, apart):
    return lax.ppermute(value, "case", [(source, source ^ apart) for source in range(4)])


def tile_swap(value, dz, dy, dcore):
    return lax.ppermute(value, "tile", tile_pairs(dz, dy, dcore))


def extended(cells, width):
    head, tail = cells[:width], cells[cells.shape[0] - width :]
    up = [(i, i + 1) for i in range(63)]
    down = [(i + 1, i) for i in range(63)]
    return jnp.concatenate([lax.ppermute(tail, "tile", up), cells, lax.ppermute(head, "tile", down)], 0)


def stencil_step(field, perm):
    wide_field = jnp.pad(field, ((0, 0), (1, 1), (0, 0)))
    wide_perm = jnp.pad(perm, ((0, 0), (1, 1)))
    center = field[1:-1]
    mid = perm[1:-1]
    north = 0.5 * (mid + perm[2:])
    south = 0.5 * (mid + perm[:-2])
    east = 0.5 * (mid + wide_perm[1:-1, 2:])
    west = 0.5 * (mid + wide_perm[1:-1, :-2])
    flux = north[:, :, None] * (field[2:] - center)
    flux = flux + south[:, :, None] * (field[:-2] - center)
    flux = flux + east[:, :, None] * (wide_field[1:-1, 2:] - center)
    flux = flux + west[:, :, None] * (wide_field[1:-1, :-2] - center)
    return center + 0.24 * flux


def total(gram):
    core = lax.axis_index("tile") % 2
    halves = gram.reshape(2, -1, 128)
    own = lax.dynamic_index_in_dim(halves, core, 0, False)
    other = lax.dynamic_index_in_dim(halves, 1 - core, 0, False)
    part = own + tile_swap(other, 0, 0, 1)
    split = lax.all_to_all(part.reshape(4, -1, 128), "tile", 0, 0, axis_index_groups=Y_GROUPS)
    part = split.sum(0)
    for dz in (1, 2, 4):
        part = part + tile_swap(part, dz, 0, 0)
    for dx in (1, 2):
        part = part + case_swap(part, dx)
    whole = jnp.broadcast_to(part, (4,) + part.shape)
    whole = lax.all_to_all(whole, "tile", 0, 0, axis_index_groups=Y_GROUPS)
    own = whole.reshape(-1, 128)
    other = tile_swap(own, 0, 0, 1)
    first = jnp.where(core == 0, own, other)
    second = jnp.where(core == 0, other, own)
    return jnp.concatenate([first, second], 0).reshape(gram.shape)


AB = (((1,), (0,)), ((), ()))
ATB = (((0,), (0,)), ((), ()))
ABT = (((1,), (1,)), ((), ()))


def parts_of(x, exact=False):
    high = x.astype(jnp.bfloat16)
    if exact:
        return (high,)
    rest = x - high.astype(jnp.float32)
    mid = rest.astype(jnp.bfloat16)
    low = (rest - mid.astype(jnp.float32)).astype(jnp.bfloat16)
    return (high, mid, low)


def product(a, b, dims=AB):
    out = None
    for i in range(len(a) - 1, -1, -1):
        for j in range(len(b) - 1, -1, -1):
            if i + j < 3:
                term = lax.dot_general(a[i], b[j], dims, preferred_element_type=jnp.float32)
                out = term if out is None else out + term
    return out


def spread(x, axis, index, size):
    piece = lax.slice_in_dim(x, index, index + 1, axis=axis)
    shape = (size, x.shape[1]) if axis == 0 else (x.shape[0], size)
    return jnp.broadcast_to(piece, shape)


def inverse_factors(mats):
    lane = lax.broadcasted_iota(jnp.int32, (8, 128), 1)
    sub = lax.broadcasted_iota(jnp.int32, (8, 128), 0)
    tiles = [[m[8 * b : 8 * b + 8] for b in range(16)] for m in mats]
    for k in range(16):
        first = 8 * k
        block = (lane >= first) & (lane < first + 8)
        for a in tiles:
            rows = [spread(a[k], 0, r, 8) for r in range(8)]
            piv = [
                [spread(rows[r], 1, first + s, 128) if s >= r else None for s in range(8)]
                for r in range(8)
            ]
            inv = [None] * 8
            mul = [[None] * 8 for _ in range(8)]
            for r in range(8):
                inv[r] = 1.0 / piv[r][r]
                for s in range(r + 1, 8):
                    mul[r][s] = piv[r][s] * inv[r]
                for s in range(r + 1, 8):
                    for t in range(s, 8):
                        piv[s][t] = piv[s][t] - mul[r][s] * piv[r][t]
            for s in range(8):
                rows[s] = jnp.where(block, jnp.where(lane == first + s, 1.0, 0.0), rows[s])
            for s in range(8):
                for r in range(s):
                    rows[s] = rows[s] - mul[r][s] * rows[r]
            scaled = [rows[r] * inv[r] for r in range(8)]
            for b in range(k + 1, 16):
                col = [spread(a[b], 1, first + r, 128) for r in range(8)]
                for r in range(8):
                    for s in range(r + 1, 8):
                        col[s] = col[s] - col[r] * mul[r][s]
                new = jnp.where(block, 0.0, a[b])
                for r in range(8):
                    new = new - col[r] * scaled[r]
                a[b] = new
            done = jnp.zeros((8, 128), jnp.float32)
            for r in range(8):
                done = jnp.where(sub == r, rows[r] * lax.rsqrt(piv[r][r]), done)
            a[k] = jnp.where(lane < first + 8, done, 0.0)
    return [jnp.concatenate(a, 0) for a in tiles]


def mixing(cells, me_ref, gram_ref, start_ref, high_ref, low_ref):
    me = me_ref[0]
    odd = lax.rem(me, 2) == 1
    upper = me // 2

    def side(index, flip):
        x = gram_ref[index]
        return jnp.where(flip, x.T, x)

    def merged(coeffs, coeff_parts, gram_parts):
        t = product(gram_parts, coeff_parts)
        return product(coeff_parts, parts_of(t), ATB)

    start = parts_of(start_ref[0].astype(jnp.float32), True)
    coeffs, inners = [], []
    for half in (0, 1):
        a, b = me ^ (2 * half), me ^ (2 * half + 1)
        near = side(4 + (upper ^ half), odd)
        gram = jnp.concatenate(
            [jnp.concatenate([gram_ref[a], near], 1), jnp.concatenate([near.T, gram_ref[b]], 1)], 0
        )
        gram = parts_of(gram)
        first = product(gram, start) / cells
        second = product(gram, parts_of(first)) / cells
        coeff = (second.astype(jnp.bfloat16),)
        coeffs.append(coeff)
        inners.append(merged(None, coeff, gram))
    inverse = inverse_factors(inners)
    scale = math.sqrt(cells)
    maps = [scale * product(c, parts_of(v), ABT) for c, v in zip(coeffs, inverse)]
    maps = [parts_of(m) for m in maps]
    low_group = upper == 0
    rows = []
    for e in (0, 1):
        line = []
        for f in (2, 3):
            a, b = me ^ e, me ^ f
            index = jnp.where(low_group, 6 + 2 * a + (b - 2), 6 + 2 * b + (a - 2))
            line.append(side(index, upper == 1))
        rows.append(jnp.concatenate(line, 1))
    across = parts_of(jnp.concatenate(rows, 0))
    cross = product(maps[0], parts_of(product(across, maps[1])), ATB)
    cross = parts_of(cross / cells)
    start = start_ref[1].astype(jnp.float32)
    top, bottom = start[:128], start[128:]
    exact = True
    for _ in range(2):
        top, bottom = (
            top + product(cross, parts_of(bottom, exact)),
            bottom + product(cross, parts_of(top, exact), ATB),
        )
        exact = False
    top, bottom = (top.astype(jnp.bfloat16),), (bottom.astype(jnp.bfloat16),)
    mixed = product(top, parts_of(product(cross, bottom)), ATB)
    inner = product(top, top, ATB) + product(bottom, bottom, ATB) + mixed + mixed.T
    (last,) = inverse_factors([inner])
    last = parts_of(last)
    for half, coeff in enumerate((top, bottom)):
        step = product(coeff, last, ABT)
        final = product(maps[half], parts_of(step))
        high = final.astype(jnp.bfloat16)
        high_ref[pl.ds(256 * half, 256), :] = high
        low_ref[pl.ds(256 * half, 256), :] = (final - high.astype(jnp.float32)).astype(jnp.bfloat16)


def mixing_call(cells, me, packed, start_codes):
    shape = jax.ShapeDtypeStruct((512, 128), jnp.bfloat16)
    vmem = pl.BlockSpec(memory_space=pltpu.VMEM)
    return pl.pallas_call(
        functools.partial(mixing, cells),
        out_shape=(shape, shape),
        in_specs=[pl.BlockSpec(memory_space=pltpu.SMEM), vmem, vmem],
        out_specs=(vmem, vmem),
    )(me.reshape(1).astype(jnp.int32), packed, start_codes)


def finish(me_ref, high_ref, low_ref, *refs):
    pieces, out_ref = refs[:16], refs[16]
    wide, done, in_sem, out_sem = refs[17:]
    me = me_ref[0]
    loads = []
    for j in range(4):
        for e in range(4):
            copy = pltpu.make_async_copy(
                pieces[4 * j + e], wide.at[j, :, pl.ds(128 * e, 128)], in_sem.at[4 * j + e]
            )
            copy.start()
            loads.append(copy)
    mix = jnp.concatenate([high_ref[...], low_ref[...]], 1)
    stores = []
    for j in range(4):
        for e in range(4):
            loads[4 * j + e].wait()
        for r in range(0, 2048, 512):
            both = jnp.dot(wide[j, r : r + 512], mix, preferred_element_type=jnp.float32)
            done[j, r : r + 512] = (both[:, :128] + both[:, 128:]).astype(jnp.bfloat16)
        where = pl.multiple_of((me ^ j) * 2048, 2048)
        copy = pltpu.make_async_copy(done.at[j], out_ref.at[pl.ds(where, 2048)], out_sem.at[j])
        copy.start()
        stores.append(copy)
    for copy in stores:
        copy.wait()


def finish_call(me, high, low, pieces):
    vmem = pl.BlockSpec(memory_space=pltpu.VMEM)
    anywhere = pl.BlockSpec(memory_space=pl.ANY)
    return pl.pallas_call(
        finish,
        out_shape=jax.ShapeDtypeStruct((8192, 128), jnp.bfloat16),
        in_specs=[pl.BlockSpec(memory_space=pltpu.SMEM), vmem, vmem] + [anywhere] * 16,
        out_specs=anywhere,
        scratch_shapes=[
            pltpu.VMEM((4, 2048, 512), jnp.bfloat16),
            pltpu.VMEM((4, 2048, 128), jnp.bfloat16),
            pltpu.SemaphoreType.DMA((16,)),
            pltpu.SemaphoreType.DMA((4,)),
        ],
        compiler_params=pltpu.CompilerParams(vmem_limit_bytes=24 << 20),
        cost_estimate=pl.CostEstimate(flops=2 * 8192 * 512 * 256, bytes_accessed=10 << 20, transcendentals=0),
    )(me.reshape(1).astype(jnp.int32), high, low, *pieces)


PAIRS = [(0, 0), (1, 1), (2, 2), (3, 3), (0, 1), (2, 3), (0, 2), (0, 3), (1, 2), (1, 3)]


def per_device(forcing, permeability, merge_weights, start_codes):
    me = lax.axis_index("case")
    tile = lax.axis_index("tile")
    count = lax.axis_size("tile")
    rows = forcing.shape[1]
    ny = forcing.shape[2]
    cells = rows * count * ny
    field = extended(forcing[0], STEPS).astype(jnp.float32)
    perm = extended(permeability[0], STEPS)
    for step in range(STEPS):
        skip = STEPS - step
        field = stencil_step(field, perm[step : perm.shape[0] - step])
        row = tile * rows + jnp.arange(field.shape[0]) - (skip - 1)
        inside = (row >= 0) & (row < rows * count)
        field = jnp.where(inside[:, None, None], field, 0.0)
    weight = jnp.sqrt(merge_weights[0].astype(jnp.float32))
    snap = (field * weight).astype(jnp.bfloat16).reshape(4, -1, 128)
    snap = jnp.stack([lax.dynamic_index_in_dim(snap, me ^ j, 0, False) for j in range(4)])
    got = {(0, j): snap[j] for j in range(4)}
    for e in (2, 1, 3):
        got[e, 0] = case_swap(snap[e], e)
    quarter = jnp.stack([got[e, 0] for e in range(4)])
    late, quarter = BAR((snap, quarter))
    for j in (1, 2, 3):
        for e in (1, 2, 3):
            got[e, j] = case_swap(late[e ^ j], e)
    groups = jnp.stack([lax.dynamic_index_in_dim(quarter, me ^ k, 0, False) for k in range(4)])
    wide = jnp.concatenate([groups[k] for k in range(4)], 1)
    gram = lax.dot_general(wide, wide, (((0,), (0,)), ((), ())), preferred_element_type=jnp.float32)
    packed = jnp.stack([gram[a * 128 : a * 128 + 128, b * 128 : b * 128 + 128] for a, b in PAIRS])
    packed = total(packed)
    high, low = mixing_call(cells, me, packed, start_codes)
    pieces = [got[e, j] for j in range(4) for e in range(4)]
    outs = finish_call(me, high, low, pieces)
    return outs.reshape(1, -1, 128)


def solution(mesh):
    placed = (P("case", "tile", None, None), P("case", "tile", None), P("case"), P())
    return jax.shard_map(
        per_device, mesh=mesh, in_specs=placed, out_specs=P("case", "tile", None), check_vma=False
    )
```

```python
import functools
import math

import jax
import jax.numpy as jnp
from jax import lax
from jax.experimental import pallas as pl
from jax.experimental.pallas import tpu as pltpu
from jax.sharding import PartitionSpec as P

STEPS = 3


def at(z, y, core):
    return (z * 4 + y) * 2 + core


PLANES = [[at(z, y, core) for z in range(8) for y in range(4)] for core in range(2)]


def case_swap(value, apart):
    return lax.ppermute(value, "case", [(source, source ^ apart) for source in range(4)])


def core_swap(value):
    return lax.ppermute(value, "tile", [(source, source ^ 1) for source in range(64)])


def plane_exchange(value):
    return lax.all_to_all(value, "tile", 0, 0, axis_index_groups=PLANES)


def edges(cells, width):
    head, tail = cells[:width], cells[cells.shape[0] - width :]
    up = [(i, i + 1) for i in range(63)]
    down = [(i + 1, i) for i in range(63)]
    return lax.ppermute(tail, "tile", up), lax.ppermute(head, "tile", down)


AB = (((1,), (0,)), ((), ()))
ATB = (((0,), (0,)), ((), ()))
ABT = (((1,), (1,)), ((), ()))


def parts_of(x, exact=False):
    high = x.astype(jnp.bfloat16)
    if exact:
        return (high,)
    rest = x - high.astype(jnp.float32)
    mid = rest.astype(jnp.bfloat16)
    low = (rest - mid.astype(jnp.float32)).astype(jnp.bfloat16)
    return (high, mid, low)


def product(a, b, dims=AB):
    out = None
    for i in range(len(a) - 1, -1, -1):
        for j in range(len(b) - 1, -1, -1):
            if i + j < 3:
                term = lax.dot_general(a[i], b[j], dims, preferred_element_type=jnp.float32)
                out = term if out is None else out + term
    return out


def spread(x, axis, index, size):
    piece = lax.slice_in_dim(x, index, index + 1, axis=axis)
    shape = (size, x.shape[1]) if axis == 0 else (x.shape[0], size)
    return jnp.broadcast_to(piece, shape)


def inverse_factors(mats):
    lane = lax.broadcasted_iota(jnp.int32, (8, 128), 1)
    sub = lax.broadcasted_iota(jnp.int32, (8, 128), 0)
    tiles = [[m[8 * b : 8 * b + 8] for b in range(16)] for m in mats]
    for k in range(16):
        first = 8 * k
        block = (lane >= first) & (lane < first + 8)
        for a in tiles:
            rows = [spread(a[k], 0, r, 8) for r in range(8)]
            piv = [
                [spread(rows[r], 1, first + s, 128) if s >= r else None for s in range(8)]
                for r in range(8)
            ]
            inv = [None] * 8
            mul = [[None] * 8 for _ in range(8)]
            for r in range(8):
                inv[r] = 1.0 / piv[r][r]
                for s in range(r + 1, 8):
                    mul[r][s] = piv[r][s] * inv[r]
                for s in range(r + 1, 8):
                    for t in range(s, 8):
                        piv[s][t] = piv[s][t] - mul[r][s] * piv[r][t]
            for s in range(8):
                rows[s] = jnp.where(block, jnp.where(lane == first + s, 1.0, 0.0), rows[s])
            for s in range(8):
                for r in range(s):
                    rows[s] = rows[s] - mul[r][s] * rows[r]
            scaled = [rows[r] * inv[r] for r in range(8)]
            for b in range(k + 1, 16):
                col = [spread(a[b], 1, first + r, 128) for r in range(8)]
                for r in range(8):
                    for s in range(r + 1, 8):
                        col[s] = col[s] - col[r] * mul[r][s]
                new = jnp.where(block, 0.0, a[b])
                for r in range(8):
                    new = new - col[r] * scaled[r]
                a[b] = new
            done = jnp.zeros((8, 128), jnp.float32)
            for r in range(8):
                done = jnp.where(sub == r, rows[r] * lax.rsqrt(piv[r][r]), done)
            a[k] = jnp.where(lane < first + 8, done, 0.0)
    return [jnp.concatenate(a, 0) for a in tiles]


def mixing(cells, me_ref, core_ref, own_ref, other_ref, start_ref, high_ref, low_ref, gram_ref):
    me, core = me_ref[0], core_ref[0]
    for side in (0, 1):

        @pl.when(core == side)
        def _(side=side):
            for half, ref in enumerate((own_ref, other_ref) if side == 0 else (other_ref, own_ref)):
                rows = ref[:, 0:16].reshape(4, 128, 128)
                for i in range(4):
                    gram_ref[5 * half + i] = rows[i]
                for k in range(32):
                    gram_ref[5 * half + 4, 4 * k : 4 * k + 4] = ref[k, 16:20]

    odd = lax.rem(me, 2) == 1
    upper = me // 2

    def side(index, flip):
        x = gram_ref[index]
        return jnp.where(flip, x.T, x)

    def merged(coeff_parts, gram_parts):
        t = product(gram_parts, coeff_parts)
        return product(coeff_parts, parts_of(t), ATB)

    start = parts_of(start_ref[0].astype(jnp.float32), True)
    coeffs, inners = [], []
    for half in (0, 1):
        a, b = me ^ (2 * half), me ^ (2 * half + 1)
        near = side(4 + (upper ^ half), odd)
        gram = jnp.concatenate(
            [jnp.concatenate([gram_ref[a], near], 1), jnp.concatenate([near.T, gram_ref[b]], 1)], 0
        )
        gram = parts_of(gram)
        first = product(gram, start) / cells
        second = product(gram, parts_of(first)) / cells
        coeff = (second.astype(jnp.bfloat16),)
        coeffs.append(coeff)
        inners.append(merged(coeff, gram))
    inverse = inverse_factors(inners)
    scale = math.sqrt(cells)
    maps = [scale * product(c, parts_of(v), ABT) for c, v in zip(coeffs, inverse)]
    maps = [parts_of(m) for m in maps]
    low_group = upper == 0
    rows = []
    for e in (0, 1):
        line = []
        for f in (2, 3):
            a, b = me ^ e, me ^ f
            index = jnp.where(low_group, 6 + 2 * a + (b - 2), 6 + 2 * b + (a - 2))
            line.append(side(index, upper == 1))
        rows.append(jnp.concatenate(line, 1))
    across = parts_of(jnp.concatenate(rows, 0))
    cross = product(maps[0], parts_of(product(across, maps[1])), ATB)
    cross = parts_of(cross / cells)
    start = start_ref[1].astype(jnp.float32)
    top, bottom = start[:128], start[128:]
    exact = True
    for _ in range(2):
        top, bottom = (
            top + product(cross, parts_of(bottom, exact)),
            bottom + product(cross, parts_of(top, exact), ATB),
        )
        exact = False
    top, bottom = (top.astype(jnp.bfloat16),), (bottom.astype(jnp.bfloat16),)
    mixed = product(top, parts_of(product(cross, bottom)), ATB)
    inner = product(top, top, ATB) + product(bottom, bottom, ATB) + mixed + mixed.T
    (last,) = inverse_factors([inner])
    last = parts_of(last)
    for half, coeff in enumerate((top, bottom)):
        step = product(coeff, last, ABT)
        final = product(maps[half], parts_of(step))
        high = final.astype(jnp.bfloat16)
        high_ref[pl.ds(256 * half, 256), :] = high
        low_ref[pl.ds(256 * half, 256), :] = (final - high.astype(jnp.float32)).astype(jnp.bfloat16)


NY, LANES, PAD = 512, 128, 8
HALO = 3
EXT = 16 + 2 * HALO
GROUP = 128


def diffuse(me_ref, tile_ref, scale_ref, own_ref, low_ref, high_ref, kp_ref, kp_low_ref, kp_high_ref, *rest):
    outs, (first, second, east, north, perm_ref) = rest[:6], rest[6:]
    me, tile = me_ref[0], tile_ref[0]
    zero_pad = jnp.zeros((PAD, LANES), jnp.float32)

    def fill(source, base, count):
        def one(i, _):
            first[base + i, PAD : PAD + NY] = source[i].astype(jnp.float32)
            return 0

        lax.fori_loop(0, count, one, 0)

    def clear(i, _):
        for buf in (first, second):
            buf[i, 0:PAD] = zero_pad
            buf[i, PAD + NY : PAD + NY + PAD] = zero_pad
        return 0

    lax.fori_loop(0, EXT, clear, 0)
    fill(low_ref, 0, HALO)
    fill(own_ref, HALO, 16)
    fill(high_ref, HALO + 16, HALO)

    rows = jnp.concatenate(
        [kp_low_ref[...], kp_ref[...], kp_high_ref[...], jnp.zeros((LANES - EXT, NY), jnp.float32)], 0
    )
    perm_ref[0:PAD] = zero_pad
    perm_ref[PAD : PAD + NY] = rows.T
    perm_ref[PAD + NY : PAD + NY + PAD] = zero_pad

    def spread_rows(g, _):
        at0 = pl.multiple_of(g * 8, 8)
        here = perm_ref[pl.ds(at0, 8)]
        after = perm_ref[pl.ds(at0 + 8, 8)]
        sub = lax.broadcasted_iota(jnp.int32, (8, LANES), 0)
        shifted = pltpu.roll(jnp.where(sub == 0, after, here), 7, axis=0)
        e = 0.12 * (here + shifted)
        n = 0.12 * (here + pltpu.roll(here, LANES - 1, axis=1))
        for i in range(EXT):
            if 1 <= i < EXT - 1:
                east[i, pl.ds(at0, 8)] = jnp.broadcast_to(e[:, i : i + 1], (8, LANES))
            if i < EXT - 1:
                north[i, pl.ds(at0, 8)] = jnp.broadcast_to(n[:, i : i + 1], (8, LANES))
        return 0

    lax.fori_loop(0, (PAD + NY) // 8, spread_rows, 0, unroll=5)

    def sweep(source, begin, count, write):
        for g in range(NY // GROUP):
            c = PAD + g * GROUP
            here = pl.ds(c, GROUP)

            def one(i, carry):
                row = begin + i
                center, south = carry
                above = source[row + 1, c : c + GROUP]
                up = north[row, c : c + GROUP] * (above - center)
                flux = up - south
                flux = flux + east[row, c : c + GROUP] * (source[row, c + 1 : c + GROUP + 1] - center)
                flux = flux + east[row, c - 1 : c + GROUP - 1] * (source[row, c - 1 : c + GROUP - 1] - center)
                write(row, c, center + flux)
                return above, up

            center = source[begin, c : c + GROUP]
            south = north[begin - 1, c : c + GROUP] * (center - source[begin - 1, c : c + GROUP])
            lax.fori_loop(0, count, one, (center, south))

    def store_to(buf):
        def write(row, c, value):
            buf[row, c : c + GROUP] = value

        return write

    def blank(buf, rows):
        for row in rows:
            buf[row, PAD : PAD + NY] = jnp.zeros((NY, LANES), jnp.float32)

    sweep(first, 1, EXT - 2, store_to(second))

    @pl.when(tile == 0)
    def _():
        blank(second, (1, 2))

    @pl.when(tile == 63)
    def _():
        blank(second, (EXT - 3, EXT - 2))

    sweep(second, 2, EXT - 4, store_to(first))

    @pl.when(tile == 0)
    def _():
        blank(first, (2,))

    @pl.when(tile == 63)
    def _():
        blank(first, (EXT - 3,))

    scale = jnp.sqrt(scale_ref[0].astype(jnp.float32) * jnp.ones((8, LANES), jnp.float32))
    scale = jnp.broadcast_to(scale[0:1], (GROUP, LANES))
    for j in range(4):
        begin = HALO + 4 * (me ^ j)

        def write(row, c, value, j=j, begin=begin):
            at0 = pl.multiple_of((row - begin) * NY + (c - PAD), GROUP)
            value = (value * scale).astype(jnp.bfloat16)
            outs[j][pl.ds(at0, GROUP)] = value
            outs[4 + j // 2][pl.ds(at0 + (j % 2) * 4 * NY, GROUP)] = value

        sweep(first, begin, 4, write)


def diffuse_call(me, tile, weights, own, low, high, kp, kp_low, kp_high):
    vmem = pl.BlockSpec(memory_space=pltpu.VMEM)
    smem = pl.BlockSpec(memory_space=pltpu.SMEM)
    big = pltpu.VMEM((EXT, PAD + NY + PAD, LANES), jnp.float32)
    shapes = [jax.ShapeDtypeStruct((2048, LANES), jnp.bfloat16)] * 4
    shapes += [jax.ShapeDtypeStruct((4096, LANES), jnp.bfloat16)] * 2
    return pl.pallas_call(
        diffuse,
        out_shape=shapes,
        in_specs=[smem] * 3 + [vmem] * 6,
        out_specs=[vmem] * 6,
        scratch_shapes=[big, big, big, big, pltpu.VMEM((PAD + NY + PAD, LANES), jnp.float32)],
        compiler_params=pltpu.CompilerParams(vmem_limit_bytes=52 << 20),
        cost_estimate=pl.CostEstimate(flops=40 << 20, bytes_accessed=8 << 20, transcendentals=0),
    )(me, tile, weights, own, low, high, kp, kp_low, kp_high)


def grams(me_ref, core_ref, *refs):
    pieces, own_ref, other_ref, wide = refs[:4], refs[4], refs[5], refs[6]
    me, core = me_ref[0], core_ref[0]
    for e in range(4):
        lanes = pl.ds(pl.multiple_of((me ^ e) * 128, 128), 128)
        wide[:, lanes] = pieces[e][...]
    left, right = wide[:, :256], wide[:, 256:]
    near = lax.dot_general(left, left, ATB, preferred_element_type=jnp.float32)
    far = lax.dot_general(right, right, ATB, preferred_element_type=jnp.float32)
    cross = lax.dot_general(left, right, ATB, preferred_element_type=jnp.float32)
    blocks = [
        near[:128, :128], near[128:, 128:], far[:128, :128], far[128:, 128:], near[:128, 128:],
        far[:128, 128:], cross[:128, :128], cross[:128, 128:], cross[128:, :128], cross[128:, 128:],
    ]
    for side in (0, 1):

        @pl.when(core == side)
        def _(side=side):
            for half, ref in enumerate((own_ref, other_ref) if side == 0 else (other_ref, own_ref)):
                mine = blocks[5 * half : 5 * half + 5]
                ref[:, 0:16] = jnp.concatenate(mine[:4], 0).reshape(32, 16, 128)
                ref[:, 16:24] = jnp.zeros((32, 8, 128), jnp.float32)
                for k in range(32):
                    ref[k, 16:20] = mine[4][4 * k : 4 * k + 4]


def grams_call(me, core, pieces):
    vmem = pl.BlockSpec(memory_space=pltpu.VMEM)
    smem = pl.BlockSpec(memory_space=pltpu.SMEM)
    shape = jax.ShapeDtypeStruct((32, 24, 128), jnp.float32)
    return pl.pallas_call(
        grams,
        out_shape=(shape, shape),
        in_specs=[smem, smem] + [vmem] * 4,
        out_specs=(vmem, vmem),
        scratch_shapes=[pltpu.VMEM((2048, 512), jnp.bfloat16)],
        compiler_params=pltpu.CompilerParams(vmem_limit_bytes=24 << 20),
        cost_estimate=pl.CostEstimate(flops=2 * 2048 * 512 * 512, bytes_accessed=3 << 20, transcendentals=0),
    )(me, core, *pieces)


def mixing_call(cells, me, core, own, other, start_codes):
    shape = jax.ShapeDtypeStruct((512, 128), jnp.bfloat16)
    vmem = pl.BlockSpec(memory_space=pltpu.VMEM)
    smem = pl.BlockSpec(memory_space=pltpu.SMEM)
    return pl.pallas_call(
        functools.partial(mixing, cells),
        out_shape=(shape, shape),
        in_specs=[smem, smem, vmem, vmem, vmem],
        out_specs=(vmem, vmem),
        scratch_shapes=[pltpu.VMEM((10, 128, 128), jnp.float32)],
        cost_estimate=pl.CostEstimate(flops=1 << 30, bytes_accessed=1 << 20, transcendentals=0),
    )(me, core, own, other, start_codes)


def finish(where, me_ref, high_ref, low_ref, *refs):
    pieces, out_ref = refs[:-5], refs[-5]
    wide, done, in_sem, out_sem = refs[-4:]
    me = me_ref[0]
    loads = []
    for j in range(4):
        for e in range(4):
            index, begin = where[4 * j + e]
            copy = pltpu.make_async_copy(
                pieces[index].at[pl.ds(begin, 2048)],
                wide.at[j, :, pl.ds(128 * e, 128)],
                in_sem.at[4 * j + e],
            )
            copy.start()
            loads.append(copy)
    mix = jnp.concatenate([high_ref[...], low_ref[...]], 1)
    stores = []
    for j in range(4):
        for e in range(4):
            loads[4 * j + e].wait()
        for r in range(0, 2048, 512):
            both = jnp.dot(wide[j, r : r + 512], mix, preferred_element_type=jnp.float32)
            done[j, r : r + 512] = (both[:, :128] + both[:, 128:]).astype(jnp.bfloat16)
        target = pl.multiple_of((me ^ j) * 2048, 2048)
        copy = pltpu.make_async_copy(done.at[j], out_ref.at[pl.ds(target, 2048)], out_sem.at[j])
        copy.start()
        stores.append(copy)
    for copy in stores:
        copy.wait()


def finish_call(me, high, low, pieces, where):
    vmem = pl.BlockSpec(memory_space=pltpu.VMEM)
    anywhere = pl.BlockSpec(memory_space=pl.ANY)
    return pl.pallas_call(
        functools.partial(finish, where),
        out_shape=jax.ShapeDtypeStruct((8192, 128), jnp.bfloat16),
        in_specs=[pl.BlockSpec(memory_space=pltpu.SMEM), vmem, vmem] + [anywhere] * len(pieces),
        out_specs=anywhere,
        scratch_shapes=[
            pltpu.VMEM((4, 2048, 512), jnp.bfloat16),
            pltpu.VMEM((4, 2048, 128), jnp.bfloat16),
            pltpu.SemaphoreType.DMA((16,)),
            pltpu.SemaphoreType.DMA((4,)),
        ],
        compiler_params=pltpu.CompilerParams(vmem_limit_bytes=24 << 20),
        cost_estimate=pl.CostEstimate(flops=2 * 8192 * 512 * 256, bytes_accessed=10 << 20, transcendentals=0),
    )(me, high, low, *pieces)


def merged_bases(forcing, permeability, merge_weights, start_codes):
    me = lax.axis_index("case").astype(jnp.int32).reshape(1)
    tile = lax.axis_index("tile").astype(jnp.int32).reshape(1)
    core = tile % 2
    cells = forcing.shape[1] * lax.axis_size("tile") * forcing.shape[2]
    low, high = edges(forcing[0], STEPS)
    kp_low, kp_high = edges(permeability[0], STEPS)
    *snap, front, back = diffuse_call(
        me, tile, merge_weights, forcing[0], low, high, permeability[0], kp_low, kp_high
    )
    met = [snap[0]] + [case_swap(snap[e], e) for e in (1, 2, 3)]
    next_piece = {e: case_swap(snap[e ^ 1], e) for e in (1, 2, 3)}
    own, other = grams_call(me, core, met)
    part = own + core_swap(other)
    part = plane_exchange(part).sum(0)
    part = part + case_swap(part, 1) + case_swap(part, 2) + case_swap(part, 3)
    last_pieces = {1: case_swap(back, 1), 2: case_swap(front, 2), 3: case_swap(front, 3)}
    own = plane_exchange(jnp.broadcast_to(part, (32,) + part.shape))
    other = core_swap(own)
    high, low = mixing_call(cells, me, core, own, other, start_codes)
    pieces = snap + met[1:] + [next_piece[e] for e in (1, 2, 3)] + [last_pieces[e] for e in (1, 2, 3)]
    where = []
    for j in range(4):
        for e in range(4):
            if e == 0:
                where.append((j, 0))
            elif j == 0:
                where.append((3 + e, 0))
            elif j == 1:
                where.append((6 + e, 0))
            else:
                where.append((9 + e, ((e ^ j) % 2) * 2048))
    return finish_call(me, high, low, pieces, tuple(where))[None]


def solution(mesh):
    placed = (P("case", "tile", None, None), P("case", "tile", None), P("case"), P())
    return jax.shard_map(
        merged_bases, mesh=mesh, in_specs=placed, out_specs=P("case", "tile", None), check_vma=False
    )
```

```python
import functools
import math

import jax
import jax.numpy as jnp
from jax import lax
from jax.experimental import pallas as pl
from jax.experimental.pallas import tpu as pltpu
from jax.sharding import PartitionSpec as P

STEPS = 3


def at(z, y, core):
    return (z * 4 + y) * 2 + core


PLANES = [[at(z, y, core) for z in range(8) for y in range(4)] for core in range(2)]


def case_swap(value, apart):
    return lax.ppermute(value, "case", [(source, source ^ apart) for source in range(4)])


def core_swap(value):
    return lax.ppermute(value, "tile", [(source, source ^ 1) for source in range(64)])


def plane_exchange(value):
    return lax.all_to_all(value, "tile", 0, 0, axis_index_groups=PLANES)


AB = (((1,), (0,)), ((), ()))
ATB = (((0,), (0,)), ((), ()))
ABT = (((1,), (1,)), ((), ()))


def parts_of(x, exact=False):
    high = x.astype(jnp.bfloat16)
    if exact:
        return (high,)
    rest = x - high.astype(jnp.float32)
    mid = rest.astype(jnp.bfloat16)
    low = (rest - mid.astype(jnp.float32)).astype(jnp.bfloat16)
    return (high, mid, low)


def product(a, b, dims=AB):
    out = None
    for i in range(len(a) - 1, -1, -1):
        for j in range(len(b) - 1, -1, -1):
            if i + j < 3:
                term = lax.dot_general(a[i], b[j], dims, preferred_element_type=jnp.float32)
                out = term if out is None else out + term
    return out


def spread(x, axis, index, size):
    piece = lax.slice_in_dim(x, index, index + 1, axis=axis)
    shape = (size, x.shape[1]) if axis == 0 else (x.shape[0], size)
    return jnp.broadcast_to(piece, shape)


def inverse_factors(mats):
    lane = lax.broadcasted_iota(jnp.int32, (8, 128), 1)
    sub = lax.broadcasted_iota(jnp.int32, (8, 128), 0)
    tiles = [[m[8 * b : 8 * b + 8] for b in range(16)] for m in mats]
    for k in range(16):
        first = 8 * k
        block = (lane >= first) & (lane < first + 8)
        for a in tiles:
            rows = [spread(a[k], 0, r, 8) for r in range(8)]
            piv = [
                [spread(rows[r], 1, first + s, 128) if s >= r else None for s in range(8)]
                for r in range(8)
            ]
            inv = [None] * 8
            mul = [[None] * 8 for _ in range(8)]
            for r in range(8):
                inv[r] = 1.0 / piv[r][r]
                for s in range(r + 1, 8):
                    mul[r][s] = piv[r][s] * inv[r]
                for s in range(r + 1, 8):
                    for t in range(s, 8):
                        piv[s][t] = piv[s][t] - mul[r][s] * piv[r][t]
            for s in range(8):
                rows[s] = jnp.where(block, jnp.where(lane == first + s, 1.0, 0.0), rows[s])
            for s in range(8):
                for r in range(s):
                    rows[s] = rows[s] - mul[r][s] * rows[r]
            scaled = [rows[r] * inv[r] for r in range(8)]
            for b in range(k + 1, 16):
                col = [spread(a[b], 1, first + r, 128) for r in range(8)]
                for r in range(8):
                    for s in range(r + 1, 8):
                        col[s] = col[s] - col[r] * mul[r][s]
                new = jnp.where(block, 0.0, a[b])
                for r in range(8):
                    new = new - col[r] * scaled[r]
                a[b] = new
            done = jnp.zeros((8, 128), jnp.float32)
            for r in range(8):
                done = jnp.where(sub == r, rows[r] * lax.rsqrt(piv[r][r]), done)
            a[k] = jnp.where(lane < first + 8, done, 0.0)
    return [jnp.concatenate(a, 0) for a in tiles]


def mixing(cells, me_ref, core_ref, own_hbm, other_hbm, start_ref, high_ref, low_ref, *scratch):
    gram_ref, own_ref, other_ref, sems = scratch
    me, core = me_ref[0], core_ref[0]
    loads = [
        pltpu.make_async_copy(own_hbm, own_ref, sems.at[0]),
        pltpu.make_async_copy(other_hbm, other_ref, sems.at[1]),
    ]
    for copy in loads:
        copy.start()
    for copy in loads:
        copy.wait()
    for side in (0, 1):

        @pl.when(core == side)
        def _(side=side):
            for half, ref in enumerate((own_ref, other_ref) if side == 0 else (other_ref, own_ref)):
                rows = ref[:, 0:16].reshape(4, 128, 128)
                for i in range(4):
                    gram_ref[5 * half + i] = rows[i]
                for k in range(32):
                    gram_ref[5 * half + 4, 4 * k : 4 * k + 4] = ref[k, 16:20]

    odd = lax.rem(me, 2) == 1
    upper = me // 2

    def side(index, flip):
        x = gram_ref[index]
        return jnp.where(flip, x.T, x)

    def merged(coeff_parts, gram_parts):
        t = product(gram_parts, coeff_parts)
        return product(coeff_parts, parts_of(t), ATB)

    start = parts_of(start_ref[0].astype(jnp.float32), True)
    coeffs, inners = [], []
    for half in (0, 1):
        a, b = me ^ (2 * half), me ^ (2 * half + 1)
        near = side(4 + (upper ^ half), odd)
        gram = jnp.concatenate(
            [jnp.concatenate([gram_ref[a], near], 1), jnp.concatenate([near.T, gram_ref[b]], 1)], 0
        )
        gram = parts_of(gram)
        first = product(gram, start) / cells
        second = product(gram, parts_of(first)) / cells
        coeff = (second.astype(jnp.bfloat16),)
        coeffs.append(coeff)
        inners.append(merged(coeff, gram))
    inverse = inverse_factors(inners)
    scale = math.sqrt(cells)
    maps = [scale * product(c, parts_of(v), ABT) for c, v in zip(coeffs, inverse)]
    maps = [parts_of(m) for m in maps]
    low_group = upper == 0
    rows = []
    for e in (0, 1):
        line = []
        for f in (2, 3):
            a, b = me ^ e, me ^ f
            index = jnp.where(low_group, 6 + 2 * a + (b - 2), 6 + 2 * b + (a - 2))
            line.append(side(index, upper == 1))
        rows.append(jnp.concatenate(line, 1))
    across = parts_of(jnp.concatenate(rows, 0))
    cross = product(maps[0], parts_of(product(across, maps[1])), ATB)
    cross = parts_of(cross / cells)
    start = start_ref[1].astype(jnp.float32)
    top, bottom = start[:128], start[128:]
    exact = True
    for _ in range(2):
        top, bottom = (
            top + product(cross, parts_of(bottom, exact)),
            bottom + product(cross, parts_of(top, exact), ATB),
        )
        exact = False
    top, bottom = (top.astype(jnp.bfloat16),), (bottom.astype(jnp.bfloat16),)
    mixed = product(top, parts_of(product(cross, bottom)), ATB)
    inner = product(top, top, ATB) + product(bottom, bottom, ATB) + mixed + mixed.T
    (last,) = inverse_factors([inner])
    last = parts_of(last)
    for half, coeff in enumerate((top, bottom)):
        step = product(coeff, last, ABT)
        final = product(maps[half], parts_of(step))
        high = final.astype(jnp.bfloat16)
        high_ref[pl.ds(256 * half, 256), :] = high
        low_ref[pl.ds(256 * half, 256), :] = (final - high.astype(jnp.float32)).astype(jnp.bfloat16)


NY, LANES, PAD = 512, 128, 8
WIDE = PAD + NY + PAD
GROUP = 128
INNER, OUTER = 10 * GROUP, 6 * GROUP
PIECE = INNER + OUTER


def spread_faces(perm_ref, east, north, count):
    def one(g, _):
        at0 = pl.multiple_of(g * 8, 8)
        here = perm_ref[pl.ds(at0, 8)]
        after = perm_ref[pl.ds(at0 + 8, 8)]
        sub = lax.broadcasted_iota(jnp.int32, (8, LANES), 0)
        shifted = pltpu.roll(jnp.where(sub == 0, after, here), 7, axis=0)
        e = 0.12 * (here + shifted)
        n = 0.12 * (here + pltpu.roll(here, LANES - 1, axis=1))
        for i in range(count):
            east[i, pl.ds(at0, 8)] = jnp.broadcast_to(e[:, i : i + 1], (8, LANES))
            north[i, pl.ds(at0, 8)] = jnp.broadcast_to(n[:, i : i + 1], (8, LANES))
        return 0

    lax.fori_loop(0, (PAD + NY) // 8, one, 0, unroll=5)


def set_perm(perm_ref, rows):
    count = rows.shape[0]
    rows = jnp.concatenate([rows, jnp.zeros((LANES - count, NY), jnp.float32)], 0)
    perm_ref[0:PAD] = jnp.zeros((PAD, LANES), jnp.float32)
    perm_ref[PAD : PAD + NY] = rows.T
    perm_ref[PAD + NY : WIDE] = jnp.zeros((PAD, LANES), jnp.float32)


def clear_pads(buf, count):
    def one(i, _):
        buf[i, 0:PAD] = jnp.zeros((PAD, LANES), jnp.float32)
        buf[i, PAD + NY : WIDE] = jnp.zeros((PAD, LANES), jnp.float32)
        return 0

    lax.fori_loop(0, count, one, 0)


def sweep(source, east, north, begin, face, count, write):
    for g in range(NY // GROUP):
        c = PAD + g * GROUP

        def one(i, carry, c=c, g=g):
            row, plane = begin + i, face + i
            center, south = carry
            above = source[row + 1, c : c + GROUP]
            up = north[plane, c : c + GROUP] * (above - center)
            flux = up - south
            flux = flux + east[plane, c : c + GROUP] * (source[row, c + 1 : c + GROUP + 1] - center)
            flux = flux + east[plane, c - 1 : c + GROUP - 1] * (source[row, c - 1 : c + GROUP - 1] - center)
            write(i, g, center + flux)
            return above, up

        center = source[begin, c : c + GROUP]
        south = north[face - 1, c : c + GROUP] * (center - source[begin - 1, c : c + GROUP])
        lax.fori_loop(0, count, one, (center, south))


def into(buf, base):
    def write(i, g, value):
        buf[base + i, PAD + g * GROUP : PAD + g * GROUP + GROUP] = value

    return write


def into_snap(snap, base, scale_ref):
    scale = jnp.sqrt(jnp.full((8, LANES), scale_ref[0].astype(jnp.float32)))
    scale = jnp.broadcast_to(scale[0:1], (GROUP, LANES))

    def write(i, g, value):
        at0 = pl.multiple_of((base + i) * GROUP, GROUP)
        snap[g, pl.ds(at0, GROUP)] = (value * scale).astype(jnp.bfloat16)

    return write


def send_out(me, snap, singles, stacks, begin, size, sems):
    copies = []
    for e in (1, 2, 3):
        copies.append(pltpu.make_async_copy(snap.at[me ^ e], singles[e - 1], sems.at[len(copies)]))
        for j in (1, 2, 3):
            target = stacks[e - 1].at[pl.ds(PIECE * (j - 1) + begin, size)]
            copies.append(pltpu.make_async_copy(snap.at[me ^ e ^ j], target, sems.at[len(copies)]))
    for copy in copies:
        copy.start()
    return copies


def inner_rows(me_ref, scale_ref, own_ref, kp_ref, *refs):
    singles, stacks, edge_one, edge_two = refs[:3], refs[3:6], refs[6], refs[7]
    first, second, east, north, perm_ref, snap, held, sems, edge_sems = refs[8:]
    me = me_ref[0]
    load = pltpu.make_async_copy(own_ref, held, sems.at[0])
    load.start()
    clear_pads(first, 16)
    clear_pads(second, 16)

    def fill(i, _):
        first[i, PAD : PAD + NY] = held[i].astype(jnp.float32)
        return 0

    set_perm(perm_ref, kp_ref[...])
    spread_faces(perm_ref, east, north, 15)
    load.wait()
    lax.fori_loop(0, 16, fill, 0)
    sweep(first, east, north, 1, 1, 14, into(second, 1))
    sweep(second, east, north, 2, 2, 12, into(first, 2))
    edges_out = [
        pltpu.make_async_copy(second.at[pl.ds(1, 2)], edge_one.at[pl.ds(0, 2)], edge_sems.at[0]),
        pltpu.make_async_copy(second.at[pl.ds(13, 2)], edge_one.at[pl.ds(2, 2)], edge_sems.at[1]),
        pltpu.make_async_copy(first.at[pl.ds(2, 2)], edge_two.at[pl.ds(0, 2)], edge_sems.at[2]),
        pltpu.make_async_copy(first.at[pl.ds(12, 2)], edge_two.at[pl.ds(2, 2)], edge_sems.at[3]),
    ]
    for copy in edges_out:
        copy.start()
    sweep(first, east, north, 3, 3, 10, into_snap(snap, 0, scale_ref))
    for copy in edges_out + send_out(me, snap, singles, stacks, 0, INNER, sems):
        copy.wait()


def outer_rows(me_ref, tile_ref, scale_ref, own_hbm, kp_ref, low_hbm, high_hbm, edge_one, edge_two, *refs):
    singles, stacks = refs[3:6], refs[6:9]
    low0, low1, low2, high0, high1, high2, east, north, perm_ref, snap = refs[9:19]
    low_ref, high_ref, own_ref, sems, edge_sems = refs[19:]
    me, tile = me_ref[0], tile_ref[0]
    loads = [
        pltpu.make_async_copy(low_hbm, low_ref, sems.at[0]),
        pltpu.make_async_copy(high_hbm, high_ref, sems.at[1]),
        pltpu.make_async_copy(own_hbm.at[pl.ds(0, 2)], own_ref.at[pl.ds(0, 2)], sems.at[2]),
        pltpu.make_async_copy(own_hbm.at[pl.ds(14, 2)], own_ref.at[pl.ds(2, 2)], sems.at[3]),
    ]
    for copy in loads:
        copy.start()
    edges_in = [
        pltpu.make_async_copy(edge_one.at[pl.ds(0, 2)], low1.at[pl.ds(3, 2)], edge_sems.at[0]),
        pltpu.make_async_copy(edge_one.at[pl.ds(2, 2)], high1.at[pl.ds(0, 2)], edge_sems.at[1]),
        pltpu.make_async_copy(edge_two.at[pl.ds(0, 2)], low2.at[pl.ds(3, 2)], edge_sems.at[2]),
        pltpu.make_async_copy(edge_two.at[pl.ds(2, 2)], high2.at[pl.ds(0, 2)], edge_sems.at[3]),
    ]
    for copy in edges_in:
        copy.start()
    for buf in (low0, high0):
        clear_pads(buf, 5)
    for buf in (low1, low2):
        clear_pads(buf, 3)
    for buf in (high1, high2):
        clear_pads(buf.at[pl.ds(2, 3)], 3)
    for copy in loads:
        copy.wait()
    for i in range(3):
        low0[i, PAD : PAD + NY] = low_ref[NY * i : NY * i + NY].astype(jnp.float32)
        high0[2 + i, PAD : PAD + NY] = high_ref[NY * i : NY * i + NY].astype(jnp.float32)
    for i in range(2):
        low0[3 + i, PAD : PAD + NY] = own_ref[i].astype(jnp.float32)
        high0[i, PAD : PAD + NY] = own_ref[2 + i].astype(jnp.float32)

    def far_perm(ref):
        both = ref[3 * NY : 3 * NY + 32].astype(jnp.float32)
        packed = both[0:12] + both[12:24]
        return [
            jnp.concatenate([packed[4 * i + q : 4 * i + q + 1] for q in range(4)], 1) for i in range(3)
        ]

    kp = kp_ref[...]
    set_perm(perm_ref, jnp.concatenate(far_perm(low_ref) + [kp[0:4], kp[12:16]] + far_perm(high_ref), 0))
    spread_faces(perm_ref, east, north, 13)
    sweep(low0, east, north, 1, 1, 3, into(low1, 0))
    sweep(high0, east, north, 1, 10, 3, into(high1, 2))
    blank = jnp.zeros((NY, LANES), jnp.float32)

    @pl.when(tile == 0)
    def _():
        low1[0, PAD : PAD + NY] = blank
        low1[1, PAD : PAD + NY] = blank

    @pl.when(tile == 63)
    def _():
        high1[3, PAD : PAD + NY] = blank
        high1[4, PAD : PAD + NY] = blank

    for copy in edges_in:
        copy.wait()
    sweep(low1, east, north, 1, 2, 3, into(low2, 0))
    sweep(high1, east, north, 1, 9, 3, into(high2, 2))

    @pl.when(tile == 0)
    def _():
        low2[0, PAD : PAD + NY] = blank

    @pl.when(tile == 63)
    def _():
        high2[4, PAD : PAD + NY] = blank

    sweep(low2, east, north, 1, 3, 3, into_snap(snap, 0, scale_ref))
    sweep(high2, east, north, 1, 8, 3, into_snap(snap, 3, scale_ref))
    for copy in send_out(me, snap, singles, stacks, INNER, OUTER, sems):
        copy.wait()


VM = pl.BlockSpec(memory_space=pltpu.VMEM)
SM = pl.BlockSpec(memory_space=pltpu.SMEM)
ANY = pl.BlockSpec(memory_space=pl.ANY)


def half(rows):
    return jax.ShapeDtypeStruct((rows, LANES), jnp.bfloat16)


def planes(count):
    return pltpu.VMEM((count, WIDE, LANES), jnp.float32)


def inner_call(me, weights, own, kp):
    edge = jax.ShapeDtypeStruct((4, WIDE, LANES), jnp.float32)
    return pl.pallas_call(
        inner_rows,
        out_shape=[half(INNER)] * 3 + [half(3 * PIECE)] * 3 + [edge] * 2,
        in_specs=[SM, SM, ANY, VM],
        out_specs=[ANY] * 8,
        scratch_shapes=[planes(16), planes(16), planes(15), planes(15)]
        + [pltpu.VMEM((WIDE, LANES), jnp.float32), pltpu.VMEM((4, INNER, LANES), jnp.bfloat16)]
        + [pltpu.VMEM((16, NY, LANES), jnp.bfloat16)]
        + [pltpu.SemaphoreType.DMA((12,)), pltpu.SemaphoreType.DMA((4,))],
        compiler_params=pltpu.CompilerParams(vmem_limit_bytes=63 << 20),
        cost_estimate=pl.CostEstimate(flops=400 << 20, bytes_accessed=9 << 20, transcendentals=0),
    )(me, weights, own, kp)


def outer_call(me, tile, weights, own, kp, low, high, edge_one, edge_two, stacks):
    return pl.pallas_call(
        outer_rows,
        out_shape=[half(OUTER)] * 3 + [half(3 * PIECE)] * 3,
        in_specs=[SM, SM, SM, ANY, VM] + [ANY] * 7,
        out_specs=[ANY] * 6,
        input_output_aliases={9: 3, 10: 4, 11: 5},
        scratch_shapes=[planes(5)] * 6
        + [planes(13), planes(13), pltpu.VMEM((WIDE, LANES), jnp.float32)]
        + [pltpu.VMEM((4, OUTER, LANES), jnp.bfloat16)]
        + [pltpu.VMEM((3 * NY + 32, LANES), jnp.bfloat16)] * 2
        + [pltpu.VMEM((4, NY, LANES), jnp.bfloat16)]
        + [pltpu.SemaphoreType.DMA((12,)), pltpu.SemaphoreType.DMA((4,))],
        compiler_params=pltpu.CompilerParams(vmem_limit_bytes=63 << 20),
        cost_estimate=pl.CostEstimate(flops=200 << 20, bytes_accessed=9 << 20, transcendentals=0),
    )(me, tile, weights, own, kp, low, high, edge_one, edge_two, *stacks)


def grams(me_ref, core_ref, *refs):
    pieces, own_ref, other_ref, wide, sems = refs[:7], refs[7], refs[8], refs[9], refs[10]
    me, core = me_ref[0], core_ref[0]
    copies = []
    for e in range(4):
        lanes = pl.ds(pl.multiple_of((me ^ e) * 128, 128), 128)
        if e == 0:
            moves = [(pieces[0].at[pl.ds(0, PIECE)], 0, PIECE)]
        else:
            moves = [(pieces[e], 0, INNER), (pieces[3 + e], INNER, OUTER)]
        for source, begin, size in moves:
            target = wide.at[pl.ds(begin, size), lanes]
            copies.append(pltpu.make_async_copy(source, target, sems.at[len(copies)]))
    for copy in copies:
        copy.start()
    for copy in copies:
        copy.wait()
    left, right = wide[:, :256], wide[:, 256:]
    near = lax.dot_general(left, left, ATB, preferred_element_type=jnp.float32)
    far = lax.dot_general(right, right, ATB, preferred_element_type=jnp.float32)
    cross = lax.dot_general(left, right, ATB, preferred_element_type=jnp.float32)
    blocks = [
        near[:128, :128], near[128:, 128:], far[:128, :128], far[128:, 128:], near[:128, 128:],
        far[:128, 128:], cross[:128, :128], cross[:128, 128:], cross[128:, :128], cross[128:, 128:],
    ]
    for side in (0, 1):

        @pl.when(core == side)
        def _(side=side):
            for half, ref in enumerate((own_ref, other_ref) if side == 0 else (other_ref, own_ref)):
                mine = blocks[5 * half : 5 * half + 5]
                ref[:, 0:16] = jnp.concatenate(mine[:4], 0).reshape(32, 16, 128)
                ref[:, 16:24] = jnp.zeros((32, 8, 128), jnp.float32)
                for k in range(32):
                    ref[k, 16:20] = mine[4][4 * k : 4 * k + 4]


def grams_call(me, core, pieces):
    shape = jax.ShapeDtypeStruct((32, 24, 128), jnp.float32)
    return pl.pallas_call(
        grams,
        out_shape=(shape, shape),
        in_specs=[SM, SM] + [ANY] * 7,
        out_specs=(VM, VM),
        scratch_shapes=[pltpu.VMEM((PIECE, 512), jnp.bfloat16), pltpu.SemaphoreType.DMA((7,))],
        compiler_params=pltpu.CompilerParams(vmem_limit_bytes=63 << 20),
        cost_estimate=pl.CostEstimate(flops=2 * 2048 * 512 * 512, bytes_accessed=3 << 20, transcendentals=0),
    )(me, core, *pieces)


def mixing_call(cells, me, core, own, other, start_codes):
    shape = jax.ShapeDtypeStruct((512, 128), jnp.bfloat16)
    vmem = pl.BlockSpec(memory_space=pltpu.VMEM)
    smem = pl.BlockSpec(memory_space=pltpu.SMEM)
    return pl.pallas_call(
        functools.partial(mixing, cells),
        out_shape=(shape, shape),
        in_specs=[smem, smem, ANY, ANY, vmem],
        out_specs=(vmem, vmem),
        scratch_shapes=[pltpu.VMEM((10, 128, 128), jnp.float32)]
        + [pltpu.VMEM((32, 24, 128), jnp.float32)] * 2
        + [pltpu.SemaphoreType.DMA((2,))],
        compiler_params=pltpu.CompilerParams(vmem_limit_bytes=62 << 20),
        cost_estimate=pl.CostEstimate(flops=1 << 30, bytes_accessed=1 << 20, transcendentals=0),
    )(me, core, own, other, start_codes)


def finish(plan, me_ref, high_ref, low_ref, *refs):
    pieces, out_ref = refs[:-5], refs[-5]
    wide, done, in_sems, out_sems = refs[-4:]
    me = me_ref[0]
    loads = []
    for j in range(4):
        group = []
        for e in range(4):
            for index, source, target, size in plan[4 * j + e]:
                group.append(
                    pltpu.make_async_copy(
                        pieces[index].at[pl.ds(source, size)],
                        wide.at[j, pl.ds(target, size), pl.ds(128 * e, 128)],
                        in_sems.at[len(loads), len(group)],
                    )
                )
                group[-1].start()
        loads.append(group)
    mix = jnp.concatenate([high_ref[...], low_ref[...]], 1)
    stores = []
    for j in range(4):
        for copy in loads[j]:
            copy.wait()
        for r in range(16):
            both = jnp.dot(wide[j, 128 * r : 128 * r + 128], mix, preferred_element_type=jnp.float32)
            done[j, r] = (both[:, :128] + both[:, 128:]).astype(jnp.bfloat16)
        columns = pl.ds(pl.multiple_of((me ^ j) * GROUP, GROUP), GROUP)
        for n, (source, target, size) in enumerate(((0, 3, 10), (10, 0, 3), (13, 13, 3))):
            copy = pltpu.make_async_copy(
                done.at[j, pl.ds(source, size)], out_ref.at[pl.ds(target, size), columns], out_sems.at[j, n]
            )
            copy.start()
            stores.append(copy)
    for copy in stores:
        copy.wait()


def finish_call(me, high, low, pieces, plan):
    return pl.pallas_call(
        functools.partial(finish, plan),
        out_shape=jax.ShapeDtypeStruct((16, NY, LANES), jnp.bfloat16),
        in_specs=[SM, VM, VM] + [ANY] * len(pieces),
        out_specs=ANY,
        scratch_shapes=[
            pltpu.VMEM((4, PIECE, 512), jnp.bfloat16),
            pltpu.VMEM((4, 16, GROUP, LANES), jnp.bfloat16),
            pltpu.SemaphoreType.DMA((4, 8)),
            pltpu.SemaphoreType.DMA((4, 3)),
        ],
        compiler_params=pltpu.CompilerParams(vmem_limit_bytes=63 << 20),
        cost_estimate=pl.CostEstimate(flops=2 * 8192 * 512 * 256, bytes_accessed=10 << 20, transcendentals=0),
    )(me, high, low, *pieces)


def packed_edge(cells, perm):
    high = perm.astype(jnp.bfloat16)
    low = (perm - high.astype(jnp.float32)).astype(jnp.bfloat16)
    parts = [cells.reshape(-1, LANES), high.reshape(-1, LANES), low.reshape(-1, LANES)]
    return jnp.concatenate(parts + [jnp.zeros((8, LANES), jnp.bfloat16)], 0)


def merged_bases(forcing, permeability, merge_weights, start_codes):
    me = lax.axis_index("case").astype(jnp.int32).reshape(1)
    tile = lax.axis_index("tile").astype(jnp.int32).reshape(1)
    core = tile & 1
    cells = forcing.shape[1] * lax.axis_size("tile") * forcing.shape[2]
    own, kp = forcing[0], permeability[0]
    up = [(i, i + 1) for i in range(63)]
    down = [(i + 1, i) for i in range(63)]
    low = lax.ppermute(packed_edge(own[-STEPS:], kp[-STEPS:]), "tile", up)
    high = lax.ppermute(packed_edge(own[:STEPS], kp[:STEPS]), "tile", down)
    inner = inner_call(me, merge_weights, own, kp)
    met = [case_swap(inner[e - 1], e) for e in (1, 2, 3)]
    outer = outer_call(me, tile, merge_weights, own, kp, low, high, inner[6], inner[7], inner[3:6])
    stacks = outer[3:]
    met = met + [case_swap(outer[e - 1], e) for e in (1, 2, 3)]
    far = [case_swap(stacks[e - 1], e) for e in (1, 2, 3)]
    own_part, other_part = grams_call(me, core, [stacks[0]] + met)
    part = own_part + core_swap(other_part)
    part = plane_exchange(part).sum(0)
    part = part + case_swap(part, 1) + case_swap(part, 2) + case_swap(part, 3)
    mine = plane_exchange(jnp.broadcast_to(part, (32,) + part.shape))
    yours = core_swap(mine)
    high, low = mixing_call(cells, me, core, mine, yours, start_codes)
    own_at = {0: (0, 0), 3: (0, 1), 2: (0, 2), 1: (1, 2)}
    plan = []
    for j in range(4):
        for e in range(4):
            if e == 0:
                index, slot = own_at[j]
                plan.append(((index, PIECE * slot, 0, PIECE),))
            elif j == 0:
                plan.append(((1 + e, 0, 0, INNER), (4 + e, 0, INNER, OUTER)))
            else:
                plan.append(((7 + e, PIECE * (j - 1), 0, PIECE),))
    pieces = [stacks[0], stacks[1]] + met + far
    return finish_call(me, high, low, pieces, tuple(plan)).reshape(1, -1, LANES)


def solution(mesh):
    placed = (P("case", "tile", None, None), P("case", "tile", None), P("case"), P())
    return jax.shard_map(
        merged_bases, mesh=mesh, in_specs=placed, out_specs=P("case", "tile", None), check_vma=False
    )
```

```python
import functools
import math

import jax
import jax.numpy as jnp
from jax import lax
from jax.experimental import pallas as pl
from jax.experimental.pallas import tpu as pltpu
from jax.sharding import PartitionSpec as P

STEPS = 3


def at(z, y, core):
    return (z * 4 + y) * 2 + core


PLANES = [[at(z, y, core) for z in range(8) for y in range(4)] for core in range(2)]


def case_swap(value, apart):
    return lax.ppermute(value, "case", [(source, source ^ apart) for source in range(4)])


def core_swap(value):
    return lax.ppermute(value, "tile", [(source, source ^ 1) for source in range(64)])


def plane_exchange(value):
    return lax.all_to_all(value, "tile", 0, 0, axis_index_groups=PLANES)


AB = (((1,), (0,)), ((), ()))
ATB = (((0,), (0,)), ((), ()))
ABT = (((1,), (1,)), ((), ()))


def parts_of(x, exact=False):
    high = x.astype(jnp.bfloat16)
    if exact:
        return (high,)
    rest = x - high.astype(jnp.float32)
    mid = rest.astype(jnp.bfloat16)
    low = (rest - mid.astype(jnp.float32)).astype(jnp.bfloat16)
    return (high, mid, low)


def product(a, b, dims=AB):
    out = None
    for i in range(len(a) - 1, -1, -1):
        for j in range(len(b) - 1, -1, -1):
            if i + j < 3:
                term = lax.dot_general(a[i], b[j], dims, preferred_element_type=jnp.float32)
                out = term if out is None else out + term
    return out


def spread(x, axis, index, size):
    piece = lax.slice_in_dim(x, index, index + 1, axis=axis)
    shape = (size, x.shape[1]) if axis == 0 else (x.shape[0], size)
    return jnp.broadcast_to(piece, shape)


def inverse_factors(mats):
    lane = lax.broadcasted_iota(jnp.int32, (8, 128), 1)
    sub = lax.broadcasted_iota(jnp.int32, (8, 128), 0)
    tiles = [[m[8 * b : 8 * b + 8] for b in range(16)] for m in mats]
    for k in range(16):
        first = 8 * k
        block = (lane >= first) & (lane < first + 8)
        for a in tiles:
            rows = [spread(a[k], 0, r, 8) for r in range(8)]
            piv = [
                [spread(rows[r], 1, first + s, 128) if s >= r else None for s in range(8)]
                for r in range(8)
            ]
            inv = [None] * 8
            mul = [[None] * 8 for _ in range(8)]
            for r in range(8):
                inv[r] = 1.0 / piv[r][r]
                for s in range(r + 1, 8):
                    mul[r][s] = piv[r][s] * inv[r]
                for s in range(r + 1, 8):
                    for t in range(s, 8):
                        piv[s][t] = piv[s][t] - mul[r][s] * piv[r][t]
            for s in range(8):
                rows[s] = jnp.where(block, jnp.where(lane == first + s, 1.0, 0.0), rows[s])
            for s in range(8):
                for r in range(s):
                    rows[s] = rows[s] - mul[r][s] * rows[r]
            scaled = [rows[r] * inv[r] for r in range(8)]
            for b in range(k + 1, 16):
                col = [spread(a[b], 1, first + r, 128) for r in range(8)]
                for r in range(8):
                    for s in range(r + 1, 8):
                        col[s] = col[s] - col[r] * mul[r][s]
                new = jnp.where(block, 0.0, a[b])
                for r in range(8):
                    new = new - col[r] * scaled[r]
                a[b] = new
            done = jnp.zeros((8, 128), jnp.float32)
            for r in range(8):
                done = jnp.where(sub == r, rows[r] * lax.rsqrt(piv[r][r]), done)
            a[k] = jnp.where(lane < first + 8, done, 0.0)
    return [jnp.concatenate(a, 0) for a in tiles]


def mixing(cells, me_ref, core_ref, own_hbm, other_hbm, start_ref, high_ref, low_ref, *scratch):
    gram_ref, own_ref, other_ref, sems = scratch
    me, core = me_ref[0], core_ref[0]
    loads = [
        pltpu.make_async_copy(own_hbm, own_ref, sems.at[0]),
        pltpu.make_async_copy(other_hbm, other_ref, sems.at[1]),
    ]
    for copy in loads:
        copy.start()
    for copy in loads:
        copy.wait()
    for side in (0, 1):

        @pl.when(core == side)
        def _(side=side):
            for half, ref in enumerate((own_ref, other_ref) if side == 0 else (other_ref, own_ref)):
                rows = ref[:, 0:16].reshape(4, 128, 128)
                for i in range(4):
                    gram_ref[5 * half + i] = rows[i]
                for k in range(32):
                    gram_ref[5 * half + 4, 4 * k : 4 * k + 4] = ref[k, 16:20]

    odd = lax.rem(me, 2) == 1
    upper = me // 2

    def side(index, flip):
        x = gram_ref[index]
        return jnp.where(flip, x.T, x)

    def merged(coeff_parts, gram_parts):
        t = product(gram_parts, coeff_parts)
        return product(coeff_parts, parts_of(t), ATB)

    start = parts_of(start_ref[0].astype(jnp.float32), True)
    coeffs, inners = [], []
    for half in (0, 1):
        a, b = me ^ (2 * half), me ^ (2 * half + 1)
        near = side(4 + (upper ^ half), odd)
        gram = jnp.concatenate(
            [jnp.concatenate([gram_ref[a], near], 1), jnp.concatenate([near.T, gram_ref[b]], 1)], 0
        )
        gram = parts_of(gram)
        first = product(gram, start) / cells
        second = product(gram, parts_of(first)) / cells
        coeff = (second.astype(jnp.bfloat16),)
        coeffs.append(coeff)
        inners.append(merged(coeff, gram))
    inverse = inverse_factors(inners)
    scale = math.sqrt(cells)
    maps = [scale * product(c, parts_of(v), ABT) for c, v in zip(coeffs, inverse)]
    maps = [parts_of(m) for m in maps]
    low_group = upper == 0
    rows = []
    for e in (0, 1):
        line = []
        for f in (2, 3):
            a, b = me ^ e, me ^ f
            index = jnp.where(low_group, 6 + 2 * a + (b - 2), 6 + 2 * b + (a - 2))
            line.append(side(index, upper == 1))
        rows.append(jnp.concatenate(line, 1))
    across = parts_of(jnp.concatenate(rows, 0))
    cross = product(maps[0], parts_of(product(across, maps[1])), ATB)
    cross = parts_of(cross / cells)
    start = start_ref[1].astype(jnp.float32)
    top, bottom = start[:128], start[128:]
    exact = True
    for _ in range(2):
        top, bottom = (
            top + product(cross, parts_of(bottom, exact)),
            bottom + product(cross, parts_of(top, exact), ATB),
        )
        exact = False
    top, bottom = (top.astype(jnp.bfloat16),), (bottom.astype(jnp.bfloat16),)
    mixed = product(top, parts_of(product(cross, bottom)), ATB)
    inner = product(top, top, ATB) + product(bottom, bottom, ATB) + mixed + mixed.T
    (last,) = inverse_factors([inner])
    last = parts_of(last)
    for half, coeff in enumerate((top, bottom)):
        step = product(coeff, last, ABT)
        final = product(maps[half], parts_of(step))
        high = final.astype(jnp.bfloat16)
        high_ref[pl.ds(256 * half, 256), :] = high
        low_ref[pl.ds(256 * half, 256), :] = (final - high.astype(jnp.float32)).astype(jnp.bfloat16)


NY, LANES, PAD = 512, 128, 8
WIDE = PAD + NY + PAD
GROUP = 128
INNER, OUTER = 10 * GROUP, 6 * GROUP
PIECE = INNER + OUTER


def spread_faces(perm_ref, east, north, count):
    def one(g, _):
        at0 = pl.multiple_of(g * 8, 8)
        here = perm_ref[pl.ds(at0, 8)]
        after = perm_ref[pl.ds(at0 + 8, 8)]
        sub = lax.broadcasted_iota(jnp.int32, (8, LANES), 0)
        shifted = pltpu.roll(jnp.where(sub == 0, after, here), 7, axis=0)
        e = 0.12 * (here + shifted)
        n = 0.12 * (here + pltpu.roll(here, LANES - 1, axis=1))
        for i in range(count):
            east[i, pl.ds(at0, 8)] = jnp.broadcast_to(e[:, i : i + 1], (8, LANES))
            north[i, pl.ds(at0, 8)] = jnp.broadcast_to(n[:, i : i + 1], (8, LANES))
        return 0

    lax.fori_loop(0, (PAD + NY) // 8, one, 0, unroll=5)


def set_perm(perm_ref, rows):
    count = rows.shape[0]
    rows = jnp.concatenate([rows, jnp.zeros((LANES - count, NY), jnp.float32)], 0)
    perm_ref[0:PAD] = jnp.zeros((PAD, LANES), jnp.float32)
    perm_ref[PAD : PAD + NY] = rows.T
    perm_ref[PAD + NY : WIDE] = jnp.zeros((PAD, LANES), jnp.float32)


def clear_pads(buf, count):
    def one(i, _):
        buf[i, 0:PAD] = jnp.zeros((PAD, LANES), jnp.float32)
        buf[i, PAD + NY : WIDE] = jnp.zeros((PAD, LANES), jnp.float32)
        return 0

    lax.fori_loop(0, count, one, 0)


def sweep(source, east, north, begin, face, count, write):
    for g in range(NY // GROUP):
        c = PAD + g * GROUP

        def one(i, carry, c=c, g=g):
            row, plane = begin + i, face + i
            center, south = carry
            above = source[row + 1, c : c + GROUP]
            up = north[plane, c : c + GROUP] * (above - center)
            east_here = east[plane, c : c + GROUP]
            flux = east_here * (source[row, c + 1 : c + GROUP + 1] - center)
            before = source[row, c - PAD : c]
            edge = east[plane, c - PAD : c] * (source[row, c - PAD + 1 : c + 1] - before)
            shifted = jnp.concatenate([edge, flux], 0)[PAD - 1 : PAD - 1 + GROUP]
            write(i, g, center + ((up - south) + (flux - shifted)))
            return above, up

        center = source[begin, c : c + GROUP]
        south = north[face - 1, c : c + GROUP] * (center - source[begin - 1, c : c + GROUP])
        lax.fori_loop(0, count, one, (center, south))


def into(buf, base):
    def write(i, g, value):
        buf[base + i, PAD + g * GROUP : PAD + g * GROUP + GROUP] = value

    return write


def into_snap(snap, base, scale_ref):
    scale = jnp.sqrt(jnp.full((8, LANES), scale_ref[0].astype(jnp.float32)))
    scale = jnp.broadcast_to(scale[0:1], (GROUP, LANES))

    def write(i, g, value):
        at0 = pl.multiple_of((base + i) * GROUP, GROUP)
        snap[g, pl.ds(at0, GROUP)] = (value * scale).astype(jnp.bfloat16)

    return write


def send_out(me, snap, singles, moves, sems):
    copies = []
    for e in (1, 2, 3):
        copies.append(pltpu.make_async_copy(snap.at[me ^ e], singles[e - 1], sems.at[len(copies)]))
        for stacks, j, begin, size in moves:
            target = stacks[e - 1].at[pl.ds(begin, size)]
            copies.append(pltpu.make_async_copy(snap.at[me ^ e ^ j], target, sems.at[len(copies)]))
    for copy in copies:
        copy.start()
    return copies


def inner_rows(me_ref, scale_ref, own_ref, kp_ref, *refs):
    singles, near, late, edge_one, edge_two = refs[:3], refs[3:6], refs[6:9], refs[9], refs[10]
    first, second, east, north, perm_ref, snap, held, sems, edge_sems = refs[11:]
    me = me_ref[0]
    load = pltpu.make_async_copy(own_ref, held, sems.at[0])
    load.start()
    clear_pads(first, 16)
    clear_pads(second, 16)

    def fill(i, _):
        first[i, PAD : PAD + NY] = held[i].astype(jnp.float32)
        return 0

    set_perm(perm_ref, kp_ref[...])
    spread_faces(perm_ref, east, north, 15)
    load.wait()
    lax.fori_loop(0, 16, fill, 0)
    sweep(first, east, north, 1, 1, 14, into(second, 1))
    sweep(second, east, north, 2, 2, 12, into(first, 2))
    edges_out = [
        pltpu.make_async_copy(second.at[pl.ds(1, 2)], edge_one.at[pl.ds(0, 2)], edge_sems.at[0]),
        pltpu.make_async_copy(second.at[pl.ds(13, 2)], edge_one.at[pl.ds(2, 2)], edge_sems.at[1]),
        pltpu.make_async_copy(first.at[pl.ds(2, 2)], edge_two.at[pl.ds(0, 2)], edge_sems.at[2]),
        pltpu.make_async_copy(first.at[pl.ds(12, 2)], edge_two.at[pl.ds(2, 2)], edge_sems.at[3]),
    ]
    for copy in edges_out:
        copy.start()
    sweep(first, east, north, 3, 3, 10, into_snap(snap, 0, scale_ref))
    moves = ((near, 1, 0, INNER), (late, 3, 0, INNER), (late, 2, PIECE, INNER))
    for copy in edges_out + send_out(me, snap, singles, moves, sems):
        copy.wait()


def outer_rows(me_ref, tile_ref, scale_ref, own_hbm, kp_ref, low_hbm, high_hbm, edge_one, edge_two, *refs):
    singles, near, late = refs[6:9], refs[9:12], refs[12:15]
    low0, low1, low2, high0, high1, high2, east, north, perm_ref, snap = refs[15:25]
    low_ref, high_ref, own_ref, sems, edge_sems = refs[25:]
    me, tile = me_ref[0], tile_ref[0]
    loads = [
        pltpu.make_async_copy(low_hbm, low_ref, sems.at[0]),
        pltpu.make_async_copy(high_hbm, high_ref, sems.at[1]),
        pltpu.make_async_copy(own_hbm.at[pl.ds(0, 2)], own_ref.at[pl.ds(0, 2)], sems.at[2]),
        pltpu.make_async_copy(own_hbm.at[pl.ds(14, 2)], own_ref.at[pl.ds(2, 2)], sems.at[3]),
    ]
    for copy in loads:
        copy.start()
    edges_in = [
        pltpu.make_async_copy(edge_one.at[pl.ds(0, 2)], low1.at[pl.ds(3, 2)], edge_sems.at[0]),
        pltpu.make_async_copy(edge_one.at[pl.ds(2, 2)], high1.at[pl.ds(0, 2)], edge_sems.at[1]),
        pltpu.make_async_copy(edge_two.at[pl.ds(0, 2)], low2.at[pl.ds(3, 2)], edge_sems.at[2]),
        pltpu.make_async_copy(edge_two.at[pl.ds(2, 2)], high2.at[pl.ds(0, 2)], edge_sems.at[3]),
    ]
    for copy in edges_in:
        copy.start()
    for buf in (low0, high0):
        clear_pads(buf, 5)
    for buf in (low1, low2):
        clear_pads(buf, 3)
    for buf in (high1, high2):
        clear_pads(buf.at[pl.ds(2, 3)], 3)
    for copy in loads:
        copy.wait()
    for i in range(3):
        low0[i, PAD : PAD + NY] = low_ref[NY * i : NY * i + NY].astype(jnp.float32)
        high0[2 + i, PAD : PAD + NY] = high_ref[NY * i : NY * i + NY].astype(jnp.float32)
    for i in range(2):
        low0[3 + i, PAD : PAD + NY] = own_ref[i].astype(jnp.float32)
        high0[i, PAD : PAD + NY] = own_ref[2 + i].astype(jnp.float32)

    def far_perm(ref):
        both = ref[3 * NY : 3 * NY + 32].astype(jnp.float32)
        packed = both[0:12] + both[12:24]
        return [
            jnp.concatenate([packed[4 * i + q : 4 * i + q + 1] for q in range(4)], 1) for i in range(3)
        ]

    kp = kp_ref[...]
    set_perm(perm_ref, jnp.concatenate(far_perm(low_ref) + [kp[0:4], kp[12:16]] + far_perm(high_ref), 0))
    spread_faces(perm_ref, east, north, 13)
    sweep(low0, east, north, 1, 1, 3, into(low1, 0))
    sweep(high0, east, north, 1, 10, 3, into(high1, 2))
    blank = jnp.zeros((NY, LANES), jnp.float32)

    @pl.when(tile == 0)
    def _():
        low1[0, PAD : PAD + NY] = blank
        low1[1, PAD : PAD + NY] = blank

    @pl.when(tile == 63)
    def _():
        high1[3, PAD : PAD + NY] = blank
        high1[4, PAD : PAD + NY] = blank

    for copy in edges_in:
        copy.wait()
    sweep(low1, east, north, 1, 2, 3, into(low2, 0))
    sweep(high1, east, north, 1, 9, 3, into(high2, 2))

    @pl.when(tile == 0)
    def _():
        low2[0, PAD : PAD + NY] = blank

    @pl.when(tile == 63)
    def _():
        high2[4, PAD : PAD + NY] = blank

    sweep(low2, east, north, 1, 3, 3, into_snap(snap, 0, scale_ref))
    sweep(high2, east, north, 1, 8, 3, into_snap(snap, 3, scale_ref))
    moves = ((near, 1, INNER, OUTER), (near, 2, PIECE, OUTER), (late, 3, INNER, OUTER))
    for copy in send_out(me, snap, singles, moves, sems):
        copy.wait()


VM = pl.BlockSpec(memory_space=pltpu.VMEM)
SM = pl.BlockSpec(memory_space=pltpu.SMEM)
ANY = pl.BlockSpec(memory_space=pl.ANY)


def half(rows):
    return jax.ShapeDtypeStruct((rows, LANES), jnp.bfloat16)


def planes(count):
    return pltpu.VMEM((count, WIDE, LANES), jnp.float32)


def inner_call(me, weights, own, kp):
    edge = jax.ShapeDtypeStruct((4, WIDE, LANES), jnp.float32)
    return pl.pallas_call(
        inner_rows,
        out_shape=[half(INNER)] * 3 + [half(PIECE + OUTER)] * 3 + [half(PIECE + INNER)] * 3 + [edge] * 2,
        in_specs=[SM, SM, ANY, VM],
        out_specs=[ANY] * 11,
        scratch_shapes=[planes(16), planes(16), planes(15), planes(15)]
        + [pltpu.VMEM((WIDE, LANES), jnp.float32), pltpu.VMEM((4, INNER, LANES), jnp.bfloat16)]
        + [pltpu.VMEM((16, NY, LANES), jnp.bfloat16)]
        + [pltpu.SemaphoreType.DMA((12,)), pltpu.SemaphoreType.DMA((4,))],
        compiler_params=pltpu.CompilerParams(vmem_limit_bytes=63 << 20),
        cost_estimate=pl.CostEstimate(flops=400 << 20, bytes_accessed=9 << 20, transcendentals=0),
    )(me, weights, own, kp)


def outer_call(me, tile, weights, own, kp, low, high, edge_one, edge_two, stacks):
    return pl.pallas_call(
        outer_rows,
        out_shape=[half(OUTER)] * 3 + [half(PIECE + OUTER)] * 3 + [half(PIECE + INNER)] * 3,
        in_specs=[SM, SM, SM, ANY, VM] + [ANY] * 10,
        out_specs=[ANY] * 9,
        input_output_aliases={9 + n: 3 + n for n in range(6)},
        scratch_shapes=[planes(5)] * 6
        + [planes(13), planes(13), pltpu.VMEM((WIDE, LANES), jnp.float32)]
        + [pltpu.VMEM((4, OUTER, LANES), jnp.bfloat16)]
        + [pltpu.VMEM((3 * NY + 32, LANES), jnp.bfloat16)] * 2
        + [pltpu.VMEM((4, NY, LANES), jnp.bfloat16)]
        + [pltpu.SemaphoreType.DMA((12,)), pltpu.SemaphoreType.DMA((4,))],
        compiler_params=pltpu.CompilerParams(vmem_limit_bytes=63 << 20),
        cost_estimate=pl.CostEstimate(flops=200 << 20, bytes_accessed=9 << 20, transcendentals=0),
    )(me, tile, weights, own, kp, low, high, edge_one, edge_two, *stacks)


def grams(me_ref, core_ref, *refs):
    pieces, own_ref, other_ref, wide, sems = refs[:7], refs[7], refs[8], refs[9], refs[10]
    me, core = me_ref[0], core_ref[0]
    copies = []
    for e in range(4):
        lanes = pl.ds(pl.multiple_of((me ^ e) * 128, 128), 128)
        if e == 0:
            moves = [(pieces[0].at[pl.ds(0, PIECE)], 0, PIECE)]
        else:
            moves = [(pieces[e], 0, INNER), (pieces[3 + e], INNER, OUTER)]
        for source, begin, size in moves:
            target = wide.at[pl.ds(begin, size), lanes]
            copies.append(pltpu.make_async_copy(source, target, sems.at[len(copies)]))
    for copy in copies:
        copy.start()
    for copy in copies:
        copy.wait()
    left, right = wide[:, :256], wide[:, 256:]
    near = lax.dot_general(left, left, ATB, preferred_element_type=jnp.float32)
    far = lax.dot_general(right, right, ATB, preferred_element_type=jnp.float32)
    cross = lax.dot_general(left, right, ATB, preferred_element_type=jnp.float32)
    blocks = [
        near[:128, :128], near[128:, 128:], far[:128, :128], far[128:, 128:], near[:128, 128:],
        far[:128, 128:], cross[:128, :128], cross[:128, 128:], cross[128:, :128], cross[128:, 128:],
    ]
    for side in (0, 1):

        @pl.when(core == side)
        def _(side=side):
            for half, ref in enumerate((own_ref, other_ref) if side == 0 else (other_ref, own_ref)):
                mine = blocks[5 * half : 5 * half + 5]
                ref[:, 0:16] = jnp.concatenate(mine[:4], 0).reshape(32, 16, 128)
                ref[:, 16:24] = jnp.zeros((32, 8, 128), jnp.float32)
                for k in range(32):
                    ref[k, 16:20] = mine[4][4 * k : 4 * k + 4]


def grams_call(me, core, pieces):
    shape = jax.ShapeDtypeStruct((32, 24, 128), jnp.float32)
    return pl.pallas_call(
        grams,
        out_shape=(shape, shape),
        in_specs=[SM, SM] + [ANY] * 7,
        out_specs=(VM, VM),
        scratch_shapes=[pltpu.VMEM((PIECE, 512), jnp.bfloat16), pltpu.SemaphoreType.DMA((7,))],
        compiler_params=pltpu.CompilerParams(vmem_limit_bytes=63 << 20),
        cost_estimate=pl.CostEstimate(flops=2 * 2048 * 512 * 512, bytes_accessed=3 << 20, transcendentals=0),
    )(me, core, *pieces)


def mixing_call(cells, me, core, own, other, start_codes):
    shape = jax.ShapeDtypeStruct((512, 128), jnp.bfloat16)
    vmem = pl.BlockSpec(memory_space=pltpu.VMEM)
    smem = pl.BlockSpec(memory_space=pltpu.SMEM)
    return pl.pallas_call(
        functools.partial(mixing, cells),
        out_shape=(shape, shape),
        in_specs=[smem, smem, ANY, ANY, vmem],
        out_specs=(vmem, vmem),
        scratch_shapes=[pltpu.VMEM((10, 128, 128), jnp.float32)]
        + [pltpu.VMEM((32, 24, 128), jnp.float32)] * 2
        + [pltpu.SemaphoreType.DMA((2,))],
        compiler_params=pltpu.CompilerParams(vmem_limit_bytes=62 << 20),
        cost_estimate=pl.CostEstimate(flops=1 << 30, bytes_accessed=1 << 20, transcendentals=0),
    )(me, core, own, other, start_codes)


def finish(plan, me_ref, high_ref, low_ref, *refs):
    pieces, out_ref = refs[:-5], refs[-5]
    wide, done, in_sems, out_sems = refs[-4:]
    me = me_ref[0]
    loads = []
    for j in range(4):
        group = []
        for e in range(4):
            for index, source, target, size in plan[4 * j + e]:
                group.append(
                    pltpu.make_async_copy(
                        pieces[index].at[pl.ds(source, size)],
                        wide.at[j, pl.ds(target, size), pl.ds(128 * e, 128)],
                        in_sems.at[len(loads), len(group)],
                    )
                )
                group[-1].start()
        loads.append(group)
    mix = jnp.concatenate([high_ref[...], low_ref[...]], 1)
    stores = []
    for j in range(4):
        for copy in loads[j]:
            copy.wait()
        for r in range(16):
            both = jnp.dot(wide[j, 128 * r : 128 * r + 128], mix, preferred_element_type=jnp.float32)
            done[j, r] = (both[:, :128] + both[:, 128:]).astype(jnp.bfloat16)
        columns = pl.ds(pl.multiple_of((me ^ j) * GROUP, GROUP), GROUP)
        for n, (source, target, size) in enumerate(((0, 3, 10), (10, 0, 3), (13, 13, 3))):
            copy = pltpu.make_async_copy(
                done.at[j, pl.ds(source, size)], out_ref.at[pl.ds(target, size), columns], out_sems.at[j, n]
            )
            copy.start()
            stores.append(copy)
    for copy in stores:
        copy.wait()


def finish_call(me, high, low, pieces, plan):
    return pl.pallas_call(
        functools.partial(finish, plan),
        out_shape=jax.ShapeDtypeStruct((16, NY, LANES), jnp.bfloat16),
        in_specs=[SM, VM, VM] + [ANY] * len(pieces),
        out_specs=ANY,
        scratch_shapes=[
            pltpu.VMEM((4, PIECE, 512), jnp.bfloat16),
            pltpu.VMEM((4, 16, GROUP, LANES), jnp.bfloat16),
            pltpu.SemaphoreType.DMA((4, 8)),
            pltpu.SemaphoreType.DMA((4, 3)),
        ],
        compiler_params=pltpu.CompilerParams(vmem_limit_bytes=63 << 20),
        cost_estimate=pl.CostEstimate(flops=2 * 8192 * 512 * 256, bytes_accessed=10 << 20, transcendentals=0),
    )(me, high, low, *pieces)


def packed_edge(cells, perm):
    high = perm.astype(jnp.bfloat16)
    low = (perm - high.astype(jnp.float32)).astype(jnp.bfloat16)
    parts = [cells.reshape(-1, LANES), high.reshape(-1, LANES), low.reshape(-1, LANES)]
    return jnp.concatenate(parts + [jnp.zeros((8, LANES), jnp.bfloat16)], 0)


def merged_bases(forcing, permeability, merge_weights, start_codes):
    me = lax.axis_index("case").astype(jnp.int32).reshape(1)
    tile = lax.axis_index("tile").astype(jnp.int32).reshape(1)
    core = tile & 1
    cells = forcing.shape[1] * lax.axis_size("tile") * forcing.shape[2]
    own, kp = forcing[0], permeability[0]
    up = [(i, i + 1) for i in range(63)]
    down = [(i + 1, i) for i in range(63)]
    low = lax.ppermute(packed_edge(own[-STEPS:], kp[-STEPS:]), "tile", up)
    high = lax.ppermute(packed_edge(own[:STEPS], kp[:STEPS]), "tile", down)
    inner = inner_call(me, merge_weights, own, kp)
    met = [case_swap(inner[e - 1], e) for e in (1, 2, 3)]
    outer = outer_call(me, tile, merge_weights, own, kp, low, high, inner[9], inner[10], inner[3:9])
    near, late = outer[3:6], outer[6:9]
    met = met + [case_swap(outer[e - 1], e) for e in (1, 2, 3)]
    far = [case_swap(near[e - 1], e) for e in (1, 2, 3)]
    far = far + [case_swap(late[e - 1], e) for e in (1, 2, 3)]
    own_part, other_part = grams_call(me, core, [near[0]] + met)
    part = own_part + core_swap(other_part)
    part = plane_exchange(part).sum(0)
    part = part + case_swap(part, 1) + case_swap(part, 2) + case_swap(part, 3)
    mine = plane_exchange(jnp.broadcast_to(part, (32,) + part.shape))
    yours = core_swap(mine)
    high, low = mixing_call(cells, me, core, mine, yours, start_codes)
    plan = []
    for j in range(4):
        for e in range(4):
            if e == 0:
                plan.append((({0: 0, 3: 1, 2: 2, 1: 3}[j], 0, 0, PIECE),))
            elif j == 0:
                plan.append(((3 + e, 0, 0, INNER), (6 + e, 0, INNER, OUTER)))
            elif j == 2:
                plan.append(((12 + e, PIECE, 0, INNER), (9 + e, PIECE, INNER, OUTER)))
            else:
                plan.append(((9 + e if j == 1 else 12 + e, 0, 0, PIECE),))
    pieces = [near[0], near[1], near[2], late[1]] + met + far
    return finish_call(me, high, low, pieces, tuple(plan)).reshape(1, -1, LANES)


def solution(mesh):
    placed = (P("case", "tile", None, None), P("case", "tile", None), P("case"), P())
    return jax.shard_map(
        merged_bases, mesh=mesh, in_specs=placed, out_specs=P("case", "tile", None), check_vma=False
    )
```

```python
import functools
import math

import jax
import jax.numpy as jnp
from jax import lax
from jax.experimental import pallas as pl
from jax.experimental.pallas import tpu as pltpu
from jax.sharding import PartitionSpec as P

STEPS = 3


def at(z, y, core):
    return (z * 4 + y) * 2 + core


PLANES = [[at(z, y, core) for z in range(8) for y in range(4)] for core in range(2)]


def case_swap(value, apart):
    return lax.ppermute(value, "case", [(source, source ^ apart) for source in range(4)])


def core_swap(value):
    return lax.ppermute(value, "tile", [(source, source ^ 1) for source in range(64)])


def plane_exchange(value):
    return lax.all_to_all(value, "tile", 0, 0, axis_index_groups=PLANES)


AB = (((1,), (0,)), ((), ()))
ATB = (((0,), (0,)), ((), ()))
ABT = (((1,), (1,)), ((), ()))


def parts_of(x, exact=False):
    high = x.astype(jnp.bfloat16)
    if exact:
        return (high,)
    rest = x - high.astype(jnp.float32)
    mid = rest.astype(jnp.bfloat16)
    low = (rest - mid.astype(jnp.float32)).astype(jnp.bfloat16)
    return (high, mid, low)


def product(a, b, dims=AB):
    out = None
    for i in range(len(a) - 1, -1, -1):
        for j in range(len(b) - 1, -1, -1):
            if i + j < 3:
                term = lax.dot_general(a[i], b[j], dims, preferred_element_type=jnp.float32)
                out = term if out is None else out + term
    return out


def spread(x, axis, index, size):
    piece = lax.slice_in_dim(x, index, index + 1, axis=axis)
    shape = (size, x.shape[1]) if axis == 0 else (x.shape[0], size)
    return jnp.broadcast_to(piece, shape)


def inverse_factors(mats):
    lane = lax.broadcasted_iota(jnp.int32, (8, 128), 1)
    sub = lax.broadcasted_iota(jnp.int32, (8, 128), 0)
    tiles = [[m[8 * b : 8 * b + 8] for b in range(16)] for m in mats]
    for k in range(16):
        first = 8 * k
        block = (lane >= first) & (lane < first + 8)
        for a in tiles:
            rows = [spread(a[k], 0, r, 8) for r in range(8)]
            piv = [
                [spread(rows[r], 1, first + s, 128) if s >= r else None for s in range(8)]
                for r in range(8)
            ]
            inv = [None] * 8
            mul = [[None] * 8 for _ in range(8)]
            for r in range(8):
                inv[r] = 1.0 / piv[r][r]
                for s in range(r + 1, 8):
                    mul[r][s] = piv[r][s] * inv[r]
                for s in range(r + 1, 8):
                    for t in range(s, 8):
                        piv[s][t] = piv[s][t] - mul[r][s] * piv[r][t]
            for s in range(8):
                rows[s] = jnp.where(block, jnp.where(lane == first + s, 1.0, 0.0), rows[s])
            for s in range(8):
                for r in range(s):
                    rows[s] = rows[s] - mul[r][s] * rows[r]
            scaled = [rows[r] * inv[r] for r in range(8)]
            for b in range(k + 1, 16):
                col = [spread(a[b], 1, first + r, 128) for r in range(8)]
                for r in range(8):
                    for s in range(r + 1, 8):
                        col[s] = col[s] - col[r] * mul[r][s]
                new = jnp.where(block, 0.0, a[b])
                for r in range(8):
                    new = new - col[r] * scaled[r]
                a[b] = new
            done = jnp.zeros((8, 128), jnp.float32)
            for r in range(8):
                done = jnp.where(sub == r, rows[r] * lax.rsqrt(piv[r][r]), done)
            a[k] = jnp.where(lane < first + 8, done, 0.0)
    return [jnp.concatenate(a, 0) for a in tiles]


def mixing(cells, me_ref, core_ref, own_hbm, other_hbm, start_ref, high_ref, low_ref, *scratch):
    gram_ref, own_ref, other_ref, sems = scratch
    me, core = me_ref[0], core_ref[0]
    loads = [
        pltpu.make_async_copy(own_hbm, own_ref, sems.at[0]),
        pltpu.make_async_copy(other_hbm, other_ref, sems.at[1]),
    ]
    for copy in loads:
        copy.start()
    for copy in loads:
        copy.wait()
    for side in (0, 1):

        @pl.when(core == side)
        def _(side=side):
            for half, ref in enumerate((own_ref, other_ref) if side == 0 else (other_ref, own_ref)):
                rows = ref[:, 0:16].reshape(4, 128, 128)
                for i in range(4):
                    gram_ref[5 * half + i] = rows[i]
                for k in range(32):
                    gram_ref[5 * half + 4, 4 * k : 4 * k + 4] = ref[k, 16:20]

    odd = lax.rem(me, 2) == 1
    upper = me // 2

    def side(index, flip):
        x = gram_ref[index]
        return jnp.where(flip, x.T, x)

    def merged(coeff_parts, gram_parts):
        t = product(gram_parts, coeff_parts)
        return product(coeff_parts, parts_of(t), ATB)

    start = parts_of(start_ref[0].astype(jnp.float32), True)
    coeffs, inners = [], []
    for half in (0, 1):
        a, b = me ^ (2 * half), me ^ (2 * half + 1)
        near = side(4 + (upper ^ half), odd)
        gram = jnp.concatenate(
            [jnp.concatenate([gram_ref[a], near], 1), jnp.concatenate([near.T, gram_ref[b]], 1)], 0
        )
        gram = parts_of(gram)
        first = product(gram, start) / cells
        second = product(gram, parts_of(first)) / cells
        coeff = (second.astype(jnp.bfloat16),)
        coeffs.append(coeff)
        inners.append(merged(coeff, gram))
    inverse = inverse_factors(inners)
    scale = math.sqrt(cells)
    maps = [scale * product(c, parts_of(v), ABT) for c, v in zip(coeffs, inverse)]
    maps = [parts_of(m) for m in maps]
    low_group = upper == 0
    rows = []
    for e in (0, 1):
        line = []
        for f in (2, 3):
            a, b = me ^ e, me ^ f
            index = jnp.where(low_group, 6 + 2 * a + (b - 2), 6 + 2 * b + (a - 2))
            line.append(side(index, upper == 1))
        rows.append(jnp.concatenate(line, 1))
    across = parts_of(jnp.concatenate(rows, 0))
    cross = product(maps[0], parts_of(product(across, maps[1])), ATB)
    cross = parts_of(cross / cells)
    start = start_ref[1].astype(jnp.float32)
    top, bottom = start[:128], start[128:]
    exact = True
    for _ in range(2):
        top, bottom = (
            top + product(cross, parts_of(bottom, exact)),
            bottom + product(cross, parts_of(top, exact), ATB),
        )
        exact = False
    top, bottom = (top.astype(jnp.bfloat16),), (bottom.astype(jnp.bfloat16),)
    mixed = product(top, parts_of(product(cross, bottom)), ATB)
    inner = product(top, top, ATB) + product(bottom, bottom, ATB) + mixed + mixed.T
    (last,) = inverse_factors([inner])
    last = parts_of(last)
    for half, coeff in enumerate((top, bottom)):
        step = product(coeff, last, ABT)
        final = product(maps[half], parts_of(step))
        high = final.astype(jnp.bfloat16)
        high_ref[pl.ds(256 * half, 256), :] = high
        low_ref[pl.ds(256 * half, 256), :] = (final - high.astype(jnp.float32)).astype(jnp.bfloat16)


NY, LANES, PAD = 512, 128, 8
WIDE = PAD + NY + PAD
GROUP = 128
INNER, OUTER = 10 * GROUP, 6 * GROUP
PIECE = INNER + OUTER


def spread_faces(perm_ref, east, north, count):
    here = perm_ref[...]
    after = jnp.concatenate([here[1:], here[:1]], 0)
    row = lax.broadcasted_iota(jnp.int32, (256, 256), 0) & 127
    second = lax.broadcasted_iota(jnp.int32, (256, 256), 1) >> 7
    faces = []
    for value in (0.12 * (here + after), 0.12 * (here + pltpu.roll(here, LANES - 1, axis=1))):
        high = value.astype(jnp.bfloat16)
        low = (value - high.astype(jnp.float32)).astype(jnp.bfloat16)
        faces.append(jnp.concatenate([high, low], 1))
    for i in range(0, count, 2):
        pick = jnp.where(row == second + i, 1.0, 0.0).astype(jnp.bfloat16)
        for face, out in zip(faces, (east, north)):
            both = jnp.dot(face, pick, preferred_element_type=jnp.float32)
            out[i] = both[:, :LANES]
            if i + 1 < count:
                out[i + 1] = both[:, LANES:]


def set_perm(perm_ref, rows):
    count = rows.shape[0]
    rows = jnp.concatenate([rows, jnp.zeros((LANES - count, NY), jnp.float32)], 0)
    perm_ref[0:PAD] = jnp.zeros((PAD, LANES), jnp.float32)
    perm_ref[PAD : PAD + NY] = rows.T
    perm_ref[PAD + NY : WIDE] = jnp.zeros((PAD, LANES), jnp.float32)


def clear_pads(buf, count):
    def one(i, _):
        buf[i, 0:PAD] = jnp.zeros((PAD, LANES), jnp.float32)
        buf[i, PAD + NY : WIDE] = jnp.zeros((PAD, LANES), jnp.float32)
        return 0

    lax.fori_loop(0, count, one, 0)


def sweep(source, east, north, begin, face, count, write):
    for g in range(NY // GROUP):
        c = PAD + g * GROUP

        def one(i, carry, c=c, g=g):
            row, plane = begin + i, face + i
            center, south = carry
            above = source[row + 1, c : c + GROUP]
            up = north[plane, c : c + GROUP] * (above - center)
            east_here = east[plane, c : c + GROUP]
            flux = east_here * (source[row, c + 1 : c + GROUP + 1] - center)
            before = source[row, c - PAD : c]
            edge = east[plane, c - PAD : c] * (source[row, c - PAD + 1 : c + 1] - before)
            shifted = jnp.concatenate([edge, flux], 0)[PAD - 1 : PAD - 1 + GROUP]
            write(i, g, center + ((up - south) + (flux - shifted)))
            return above, up

        center = source[begin, c : c + GROUP]
        south = north[face - 1, c : c + GROUP] * (center - source[begin - 1, c : c + GROUP])
        lax.fori_loop(0, count, one, (center, south))


def into(buf, base):
    def write(i, g, value):
        buf[base + i, PAD + g * GROUP : PAD + g * GROUP + GROUP] = value

    return write


def into_snap(snap, base, scale_ref):
    scale = jnp.sqrt(jnp.full((8, LANES), scale_ref[0].astype(jnp.float32)))
    scale = jnp.broadcast_to(scale[0:1], (GROUP, LANES))

    def write(i, g, value):
        at0 = pl.multiple_of((base + i) * GROUP, GROUP)
        snap[g, pl.ds(at0, GROUP)] = (value * scale).astype(jnp.bfloat16)

    return write


def send_out(me, snap, singles, moves, sems):
    copies = []
    for e in (1, 2, 3):
        copies.append(pltpu.make_async_copy(snap.at[me ^ e], singles[e - 1], sems.at[len(copies)]))
        for stacks, j, begin, size in moves:
            target = stacks[e - 1].at[pl.ds(begin, size)]
            copies.append(pltpu.make_async_copy(snap.at[me ^ e ^ j], target, sems.at[len(copies)]))
    for copy in copies:
        copy.start()
    return copies


def inner_rows(me_ref, scale_ref, own_ref, kp_ref, *refs):
    singles, near, late, edge_one, edge_two = refs[:3], refs[3:6], refs[6:9], refs[9], refs[10]
    first, second, east, north, perm_ref, snap, held, sems, edge_sems = refs[11:]
    me = me_ref[0]
    load = pltpu.make_async_copy(own_ref, held, sems.at[0])
    load.start()
    clear_pads(first, 16)
    clear_pads(second, 16)

    def fill(i, _):
        first[i, PAD : PAD + NY] = held[i].astype(jnp.float32)
        return 0

    set_perm(perm_ref, kp_ref[...])
    spread_faces(perm_ref, east, north, 15)
    load.wait()
    lax.fori_loop(0, 16, fill, 0)
    sweep(first, east, north, 1, 1, 14, into(second, 1))
    sweep(second, east, north, 2, 2, 12, into(first, 2))
    edges_out = [
        pltpu.make_async_copy(second.at[pl.ds(1, 2)], edge_one.at[pl.ds(0, 2)], edge_sems.at[0]),
        pltpu.make_async_copy(second.at[pl.ds(13, 2)], edge_one.at[pl.ds(2, 2)], edge_sems.at[1]),
        pltpu.make_async_copy(first.at[pl.ds(2, 2)], edge_two.at[pl.ds(0, 2)], edge_sems.at[2]),
        pltpu.make_async_copy(first.at[pl.ds(12, 2)], edge_two.at[pl.ds(2, 2)], edge_sems.at[3]),
    ]
    for copy in edges_out:
        copy.start()
    sweep(first, east, north, 3, 3, 10, into_snap(snap, 0, scale_ref))
    moves = ((near, 1, 0, INNER), (late, 3, 0, INNER), (late, 2, PIECE, INNER))
    for copy in edges_out + send_out(me, snap, singles, moves, sems):
        copy.wait()


def outer_rows(me_ref, tile_ref, scale_ref, own_hbm, kp_ref, low_hbm, high_hbm, edge_one, edge_two, *refs):
    singles, near, late = refs[6:9], refs[9:12], refs[12:15]
    low0, low1, low2, high0, high1, high2, east, north, perm_ref, snap = refs[15:25]
    low_ref, high_ref, own_ref, sems, edge_sems = refs[25:]
    me, tile = me_ref[0], tile_ref[0]
    loads = [
        pltpu.make_async_copy(low_hbm, low_ref, sems.at[0]),
        pltpu.make_async_copy(high_hbm, high_ref, sems.at[1]),
        pltpu.make_async_copy(own_hbm.at[pl.ds(0, 2)], own_ref.at[pl.ds(0, 2)], sems.at[2]),
        pltpu.make_async_copy(own_hbm.at[pl.ds(14, 2)], own_ref.at[pl.ds(2, 2)], sems.at[3]),
    ]
    for copy in loads:
        copy.start()
    edges_in = [
        pltpu.make_async_copy(edge_one.at[pl.ds(0, 2)], low1.at[pl.ds(3, 2)], edge_sems.at[0]),
        pltpu.make_async_copy(edge_one.at[pl.ds(2, 2)], high1.at[pl.ds(0, 2)], edge_sems.at[1]),
        pltpu.make_async_copy(edge_two.at[pl.ds(0, 2)], low2.at[pl.ds(3, 2)], edge_sems.at[2]),
        pltpu.make_async_copy(edge_two.at[pl.ds(2, 2)], high2.at[pl.ds(0, 2)], edge_sems.at[3]),
    ]
    for copy in edges_in:
        copy.start()
    for buf in (low0, high0):
        clear_pads(buf, 5)
    for buf in (low1, low2):
        clear_pads(buf, 3)
    for buf in (high1, high2):
        clear_pads(buf.at[pl.ds(2, 3)], 3)
    for copy in loads:
        copy.wait()
    for i in range(3):
        low0[i, PAD : PAD + NY] = low_ref[NY * i : NY * i + NY].astype(jnp.float32)
        high0[2 + i, PAD : PAD + NY] = high_ref[NY * i : NY * i + NY].astype(jnp.float32)
    for i in range(2):
        low0[3 + i, PAD : PAD + NY] = own_ref[i].astype(jnp.float32)
        high0[i, PAD : PAD + NY] = own_ref[2 + i].astype(jnp.float32)

    def far_perm(ref):
        both = ref[3 * NY : 3 * NY + 32].astype(jnp.float32)
        packed = both[0:12] + both[12:24]
        return [
            jnp.concatenate([packed[4 * i + q : 4 * i + q + 1] for q in range(4)], 1) for i in range(3)
        ]

    kp = kp_ref[...]
    set_perm(perm_ref, jnp.concatenate(far_perm(low_ref) + [kp[0:4], kp[12:16]] + far_perm(high_ref), 0))
    spread_faces(perm_ref, east, north, 13)
    sweep(low0, east, north, 1, 1, 3, into(low1, 0))
    sweep(high0, east, north, 1, 10, 3, into(high1, 2))
    blank = jnp.zeros((NY, LANES), jnp.float32)

    @pl.when(tile == 0)
    def _():
        low1[0, PAD : PAD + NY] = blank
        low1[1, PAD : PAD + NY] = blank

    @pl.when(tile == 63)
    def _():
        high1[3, PAD : PAD + NY] = blank
        high1[4, PAD : PAD + NY] = blank

    for copy in edges_in:
        copy.wait()
    sweep(low1, east, north, 1, 2, 3, into(low2, 0))
    sweep(high1, east, north, 1, 9, 3, into(high2, 2))

    @pl.when(tile == 0)
    def _():
        low2[0, PAD : PAD + NY] = blank

    @pl.when(tile == 63)
    def _():
        high2[4, PAD : PAD + NY] = blank

    sweep(low2, east, north, 1, 3, 3, into_snap(snap, 0, scale_ref))
    sweep(high2, east, north, 1, 8, 3, into_snap(snap, 3, scale_ref))
    moves = ((near, 1, INNER, OUTER), (near, 2, PIECE, OUTER), (late, 3, INNER, OUTER))
    for copy in send_out(me, snap, singles, moves, sems):
        copy.wait()


VM = pl.BlockSpec(memory_space=pltpu.VMEM)
SM = pl.BlockSpec(memory_space=pltpu.SMEM)
ANY = pl.BlockSpec(memory_space=pl.ANY)


def half(rows):
    return jax.ShapeDtypeStruct((rows, LANES), jnp.bfloat16)


def planes(count):
    return pltpu.VMEM((count, WIDE, LANES), jnp.float32)


def inner_call(me, weights, own, kp):
    edge = jax.ShapeDtypeStruct((4, WIDE, LANES), jnp.float32)
    return pl.pallas_call(
        inner_rows,
        out_shape=[half(INNER)] * 3 + [half(PIECE + OUTER)] * 3 + [half(PIECE + INNER)] * 3 + [edge] * 2,
        in_specs=[SM, SM, ANY, VM],
        out_specs=[ANY] * 11,
        scratch_shapes=[planes(16), planes(16), planes(15), planes(15)]
        + [pltpu.VMEM((WIDE, LANES), jnp.float32), pltpu.VMEM((4, INNER, LANES), jnp.bfloat16)]
        + [pltpu.VMEM((16, NY, LANES), jnp.bfloat16)]
        + [pltpu.SemaphoreType.DMA((12,)), pltpu.SemaphoreType.DMA((4,))],
        compiler_params=pltpu.CompilerParams(vmem_limit_bytes=63 << 20),
        cost_estimate=pl.CostEstimate(flops=400 << 20, bytes_accessed=9 << 20, transcendentals=0),
    )(me, weights, own, kp)


def outer_call(me, tile, weights, own, kp, low, high, edge_one, edge_two, stacks):
    return pl.pallas_call(
        outer_rows,
        out_shape=[half(OUTER)] * 3 + [half(PIECE + OUTER)] * 3 + [half(PIECE + INNER)] * 3,
        in_specs=[SM, SM, SM, ANY, VM] + [ANY] * 10,
        out_specs=[ANY] * 9,
        input_output_aliases={9 + n: 3 + n for n in range(6)},
        scratch_shapes=[planes(5)] * 6
        + [planes(13), planes(13), pltpu.VMEM((WIDE, LANES), jnp.float32)]
        + [pltpu.VMEM((4, OUTER, LANES), jnp.bfloat16)]
        + [pltpu.VMEM((3 * NY + 32, LANES), jnp.bfloat16)] * 2
        + [pltpu.VMEM((4, NY, LANES), jnp.bfloat16)]
        + [pltpu.SemaphoreType.DMA((12,)), pltpu.SemaphoreType.DMA((4,))],
        compiler_params=pltpu.CompilerParams(vmem_limit_bytes=63 << 20),
        cost_estimate=pl.CostEstimate(flops=200 << 20, bytes_accessed=9 << 20, transcendentals=0),
    )(me, tile, weights, own, kp, low, high, edge_one, edge_two, *stacks)


def grams(me_ref, core_ref, *refs):
    pieces, own_ref, other_ref, wide, sems = refs[:7], refs[7], refs[8], refs[9], refs[10]
    me, core = me_ref[0], core_ref[0]
    copies = []
    for e in range(4):
        lanes = pl.ds(pl.multiple_of((me ^ e) * 128, 128), 128)
        if e == 0:
            moves = [(pieces[0].at[pl.ds(0, PIECE)], 0, PIECE)]
        else:
            moves = [(pieces[e], 0, INNER), (pieces[3 + e], INNER, OUTER)]
        for source, begin, size in moves:
            target = wide.at[pl.ds(begin, size), lanes]
            copies.append(pltpu.make_async_copy(source, target, sems.at[len(copies)]))
    for copy in copies:
        copy.start()
    for copy in copies:
        copy.wait()
    left, right = wide[:, :256], wide[:, 256:]
    near = lax.dot_general(left, left, ATB, preferred_element_type=jnp.float32)
    far = lax.dot_general(right, right, ATB, preferred_element_type=jnp.float32)
    cross = lax.dot_general(left, right, ATB, preferred_element_type=jnp.float32)
    blocks = [
        near[:128, :128], near[128:, 128:], far[:128, :128], far[128:, 128:], near[:128, 128:],
        far[:128, 128:], cross[:128, :128], cross[:128, 128:], cross[128:, :128], cross[128:, 128:],
    ]
    for side in (0, 1):

        @pl.when(core == side)
        def _(side=side):
            for half, ref in enumerate((own_ref, other_ref) if side == 0 else (other_ref, own_ref)):
                mine = blocks[5 * half : 5 * half + 5]
                ref[:, 0:16] = jnp.concatenate(mine[:4], 0).reshape(32, 16, 128)
                ref[:, 16:24] = jnp.zeros((32, 8, 128), jnp.float32)
                for k in range(32):
                    ref[k, 16:20] = mine[4][4 * k : 4 * k + 4]


def grams_call(me, core, pieces):
    shape = jax.ShapeDtypeStruct((32, 24, 128), jnp.float32)
    return pl.pallas_call(
        grams,
        out_shape=(shape, shape),
        in_specs=[SM, SM] + [ANY] * 7,
        out_specs=(VM, VM),
        scratch_shapes=[pltpu.VMEM((PIECE, 512), jnp.bfloat16), pltpu.SemaphoreType.DMA((7,))],
        compiler_params=pltpu.CompilerParams(vmem_limit_bytes=63 << 20),
        cost_estimate=pl.CostEstimate(flops=2 * 2048 * 512 * 512, bytes_accessed=3 << 20, transcendentals=0),
    )(me, core, *pieces)


def mixing_call(cells, me, core, own, other, start_codes):
    shape = jax.ShapeDtypeStruct((512, 128), jnp.bfloat16)
    vmem = pl.BlockSpec(memory_space=pltpu.VMEM)
    smem = pl.BlockSpec(memory_space=pltpu.SMEM)
    return pl.pallas_call(
        functools.partial(mixing, cells),
        out_shape=(shape, shape),
        in_specs=[smem, smem, ANY, ANY, vmem],
        out_specs=(vmem, vmem),
        scratch_shapes=[pltpu.VMEM((10, 128, 128), jnp.float32)]
        + [pltpu.VMEM((32, 24, 128), jnp.float32)] * 2
        + [pltpu.SemaphoreType.DMA((2,))],
        compiler_params=pltpu.CompilerParams(vmem_limit_bytes=62 << 20),
        cost_estimate=pl.CostEstimate(flops=1 << 30, bytes_accessed=1 << 20, transcendentals=0),
    )(me, core, own, other, start_codes)


def finish(plan, me_ref, high_ref, low_ref, *refs):
    pieces, out_ref = refs[:-5], refs[-5]
    wide, done, in_sems, out_sems = refs[-4:]
    me = me_ref[0]
    loads = []
    for j in range(4):
        group = []
        for e in range(4):
            for index, source, target, size in plan[4 * j + e]:
                group.append(
                    pltpu.make_async_copy(
                        pieces[index].at[pl.ds(source, size)],
                        wide.at[j, pl.ds(target, size), pl.ds(128 * e, 128)],
                        in_sems.at[len(loads), len(group)],
                    )
                )
                group[-1].start()
        loads.append(group)
    mix = jnp.concatenate([high_ref[...], low_ref[...]], 1)
    stores = []
    for j in range(4):
        for copy in loads[j]:
            copy.wait()
        for r in range(16):
            both = jnp.dot(wide[j, 128 * r : 128 * r + 128], mix, preferred_element_type=jnp.float32)
            done[j, r] = (both[:, :128] + both[:, 128:]).astype(jnp.bfloat16)
        columns = pl.ds(pl.multiple_of((me ^ j) * GROUP, GROUP), GROUP)
        for n, (source, target, size) in enumerate(((0, 3, 10), (10, 0, 3), (13, 13, 3))):
            copy = pltpu.make_async_copy(
                done.at[j, pl.ds(source, size)], out_ref.at[pl.ds(target, size), columns], out_sems.at[j, n]
            )
            copy.start()
            stores.append(copy)
    for copy in stores:
        copy.wait()


def finish_call(me, high, low, pieces, plan):
    return pl.pallas_call(
        functools.partial(finish, plan),
        out_shape=jax.ShapeDtypeStruct((16, NY, LANES), jnp.bfloat16),
        in_specs=[SM, VM, VM] + [ANY] * len(pieces),
        out_specs=ANY,
        scratch_shapes=[
            pltpu.VMEM((4, PIECE, 512), jnp.bfloat16),
            pltpu.VMEM((4, 16, GROUP, LANES), jnp.bfloat16),
            pltpu.SemaphoreType.DMA((4, 8)),
            pltpu.SemaphoreType.DMA((4, 3)),
        ],
        compiler_params=pltpu.CompilerParams(vmem_limit_bytes=63 << 20),
        cost_estimate=pl.CostEstimate(flops=2 * 8192 * 512 * 256, bytes_accessed=10 << 20, transcendentals=0),
    )(me, high, low, *pieces)


def packed_edge(cells, perm):
    high = perm.astype(jnp.bfloat16)
    low = (perm - high.astype(jnp.float32)).astype(jnp.bfloat16)
    parts = [cells.reshape(-1, LANES), high.reshape(-1, LANES), low.reshape(-1, LANES)]
    return jnp.concatenate(parts + [jnp.zeros((8, LANES), jnp.bfloat16)], 0)


def merged_bases(forcing, permeability, merge_weights, start_codes):
    me = lax.axis_index("case").astype(jnp.int32).reshape(1)
    tile = lax.axis_index("tile").astype(jnp.int32).reshape(1)
    core = tile & 1
    cells = forcing.shape[1] * lax.axis_size("tile") * forcing.shape[2]
    own, kp = forcing[0], permeability[0]
    up = [(i, i + 1) for i in range(63)]
    down = [(i + 1, i) for i in range(63)]
    low = lax.ppermute(packed_edge(own[-STEPS:], kp[-STEPS:]), "tile", up)
    high = lax.ppermute(packed_edge(own[:STEPS], kp[:STEPS]), "tile", down)
    inner = inner_call(me, merge_weights, own, kp)
    met = [case_swap(inner[e - 1], e) for e in (1, 2, 3)]
    outer = outer_call(me, tile, merge_weights, own, kp, low, high, inner[9], inner[10], inner[3:9])
    near, late = outer[3:6], outer[6:9]
    met = met + [case_swap(outer[e - 1], e) for e in (1, 2, 3)]
    far = [case_swap(near[e - 1], e) for e in (1, 2, 3)]
    far = far + [case_swap(late[e - 1], e) for e in (1, 2, 3)]
    own_part, other_part = grams_call(me, core, [near[0]] + met)
    part = own_part + core_swap(other_part)
    part = plane_exchange(part).sum(0)
    part = part + case_swap(part, 1) + case_swap(part, 2) + case_swap(part, 3)
    mine = plane_exchange(jnp.broadcast_to(part, (32,) + part.shape))
    yours = core_swap(mine)
    high, low = mixing_call(cells, me, core, mine, yours, start_codes)
    plan = []
    for j in range(4):
        for e in range(4):
            if e == 0:
                plan.append((({0: 0, 3: 1, 2: 2, 1: 3}[j], 0, 0, PIECE),))
            elif j == 0:
                plan.append(((3 + e, 0, 0, INNER), (6 + e, 0, INNER, OUTER)))
            elif j == 2:
                plan.append(((12 + e, PIECE, 0, INNER), (9 + e, PIECE, INNER, OUTER)))
            else:
                plan.append(((9 + e if j == 1 else 12 + e, 0, 0, PIECE),))
    pieces = [near[0], near[1], near[2], late[1]] + met + far
    return finish_call(me, high, low, pieces, tuple(plan)).reshape(1, -1, LANES)


def solution(mesh):
    placed = (P("case", "tile", None, None), P("case", "tile", None), P("case"), P())
    return jax.shard_map(
        merged_bases, mesh=mesh, in_specs=placed, out_specs=P("case", "tile", None), check_vma=False
    )
```

```python
import functools
import math

import jax
import jax.numpy as jnp
from jax import lax
from jax.experimental import pallas as pl
from jax.experimental.pallas import tpu as pltpu
from jax.sharding import PartitionSpec as P

STEPS = 3


def at(z, y, core):
    return (z * 4 + y) * 2 + core


PLANES = [[at(z, y, core) for z in range(8) for y in range(4)] for core in range(2)]


def case_swap(value, apart):
    return lax.ppermute(value, "case", [(source, source ^ apart) for source in range(4)])


def core_swap(value):
    return lax.ppermute(value, "tile", [(source, source ^ 1) for source in range(64)])


def plane_exchange(value):
    return lax.all_to_all(value, "tile", 0, 0, axis_index_groups=PLANES)


AB = (((1,), (0,)), ((), ()))
ATB = (((0,), (0,)), ((), ()))
ABT = (((1,), (1,)), ((), ()))


def parts_of(x, exact=False):
    high = x.astype(jnp.bfloat16)
    if exact:
        return (high,)
    rest = x - high.astype(jnp.float32)
    mid = rest.astype(jnp.bfloat16)
    low = (rest - mid.astype(jnp.float32)).astype(jnp.bfloat16)
    return (high, mid, low)


def product(a, b, dims=AB):
    out = None
    for i in range(len(a) - 1, -1, -1):
        for j in range(len(b) - 1, -1, -1):
            if i + j < 3:
                term = lax.dot_general(a[i], b[j], dims, preferred_element_type=jnp.float32)
                out = term if out is None else out + term
    return out


def spread(x, axis, index, size):
    piece = lax.slice_in_dim(x, index, index + 1, axis=axis)
    shape = (size, x.shape[1]) if axis == 0 else (x.shape[0], size)
    return jnp.broadcast_to(piece, shape)


def inverse_factors(mats):
    lane = lax.broadcasted_iota(jnp.int32, (8, 128), 1)
    sub = lax.broadcasted_iota(jnp.int32, (8, 128), 0)
    tiles = [[m[8 * b : 8 * b + 8] for b in range(16)] for m in mats]
    for big in range(4):
        for a in tiles:
            left, right = [], []
            for k in range(4 * big, 4 * big + 4):
                first = 8 * k
                block = (lane >= first) & (lane < first + 8)
                rows = [spread(a[k], 0, r, 8) for r in range(8)]
                piv = [
                    [spread(rows[r], 1, first + s, 128) if s >= r else None for s in range(8)]
                    for r in range(8)
                ]
                inv = [None] * 8
                mul = [[None] * 8 for _ in range(8)]
                for r in range(8):
                    inv[r] = 1.0 / piv[r][r]
                    for s in range(r + 1, 8):
                        mul[r][s] = piv[r][s] * inv[r]
                    for s in range(r + 1, 8):
                        for t in range(s, 8):
                            piv[s][t] = piv[s][t] - mul[r][s] * piv[r][t]
                for s in range(8):
                    rows[s] = jnp.where(block, jnp.where(lane == first + s, 1.0, 0.0), rows[s])
                for s in range(8):
                    for r in range(s):
                        rows[s] = rows[s] - mul[r][s] * rows[r]
                scaled = [rows[r] * inv[r] for r in range(8)]
                for b in range(k + 1, 4 * big + 4):
                    col = [spread(a[b], 1, first + r, 128) for r in range(8)]
                    for r in range(8):
                        for s in range(r + 1, 8):
                            col[s] = col[s] - col[r] * mul[r][s]
                    new = jnp.where(block, 0.0, a[b])
                    for r in range(8):
                        new = new - col[r] * scaled[r]
                    a[b] = new
                plain, pivots, inverse = rows[0], piv[0][0], inv[0]
                for r in range(1, 8):
                    plain = jnp.where(sub == r, rows[r], plain)
                    pivots = jnp.where(sub == r, piv[r][r], pivots)
                    inverse = jnp.where(sub == r, inv[r], inverse)
                left.append(plain)
                later = (lane >= first + 8) & (lane < 32 * (big + 1))
                right.append(jnp.where(later, 0.0, plain * inverse))
                a[k] = jnp.where(lane < first + 8, plain * lax.rsqrt(pivots), 0.0)
            if big < 3:
                after = 32 * (big + 1)
                x = parts_of(jnp.concatenate(left, 0))
                y = parts_of(jnp.concatenate(right, 0))
                x = jnp.concatenate([x[0], x[0], x[1], x[0], x[2], x[1]], 0)
                y = jnp.concatenate([y[0], y[1], y[0], y[2], y[0], y[1]], 0)
                update = lax.dot_general(x, y, ATB, preferred_element_type=jnp.float32)
                used = (lane >= 32 * big) & (lane < after)
                for b in range(4 * big + 4, 16):
                    a[b] = jnp.where(used, 0.0, a[b]) - update[8 * b : 8 * b + 8]
    return [jnp.concatenate(a, 0) for a in tiles]


def mixing(cells, me_ref, core_ref, own_hbm, other_hbm, start_ref, high_ref, low_ref, *scratch):
    gram_ref, own_ref, other_ref, sems = scratch
    me, core = me_ref[0], core_ref[0]
    loads = [
        pltpu.make_async_copy(own_hbm, own_ref, sems.at[0]),
        pltpu.make_async_copy(other_hbm, other_ref, sems.at[1]),
    ]
    for copy in loads:
        copy.start()
    for copy in loads:
        copy.wait()
    for side in (0, 1):

        @pl.when(core == side)
        def _(side=side):
            for half, ref in enumerate((own_ref, other_ref) if side == 0 else (other_ref, own_ref)):
                rows = ref[:, 0:16].reshape(4, 128, 128)
                for i in range(4):
                    gram_ref[5 * half + i] = rows[i]
                for k in range(32):
                    gram_ref[5 * half + 4, 4 * k : 4 * k + 4] = ref[k, 16:20]

    odd = lax.rem(me, 2) == 1
    upper = me // 2

    def side(index, flip):
        x = gram_ref[index]
        return jnp.where(flip, x.T, x)

    def merged(coeff_parts, gram_parts):
        t = product(gram_parts, coeff_parts)
        return product(coeff_parts, parts_of(t), ATB)

    start = parts_of(start_ref[0].astype(jnp.float32), True)
    coeffs, inners = [], []
    for half in (0, 1):
        a, b = me ^ (2 * half), me ^ (2 * half + 1)
        near = side(4 + (upper ^ half), odd)
        gram = jnp.concatenate(
            [jnp.concatenate([gram_ref[a], near], 1), jnp.concatenate([near.T, gram_ref[b]], 1)], 0
        )
        gram = parts_of(gram)
        first = product(gram, start) / cells
        second = product(gram, parts_of(first)) / cells
        coeff = (second.astype(jnp.bfloat16),)
        coeffs.append(coeff)
        inners.append(merged(coeff, gram))
    inverse = inverse_factors(inners)
    scale = math.sqrt(cells)
    maps = [scale * product(c, parts_of(v), ABT) for c, v in zip(coeffs, inverse)]
    maps = [parts_of(m) for m in maps]
    low_group = upper == 0
    rows = []
    for e in (0, 1):
        line = []
        for f in (2, 3):
            a, b = me ^ e, me ^ f
            index = jnp.where(low_group, 6 + 2 * a + (b - 2), 6 + 2 * b + (a - 2))
            line.append(side(index, upper == 1))
        rows.append(jnp.concatenate(line, 1))
    across = parts_of(jnp.concatenate(rows, 0))
    cross = product(maps[0], parts_of(product(across, maps[1])), ATB)
    cross = parts_of(cross / cells)
    start = start_ref[1].astype(jnp.float32)
    top, bottom = start[:128], start[128:]
    exact = True
    for _ in range(2):
        top, bottom = (
            top + product(cross, parts_of(bottom, exact)),
            bottom + product(cross, parts_of(top, exact), ATB),
        )
        exact = False
    top, bottom = (top.astype(jnp.bfloat16),), (bottom.astype(jnp.bfloat16),)
    mixed = product(top, parts_of(product(cross, bottom)), ATB)
    inner = product(top, top, ATB) + product(bottom, bottom, ATB) + mixed + mixed.T
    (last,) = inverse_factors([inner])
    last = parts_of(last)
    for half, coeff in enumerate((top, bottom)):
        step = product(coeff, last, ABT)
        final = product(maps[half], parts_of(step))
        high = final.astype(jnp.bfloat16)
        high_ref[pl.ds(256 * half, 256), :] = high
        low_ref[pl.ds(256 * half, 256), :] = (final - high.astype(jnp.float32)).astype(jnp.bfloat16)


NY, LANES, PAD = 512, 128, 8
WIDE = PAD + NY + PAD
GROUP = 128
INNER, OUTER = 10 * GROUP, 6 * GROUP
PIECE = INNER + OUTER


def spread_faces(perm_ref, east, north, count):
    here = perm_ref[...]
    after = jnp.concatenate([here[1:], here[:1]], 0)
    row = lax.broadcasted_iota(jnp.int32, (256, 256), 0) & 127
    second = lax.broadcasted_iota(jnp.int32, (256, 256), 1) >> 7
    faces = []
    for value in (0.12 * (here + after), 0.12 * (here + pltpu.roll(here, LANES - 1, axis=1))):
        high = value.astype(jnp.bfloat16)
        low = (value - high.astype(jnp.float32)).astype(jnp.bfloat16)
        faces.append(jnp.concatenate([high, low], 1))
    for i in range(0, count, 2):
        pick = jnp.where(row == second + i, 1.0, 0.0).astype(jnp.bfloat16)
        for face, out in zip(faces, (east, north)):
            both = jnp.dot(face, pick, preferred_element_type=jnp.float32)
            out[i] = both[:, :LANES]
            if i + 1 < count:
                out[i + 1] = both[:, LANES:]


def set_perm(perm_ref, rows):
    count = rows.shape[0]
    rows = jnp.concatenate([rows, jnp.zeros((LANES - count, NY), jnp.float32)], 0)
    perm_ref[0:PAD] = jnp.zeros((PAD, LANES), jnp.float32)
    perm_ref[PAD : PAD + NY] = rows.T
    perm_ref[PAD + NY : WIDE] = jnp.zeros((PAD, LANES), jnp.float32)


def clear_pads(buf, count):
    def one(i, _):
        buf[i, 0:PAD] = jnp.zeros((PAD, LANES), jnp.float32)
        buf[i, PAD + NY : WIDE] = jnp.zeros((PAD, LANES), jnp.float32)
        return 0

    lax.fori_loop(0, count, one, 0)


def sweep(source, east, north, begin, face, count, write):
    for g in range(NY // GROUP):
        c = PAD + g * GROUP

        def one(i, carry, c=c, g=g):
            row, plane = begin + i, face + i
            center, south = carry
            above = source[row + 1, c : c + GROUP]
            up = north[plane, c : c + GROUP] * (above - center)
            east_here = east[plane, c : c + GROUP]
            flux = east_here * (source[row, c + 1 : c + GROUP + 1] - center)
            before = source[row, c - PAD : c]
            edge = east[plane, c - PAD : c] * (source[row, c - PAD + 1 : c + 1] - before)
            shifted = jnp.concatenate([edge, flux], 0)[PAD - 1 : PAD - 1 + GROUP]
            write(i, g, center + ((up - south) + (flux - shifted)))
            return above, up

        center = source[begin, c : c + GROUP]
        south = north[face - 1, c : c + GROUP] * (center - source[begin - 1, c : c + GROUP])
        lax.fori_loop(0, count, one, (center, south))


def into(buf, base):
    def write(i, g, value):
        buf[base + i, PAD + g * GROUP : PAD + g * GROUP + GROUP] = value

    return write


def into_snap(snap, base, scale_ref):
    scale = jnp.sqrt(jnp.full((8, LANES), scale_ref[0].astype(jnp.float32)))
    scale = jnp.broadcast_to(scale[0:1], (GROUP, LANES))

    def write(i, g, value):
        at0 = pl.multiple_of((base + i) * GROUP, GROUP)
        snap[g, pl.ds(at0, GROUP)] = (value * scale).astype(jnp.bfloat16)

    return write


def send_out(me, snap, singles, moves, sems):
    copies = []
    for e in (1, 2, 3):
        copies.append(pltpu.make_async_copy(snap.at[me ^ e], singles[e - 1], sems.at[len(copies)]))
        for stacks, j, begin, size in moves:
            target = stacks[e - 1].at[pl.ds(begin, size)]
            copies.append(pltpu.make_async_copy(snap.at[me ^ e ^ j], target, sems.at[len(copies)]))
    for copy in copies:
        copy.start()
    return copies


def inner_rows(me_ref, scale_ref, own_ref, kp_ref, *refs):
    singles, near, late, edge_one, edge_two = refs[:3], refs[3:6], refs[6:9], refs[9], refs[10]
    first, second, east, north, perm_ref, snap, held, sems, edge_sems = refs[11:]
    me = me_ref[0]
    load = pltpu.make_async_copy(own_ref, held, sems.at[0])
    load.start()
    clear_pads(first, 16)
    clear_pads(second, 16)

    def fill(i, _):
        first[i, PAD : PAD + NY] = held[i].astype(jnp.float32)
        return 0

    set_perm(perm_ref, kp_ref[...])
    spread_faces(perm_ref, east, north, 15)
    load.wait()
    lax.fori_loop(0, 16, fill, 0)
    sweep(first, east, north, 1, 1, 14, into(second, 1))
    sweep(second, east, north, 2, 2, 12, into(first, 2))
    edges_out = [
        pltpu.make_async_copy(second.at[pl.ds(1, 2)], edge_one.at[pl.ds(0, 2)], edge_sems.at[0]),
        pltpu.make_async_copy(second.at[pl.ds(13, 2)], edge_one.at[pl.ds(2, 2)], edge_sems.at[1]),
        pltpu.make_async_copy(first.at[pl.ds(2, 2)], edge_two.at[pl.ds(0, 2)], edge_sems.at[2]),
        pltpu.make_async_copy(first.at[pl.ds(12, 2)], edge_two.at[pl.ds(2, 2)], edge_sems.at[3]),
    ]
    for copy in edges_out:
        copy.start()
    sweep(first, east, north, 3, 3, 10, into_snap(snap, 0, scale_ref))
    moves = ((near, 1, 0, INNER), (near, 2, PIECE, INNER), (late, 3, 0, INNER))
    for copy in edges_out + send_out(me, snap, singles, moves, sems):
        copy.wait()


def outer_rows(me_ref, tile_ref, scale_ref, own_hbm, kp_ref, low_hbm, high_hbm, edge_one, edge_two, *refs):
    singles, near, late = refs[6:9], refs[9:12], refs[12:15]
    low0, low1, low2, high0, high1, high2, east, north, perm_ref, snap = refs[15:25]
    low_ref, high_ref, own_ref, sems, edge_sems = refs[25:]
    me, tile = me_ref[0], tile_ref[0]
    loads = [
        pltpu.make_async_copy(low_hbm, low_ref, sems.at[0]),
        pltpu.make_async_copy(high_hbm, high_ref, sems.at[1]),
        pltpu.make_async_copy(own_hbm.at[pl.ds(0, 2)], own_ref.at[pl.ds(0, 2)], sems.at[2]),
        pltpu.make_async_copy(own_hbm.at[pl.ds(14, 2)], own_ref.at[pl.ds(2, 2)], sems.at[3]),
    ]
    for copy in loads:
        copy.start()
    edges_in = [
        pltpu.make_async_copy(edge_one.at[pl.ds(0, 2)], low1.at[pl.ds(3, 2)], edge_sems.at[0]),
        pltpu.make_async_copy(edge_one.at[pl.ds(2, 2)], high1.at[pl.ds(0, 2)], edge_sems.at[1]),
        pltpu.make_async_copy(edge_two.at[pl.ds(0, 2)], low2.at[pl.ds(3, 2)], edge_sems.at[2]),
        pltpu.make_async_copy(edge_two.at[pl.ds(2, 2)], high2.at[pl.ds(0, 2)], edge_sems.at[3]),
    ]
    for copy in edges_in:
        copy.start()
    for buf in (low0, high0):
        clear_pads(buf, 5)
    for buf in (low1, low2):
        clear_pads(buf, 3)
    for buf in (high1, high2):
        clear_pads(buf.at[pl.ds(2, 3)], 3)
    for copy in loads:
        copy.wait()
    for i in range(3):
        low0[i, PAD : PAD + NY] = low_ref[NY * i : NY * i + NY].astype(jnp.float32)
        high0[2 + i, PAD : PAD + NY] = high_ref[NY * i : NY * i + NY].astype(jnp.float32)
    for i in range(2):
        low0[3 + i, PAD : PAD + NY] = own_ref[i].astype(jnp.float32)
        high0[i, PAD : PAD + NY] = own_ref[2 + i].astype(jnp.float32)

    def far_perm(ref):
        both = ref[3 * NY : 3 * NY + 32].astype(jnp.float32)
        packed = both[0:12] + both[12:24]
        return [
            jnp.concatenate([packed[4 * i + q : 4 * i + q + 1] for q in range(4)], 1) for i in range(3)
        ]

    kp = kp_ref[...]
    set_perm(perm_ref, jnp.concatenate(far_perm(low_ref) + [kp[0:4], kp[12:16]] + far_perm(high_ref), 0))
    spread_faces(perm_ref, east, north, 13)
    sweep(low0, east, north, 1, 1, 3, into(low1, 0))
    sweep(high0, east, north, 1, 10, 3, into(high1, 2))
    blank = jnp.zeros((NY, LANES), jnp.float32)

    @pl.when(tile == 0)
    def _():
        low1[0, PAD : PAD + NY] = blank
        low1[1, PAD : PAD + NY] = blank

    @pl.when(tile == 63)
    def _():
        high1[3, PAD : PAD + NY] = blank
        high1[4, PAD : PAD + NY] = blank

    for copy in edges_in:
        copy.wait()
    sweep(low1, east, north, 1, 2, 3, into(low2, 0))
    sweep(high1, east, north, 1, 9, 3, into(high2, 2))

    @pl.when(tile == 0)
    def _():
        low2[0, PAD : PAD + NY] = blank

    @pl.when(tile == 63)
    def _():
        high2[4, PAD : PAD + NY] = blank

    sweep(low2, east, north, 1, 3, 3, into_snap(snap, 0, scale_ref))
    sweep(high2, east, north, 1, 8, 3, into_snap(snap, 3, scale_ref))
    moves = ((near, 1, INNER, OUTER), (late, 3, INNER, OUTER), (late, 2, PIECE, OUTER))
    for copy in send_out(me, snap, singles, moves, sems):
        copy.wait()


VM = pl.BlockSpec(memory_space=pltpu.VMEM)
SM = pl.BlockSpec(memory_space=pltpu.SMEM)
ANY = pl.BlockSpec(memory_space=pl.ANY)


def half(rows):
    return jax.ShapeDtypeStruct((rows, LANES), jnp.bfloat16)


def planes(count):
    return pltpu.VMEM((count, WIDE, LANES), jnp.float32)


def inner_call(me, weights, own, kp):
    edge = jax.ShapeDtypeStruct((4, WIDE, LANES), jnp.float32)
    return pl.pallas_call(
        inner_rows,
        out_shape=[half(INNER)] * 3 + [half(PIECE + INNER)] * 3 + [half(PIECE + OUTER)] * 3 + [edge] * 2,
        in_specs=[SM, SM, ANY, VM],
        out_specs=[ANY] * 11,
        scratch_shapes=[planes(16), planes(16), planes(15), planes(15)]
        + [pltpu.VMEM((WIDE, LANES), jnp.float32), pltpu.VMEM((4, INNER, LANES), jnp.bfloat16)]
        + [pltpu.VMEM((16, NY, LANES), jnp.bfloat16)]
        + [pltpu.SemaphoreType.DMA((12,)), pltpu.SemaphoreType.DMA((4,))],
        compiler_params=pltpu.CompilerParams(vmem_limit_bytes=63 << 20),
        cost_estimate=pl.CostEstimate(flops=400 << 20, bytes_accessed=9 << 20, transcendentals=0),
    )(me, weights, own, kp)


def outer_call(me, tile, weights, own, kp, low, high, edge_one, edge_two, stacks):
    return pl.pallas_call(
        outer_rows,
        out_shape=[half(OUTER)] * 3 + [half(PIECE + INNER)] * 3 + [half(PIECE + OUTER)] * 3,
        in_specs=[SM, SM, SM, ANY, VM] + [ANY] * 10,
        out_specs=[ANY] * 9,
        input_output_aliases={9 + n: 3 + n for n in range(6)},
        scratch_shapes=[planes(5)] * 6
        + [planes(13), planes(13), pltpu.VMEM((WIDE, LANES), jnp.float32)]
        + [pltpu.VMEM((4, OUTER, LANES), jnp.bfloat16)]
        + [pltpu.VMEM((3 * NY + 32, LANES), jnp.bfloat16)] * 2
        + [pltpu.VMEM((4, NY, LANES), jnp.bfloat16)]
        + [pltpu.SemaphoreType.DMA((12,)), pltpu.SemaphoreType.DMA((4,))],
        compiler_params=pltpu.CompilerParams(vmem_limit_bytes=63 << 20),
        cost_estimate=pl.CostEstimate(flops=200 << 20, bytes_accessed=9 << 20, transcendentals=0),
    )(me, tile, weights, own, kp, low, high, edge_one, edge_two, *stacks)


def grams(me_ref, core_ref, *refs):
    pieces, own_ref, other_ref, wide, sems = refs[:7], refs[7], refs[8], refs[9], refs[10]
    me, core = me_ref[0], core_ref[0]
    copies = []
    for e in range(4):
        lanes = pl.ds(pl.multiple_of((me ^ e) * 128, 128), 128)
        if e == 0:
            moves = [(pieces[0].at[pl.ds(0, PIECE)], 0, PIECE)]
        else:
            moves = [(pieces[e], 0, INNER), (pieces[3 + e], INNER, OUTER)]
        for source, begin, size in moves:
            target = wide.at[pl.ds(begin, size), lanes]
            copies.append(pltpu.make_async_copy(source, target, sems.at[len(copies)]))
    for copy in copies:
        copy.start()
    for copy in copies:
        copy.wait()
    left, right = wide[:, :256], wide[:, 256:]
    near = lax.dot_general(left, left, ATB, preferred_element_type=jnp.float32)
    far = lax.dot_general(right, right, ATB, preferred_element_type=jnp.float32)
    cross = lax.dot_general(left, right, ATB, preferred_element_type=jnp.float32)
    blocks = [
        near[:128, :128], near[128:, 128:], far[:128, :128], far[128:, 128:], near[:128, 128:],
        far[:128, 128:], cross[:128, :128], cross[:128, 128:], cross[128:, :128], cross[128:, 128:],
    ]
    for side in (0, 1):

        @pl.when(core == side)
        def _(side=side):
            for half, ref in enumerate((own_ref, other_ref) if side == 0 else (other_ref, own_ref)):
                mine = blocks[5 * half : 5 * half + 5]
                ref[:, 0:16] = jnp.concatenate(mine[:4], 0).reshape(32, 16, 128)
                ref[:, 16:24] = jnp.zeros((32, 8, 128), jnp.float32)
                for k in range(32):
                    ref[k, 16:20] = mine[4][4 * k : 4 * k + 4]


def grams_call(me, core, pieces):
    shape = jax.ShapeDtypeStruct((32, 24, 128), jnp.float32)
    return pl.pallas_call(
        grams,
        out_shape=(shape, shape),
        in_specs=[SM, SM] + [ANY] * 7,
        out_specs=(VM, VM),
        scratch_shapes=[pltpu.VMEM((PIECE, 512), jnp.bfloat16), pltpu.SemaphoreType.DMA((7,))],
        compiler_params=pltpu.CompilerParams(vmem_limit_bytes=63 << 20),
        cost_estimate=pl.CostEstimate(flops=2 * 2048 * 512 * 512, bytes_accessed=3 << 20, transcendentals=0),
    )(me, core, *pieces)


def mixing_call(cells, me, core, own, other, start_codes):
    shape = jax.ShapeDtypeStruct((512, 128), jnp.bfloat16)
    vmem = pl.BlockSpec(memory_space=pltpu.VMEM)
    smem = pl.BlockSpec(memory_space=pltpu.SMEM)
    return pl.pallas_call(
        functools.partial(mixing, cells),
        out_shape=(shape, shape),
        in_specs=[smem, smem, ANY, ANY, vmem],
        out_specs=(vmem, vmem),
        scratch_shapes=[pltpu.VMEM((10, 128, 128), jnp.float32)]
        + [pltpu.VMEM((32, 24, 128), jnp.float32)] * 2
        + [pltpu.SemaphoreType.DMA((2,))],
        compiler_params=pltpu.CompilerParams(vmem_limit_bytes=62 << 20),
        cost_estimate=pl.CostEstimate(flops=1 << 30, bytes_accessed=1 << 20, transcendentals=0),
    )(me, core, own, other, start_codes)


def finish(plan, me_ref, high_ref, low_ref, *refs):
    pieces, out_ref = refs[:-5], refs[-5]
    wide, done, in_sems, out_sems = refs[-4:]
    me = me_ref[0]
    loads = []
    for j in range(4):
        group = []
        for e in range(4):
            for index, source, target, size in plan[4 * j + e]:
                group.append(
                    pltpu.make_async_copy(
                        pieces[index].at[pl.ds(source, size)],
                        wide.at[j, pl.ds(target, size), pl.ds(128 * e, 128)],
                        in_sems.at[len(loads), len(group)],
                    )
                )
                group[-1].start()
        loads.append(group)
    mix = jnp.concatenate([high_ref[...], low_ref[...]], 1)
    stores = []
    for j in range(4):
        for copy in loads[j]:
            copy.wait()
        for r in range(16):
            both = jnp.dot(wide[j, 128 * r : 128 * r + 128], mix, preferred_element_type=jnp.float32)
            done[j, r] = (both[:, :128] + both[:, 128:]).astype(jnp.bfloat16)
        columns = pl.ds(pl.multiple_of((me ^ j) * GROUP, GROUP), GROUP)
        for n, (source, target, size) in enumerate(((0, 3, 10), (10, 0, 3), (13, 13, 3))):
            copy = pltpu.make_async_copy(
                done.at[j, pl.ds(source, size)], out_ref.at[pl.ds(target, size), columns], out_sems.at[j, n]
            )
            copy.start()
            stores.append(copy)
    for copy in stores:
        copy.wait()


def finish_call(me, high, low, pieces, plan):
    return pl.pallas_call(
        functools.partial(finish, plan),
        out_shape=jax.ShapeDtypeStruct((16, NY, LANES), jnp.bfloat16),
        in_specs=[SM, VM, VM] + [ANY] * len(pieces),
        out_specs=ANY,
        scratch_shapes=[
            pltpu.VMEM((4, PIECE, 512), jnp.bfloat16),
            pltpu.VMEM((4, 16, GROUP, LANES), jnp.bfloat16),
            pltpu.SemaphoreType.DMA((4, 8)),
            pltpu.SemaphoreType.DMA((4, 3)),
        ],
        compiler_params=pltpu.CompilerParams(vmem_limit_bytes=63 << 20),
        cost_estimate=pl.CostEstimate(flops=2 * 8192 * 512 * 256, bytes_accessed=10 << 20, transcendentals=0),
    )(me, high, low, *pieces)


def packed_edge(cells, perm):
    high = perm.astype(jnp.bfloat16)
    low = (perm - high.astype(jnp.float32)).astype(jnp.bfloat16)
    parts = [cells.reshape(-1, LANES), high.reshape(-1, LANES), low.reshape(-1, LANES)]
    return jnp.concatenate(parts + [jnp.zeros((8, LANES), jnp.bfloat16)], 0)


def merged_bases(forcing, permeability, merge_weights, start_codes):
    me = lax.axis_index("case").astype(jnp.int32).reshape(1)
    tile = lax.axis_index("tile").astype(jnp.int32).reshape(1)
    core = tile & 1
    cells = forcing.shape[1] * lax.axis_size("tile") * forcing.shape[2]
    own, kp = forcing[0], permeability[0]
    up = [(i, i + 1) for i in range(63)]
    down = [(i + 1, i) for i in range(63)]
    low = lax.ppermute(packed_edge(own[-STEPS:], kp[-STEPS:]), "tile", up)
    high = lax.ppermute(packed_edge(own[:STEPS], kp[:STEPS]), "tile", down)
    inner = inner_call(me, merge_weights, own, kp)
    met = [case_swap(inner[e - 1], e) for e in (1, 2, 3)]
    outer = outer_call(me, tile, merge_weights, own, kp, low, high, inner[9], inner[10], inner[3:9])
    near, late = outer[3:6], outer[6:9]
    met = met + [case_swap(outer[e - 1], e) for e in (1, 2, 3)]
    far = [case_swap(near[e - 1], e) for e in (1, 2, 3)]
    far = far + [case_swap(late[e - 1], e) for e in (1, 2, 3)]
    own_part, other_part = grams_call(me, core, [near[0]] + met)
    part = own_part + core_swap(other_part)
    part = plane_exchange(part).sum(0)
    part = part + case_swap(part, 1) + case_swap(part, 2) + case_swap(part, 3)
    mine = plane_exchange(jnp.broadcast_to(part, (32,) + part.shape))
    yours = core_swap(mine)
    high, low = mixing_call(cells, me, core, mine, yours, start_codes)
    plan = []
    for j in range(4):
        for e in range(4):
            if e == 0:
                plan.append((({0: 0, 3: 1, 2: 2, 1: 3}[j], 0, 0, PIECE),))
            elif j == 0:
                plan.append(((3 + e, 0, 0, INNER), (6 + e, 0, INNER, OUTER)))
            elif j == 2:
                plan.append(((9 + e, PIECE, 0, INNER), (12 + e, PIECE, INNER, OUTER)))
            else:
                plan.append(((9 + e if j == 1 else 12 + e, 0, 0, PIECE),))
    pieces = [near[0], near[1], near[2], late[1]] + met + far
    return finish_call(me, high, low, pieces, tuple(plan)).reshape(1, -1, LANES)


def solution(mesh):
    placed = (P("case", "tile", None, None), P("case", "tile", None), P("case"), P())
    return jax.shard_map(merged_bases, mesh=mesh, in_specs=placed, out_specs=P("case", "tile", None), check_vma=False)
```

```python
import functools
import math

import jax
import jax.numpy as jnp
from jax import lax
from jax.experimental import pallas as pl
from jax.experimental.pallas import tpu as pltpu
from jax.sharding import PartitionSpec as P

STEPS = 3


def at(z, y, core):
    return (z * 4 + y) * 2 + core


PLANES = [[at(z, y, core) for z in range(8) for y in range(4)] for core in range(2)]


def case_swap(value, apart):
    return lax.ppermute(value, "case", [(source, source ^ apart) for source in range(4)])


def core_swap(value):
    return lax.ppermute(value, "tile", [(source, source ^ 1) for source in range(64)])


def plane_exchange(value):
    return lax.all_to_all(value, "tile", 0, 0, axis_index_groups=PLANES)


AB = (((1,), (0,)), ((), ()))
ATB = (((0,), (0,)), ((), ()))
ABT = (((1,), (1,)), ((), ()))


def parts_of(x, exact=False):
    high = x.astype(jnp.bfloat16)
    if exact:
        return (high,)
    rest = x - high.astype(jnp.float32)
    mid = rest.astype(jnp.bfloat16)
    low = (rest - mid.astype(jnp.float32)).astype(jnp.bfloat16)
    return (high, mid, low)


def product(a, b, dims=AB):
    out = None
    for i in range(len(a) - 1, -1, -1):
        for j in range(len(b) - 1, -1, -1):
            if i + j < 3:
                term = lax.dot_general(a[i], b[j], dims, preferred_element_type=jnp.float32)
                out = term if out is None else out + term
    return out


def spread(x, axis, index, size):
    piece = lax.slice_in_dim(x, index, index + 1, axis=axis)
    shape = (size, x.shape[1]) if axis == 0 else (x.shape[0], size)
    return jnp.broadcast_to(piece, shape)


def inverse_factors(mats):
    lane = lax.broadcasted_iota(jnp.int32, (8, 128), 1)
    sub = lax.broadcasted_iota(jnp.int32, (8, 128), 0)
    tiles = [[m[8 * b : 8 * b + 8] for b in range(16)] for m in mats]
    for big in range(4):
        for a in tiles:
            left, right = [], []
            for k in range(4 * big, 4 * big + 4):
                first = 8 * k
                block = (lane >= first) & (lane < first + 8)
                rows = [spread(a[k], 0, r, 8) for r in range(8)]
                piv = [
                    [spread(rows[r], 1, first + s, 128) if s >= r else None for s in range(8)]
                    for r in range(8)
                ]
                inv = [None] * 8
                mul = [[None] * 8 for _ in range(8)]
                for r in range(8):
                    inv[r] = 1.0 / piv[r][r]
                    for s in range(r + 1, 8):
                        mul[r][s] = piv[r][s] * inv[r]
                    for s in range(r + 1, 8):
                        for t in range(s, 8):
                            piv[s][t] = piv[s][t] - mul[r][s] * piv[r][t]
                for s in range(8):
                    rows[s] = jnp.where(block, jnp.where(lane == first + s, 1.0, 0.0), rows[s])
                for s in range(8):
                    for r in range(s):
                        rows[s] = rows[s] - mul[r][s] * rows[r]
                scaled = [rows[r] * inv[r] for r in range(8)]
                for b in range(k + 1, 4 * big + 4):
                    col = [spread(a[b], 1, first + r, 128) for r in range(8)]
                    for r in range(8):
                        for s in range(r + 1, 8):
                            col[s] = col[s] - col[r] * mul[r][s]
                    new = jnp.where(block, 0.0, a[b])
                    for r in range(8):
                        new = new - col[r] * scaled[r]
                    a[b] = new
                plain, pivots, inverse = rows[0], piv[0][0], inv[0]
                for r in range(1, 8):
                    plain = jnp.where(sub == r, rows[r], plain)
                    pivots = jnp.where(sub == r, piv[r][r], pivots)
                    inverse = jnp.where(sub == r, inv[r], inverse)
                left.append(plain)
                later = (lane >= first + 8) & (lane < 32 * (big + 1))
                right.append(jnp.where(later, 0.0, plain * inverse))
                a[k] = jnp.where(lane < first + 8, plain * lax.rsqrt(pivots), 0.0)
            if big < 3:
                after = 32 * (big + 1)
                x = parts_of(jnp.concatenate(left, 0))
                y = parts_of(jnp.concatenate(right, 0))
                x = jnp.concatenate([x[0], x[0], x[1], x[0], x[2], x[1]], 0)
                y = jnp.concatenate([y[0], y[1], y[0], y[2], y[0], y[1]], 0)
                update = lax.dot_general(x, y, ATB, preferred_element_type=jnp.float32)
                used = (lane >= 32 * big) & (lane < after)
                for b in range(4 * big + 4, 16):
                    a[b] = jnp.where(used, 0.0, a[b]) - update[8 * b : 8 * b + 8]
    return [jnp.concatenate(a, 0) for a in tiles]


def mixing(cells, me_ref, core_ref, own_hbm, other_hbm, start_ref, high_ref, low_ref, *scratch):
    gram_ref, own_ref, other_ref, sems = scratch
    me, core = me_ref[0], core_ref[0]
    loads = [
        pltpu.make_async_copy(own_hbm, own_ref, sems.at[0]),
        pltpu.make_async_copy(other_hbm, other_ref, sems.at[1]),
    ]
    for copy in loads:
        copy.start()
    for copy in loads:
        copy.wait()
    for side in (0, 1):

        @pl.when(core == side)
        def _(side=side):
            for half, ref in enumerate((own_ref, other_ref) if side == 0 else (other_ref, own_ref)):
                rows = ref[:, 0:16].reshape(4, 128, 128)
                for i in range(4):
                    gram_ref[5 * half + i] = rows[i]
                for k in range(32):
                    gram_ref[5 * half + 4, 4 * k : 4 * k + 4] = ref[k, 16:20]

    odd = lax.rem(me, 2) == 1
    upper = me // 2

    def side(index, flip):
        x = gram_ref[index]
        return jnp.where(flip, x.T, x)

    def merged(coeff_parts, gram_parts):
        t = product(gram_parts, coeff_parts)
        return product(coeff_parts, parts_of(t), ATB)

    start = parts_of(start_ref[0].astype(jnp.float32), True)
    coeffs, inners = [], []
    for half in (0, 1):
        a, b = me ^ (2 * half), me ^ (2 * half + 1)
        near = side(4 + (upper ^ half), odd)
        gram = jnp.concatenate(
            [jnp.concatenate([gram_ref[a], near], 1), jnp.concatenate([near.T, gram_ref[b]], 1)], 0
        )
        gram = parts_of(gram)
        first = product(gram, start) / cells
        second = product(gram, parts_of(first)) / cells
        coeff = (second.astype(jnp.bfloat16),)
        coeffs.append(coeff)
        inners.append(merged(coeff, gram))
    inverse = inverse_factors(inners)
    scale = math.sqrt(cells)
    maps = [scale * product(c, parts_of(v), ABT) for c, v in zip(coeffs, inverse)]
    maps = [parts_of(m) for m in maps]
    low_group = upper == 0
    rows = []
    for e in (0, 1):
        line = []
        for f in (2, 3):
            a, b = me ^ e, me ^ f
            index = jnp.where(low_group, 6 + 2 * a + (b - 2), 6 + 2 * b + (a - 2))
            line.append(side(index, upper == 1))
        rows.append(jnp.concatenate(line, 1))
    across = parts_of(jnp.concatenate(rows, 0))
    cross = product(maps[0], parts_of(product(across, maps[1])), ATB)
    cross = parts_of(cross / cells)
    start = start_ref[1].astype(jnp.float32)
    top, bottom = start[:128], start[128:]
    exact = True
    for _ in range(2):
        top, bottom = (
            top + product(cross, parts_of(bottom, exact)),
            bottom + product(cross, parts_of(top, exact), ATB),
        )
        exact = False
    top, bottom = (top.astype(jnp.bfloat16),), (bottom.astype(jnp.bfloat16),)
    mixed = product(top, parts_of(product(cross, bottom)), ATB)
    inner = product(top, top, ATB) + product(bottom, bottom, ATB) + mixed + mixed.T
    (last,) = inverse_factors([inner])
    last = parts_of(last)
    for half, coeff in enumerate((top, bottom)):
        step = product(coeff, last, ABT)
        final = product(maps[half], parts_of(step))
        high = final.astype(jnp.bfloat16)
        high_ref[pl.ds(256 * half, 256), :] = high
        low_ref[pl.ds(256 * half, 256), :] = (final - high.astype(jnp.float32)).astype(jnp.bfloat16)


NY, LANES, PAD = 512, 128, 8
WIDE = PAD + NY + PAD
GROUP = 128
INNER, OUTER = 10 * GROUP, 6 * GROUP
PIECE = INNER + OUTER


def spread_faces(perm_ref, east, north, count):
    here = perm_ref[...]
    after = jnp.concatenate([here[1:], here[:1]], 0)
    row = lax.broadcasted_iota(jnp.int32, (256, 256), 0) & 127
    second = lax.broadcasted_iota(jnp.int32, (256, 256), 1) >> 7
    faces = []
    for value in (0.12 * (here + after), 0.12 * (here + pltpu.roll(here, LANES - 1, axis=1))):
        high = value.astype(jnp.bfloat16)
        low = (value - high.astype(jnp.float32)).astype(jnp.bfloat16)
        faces.append(jnp.concatenate([high, low], 1))
    for i in range(0, count, 2):
        pick = jnp.where(row == second + i, 1.0, 0.0).astype(jnp.bfloat16)
        for face, out in zip(faces, (east, north)):
            both = jnp.dot(face, pick, preferred_element_type=jnp.float32)
            out[i] = both[:, :LANES]
            if i + 1 < count:
                out[i + 1] = both[:, LANES:]


def set_perm(perm_ref, rows):
    count = rows.shape[0]
    rows = jnp.concatenate([rows, jnp.zeros((LANES - count, NY), jnp.float32)], 0)
    perm_ref[0:PAD] = jnp.zeros((PAD, LANES), jnp.float32)
    perm_ref[PAD : PAD + NY] = rows.T
    perm_ref[PAD + NY : WIDE] = jnp.zeros((PAD, LANES), jnp.float32)


def clear_pads(buf, count):
    def one(i, _):
        buf[i, 0:PAD] = jnp.zeros((PAD, LANES), jnp.float32)
        buf[i, PAD + NY : WIDE] = jnp.zeros((PAD, LANES), jnp.float32)
        return 0

    lax.fori_loop(0, count, one, 0)


def sweep(source, east, north, begin, face, count, write):
    for g in range(NY // GROUP):
        c = PAD + g * GROUP

        def one(i, carry, c=c, g=g):
            row, plane = begin + i, face + i
            center, south = carry
            above = source[row + 1, c : c + GROUP]
            up = north[plane, c : c + GROUP] * (above - center)
            east_here = east[plane, c : c + GROUP]
            flux = east_here * (source[row, c + 1 : c + GROUP + 1] - center)
            before = source[row, c - PAD : c]
            edge = east[plane, c - PAD : c] * (source[row, c - PAD + 1 : c + 1] - before)
            shifted = jnp.concatenate([edge, flux], 0)[PAD - 1 : PAD - 1 + GROUP]
            write(i, g, center + ((up - south) + (flux - shifted)))
            return above, up

        center = source[begin, c : c + GROUP]
        south = north[face - 1, c : c + GROUP] * (center - source[begin - 1, c : c + GROUP])
        lax.fori_loop(0, count, one, (center, south))


def into(buf, base):
    def write(i, g, value):
        buf[base + i, PAD + g * GROUP : PAD + g * GROUP + GROUP] = value

    return write


def into_snap(snap, base, scale_ref):
    scale = jnp.sqrt(jnp.full((8, LANES), scale_ref[0].astype(jnp.float32)))
    scale = jnp.broadcast_to(scale[0:1], (GROUP, LANES))

    def write(i, g, value):
        at0 = pl.multiple_of((base + i) * GROUP, GROUP)
        snap[g, pl.ds(at0, GROUP)] = (value * scale).astype(jnp.bfloat16)

    return write


def send_out(me, snap, singles, stacks, begin, size, sems):
    one, two, three = stacks
    moves = [(singles[e - 1], e, 0) for e in (1, 2, 3)]
    moves += [(one, j ^ 1, PIECE * (j - 1) + begin) for j in (1, 2, 3)]
    moves += [(two, 2, begin), (two, 1, PIECE + begin), (three, 0, begin)]
    copies = []
    for target, j, at0 in moves:
        copies.append(
            pltpu.make_async_copy(snap.at[me ^ j], target.at[pl.ds(at0, size)], sems.at[len(copies)])
        )
    for copy in copies:
        copy.start()
    return copies


def inner_rows(me_ref, scale_ref, own_ref, kp_ref, *refs):
    singles, stacks, edge_one, edge_two = refs[:3], refs[3:6], refs[6], refs[7]
    first, second, east, north, perm_ref, snap, held, sems, edge_sems = refs[8:]
    me = me_ref[0]
    load = pltpu.make_async_copy(own_ref, held, sems.at[0])
    load.start()
    clear_pads(first, 16)
    clear_pads(second, 16)

    def fill(i, _):
        first[i, PAD : PAD + NY] = held[i].astype(jnp.float32)
        return 0

    set_perm(perm_ref, kp_ref[...])
    spread_faces(perm_ref, east, north, 15)
    load.wait()
    lax.fori_loop(0, 16, fill, 0)
    sweep(first, east, north, 1, 1, 14, into(second, 1))
    sweep(second, east, north, 2, 2, 12, into(first, 2))
    edges_out = [
        pltpu.make_async_copy(second.at[pl.ds(1, 2)], edge_one.at[pl.ds(0, 2)], edge_sems.at[0]),
        pltpu.make_async_copy(second.at[pl.ds(13, 2)], edge_one.at[pl.ds(2, 2)], edge_sems.at[1]),
        pltpu.make_async_copy(first.at[pl.ds(2, 2)], edge_two.at[pl.ds(0, 2)], edge_sems.at[2]),
        pltpu.make_async_copy(first.at[pl.ds(12, 2)], edge_two.at[pl.ds(2, 2)], edge_sems.at[3]),
    ]
    for copy in edges_out:
        copy.start()
    sweep(first, east, north, 3, 3, 10, into_snap(snap, 0, scale_ref))
    for copy in edges_out + send_out(me, snap, singles, stacks, 0, INNER, sems):
        copy.wait()


def outer_rows(me_ref, tile_ref, scale_ref, own_hbm, kp_ref, low_hbm, high_hbm, edge_one, edge_two, *refs):
    singles, stacks = refs[3:6], refs[6:9]
    low0, low1, low2, high0, high1, high2, east, north, perm_ref, snap = refs[9:19]
    low_ref, high_ref, own_ref, sems, edge_sems = refs[19:]
    me, tile = me_ref[0], tile_ref[0]
    loads = [
        pltpu.make_async_copy(low_hbm, low_ref, sems.at[0]),
        pltpu.make_async_copy(high_hbm, high_ref, sems.at[1]),
        pltpu.make_async_copy(own_hbm.at[pl.ds(0, 2)], own_ref.at[pl.ds(0, 2)], sems.at[2]),
        pltpu.make_async_copy(own_hbm.at[pl.ds(14, 2)], own_ref.at[pl.ds(2, 2)], sems.at[3]),
    ]
    for copy in loads:
        copy.start()
    edges_in = [
        pltpu.make_async_copy(edge_one.at[pl.ds(0, 2)], low1.at[pl.ds(3, 2)], edge_sems.at[0]),
        pltpu.make_async_copy(edge_one.at[pl.ds(2, 2)], high1.at[pl.ds(0, 2)], edge_sems.at[1]),
        pltpu.make_async_copy(edge_two.at[pl.ds(0, 2)], low2.at[pl.ds(3, 2)], edge_sems.at[2]),
        pltpu.make_async_copy(edge_two.at[pl.ds(2, 2)], high2.at[pl.ds(0, 2)], edge_sems.at[3]),
    ]
    for copy in edges_in:
        copy.start()
    for buf in (low0, high0):
        clear_pads(buf, 5)
    for buf in (low1, low2):
        clear_pads(buf, 3)
    for buf in (high1, high2):
        clear_pads(buf.at[pl.ds(2, 3)], 3)
    for copy in loads:
        copy.wait()
    for i in range(3):
        low0[i, PAD : PAD + NY] = low_ref[NY * i : NY * i + NY].astype(jnp.float32)
        high0[2 + i, PAD : PAD + NY] = high_ref[NY * i : NY * i + NY].astype(jnp.float32)
    for i in range(2):
        low0[3 + i, PAD : PAD + NY] = own_ref[i].astype(jnp.float32)
        high0[i, PAD : PAD + NY] = own_ref[2 + i].astype(jnp.float32)

    def far_perm(ref):
        both = ref[3 * NY : 3 * NY + 32].astype(jnp.float32)
        packed = both[0:12] + both[12:24]
        return [
            jnp.concatenate([packed[4 * i + q : 4 * i + q + 1] for q in range(4)], 1) for i in range(3)
        ]

    kp = kp_ref[...]
    set_perm(perm_ref, jnp.concatenate(far_perm(low_ref) + [kp[0:4], kp[12:16]] + far_perm(high_ref), 0))
    spread_faces(perm_ref, east, north, 13)
    sweep(low0, east, north, 1, 1, 3, into(low1, 0))
    sweep(high0, east, north, 1, 10, 3, into(high1, 2))
    blank = jnp.zeros((NY, LANES), jnp.float32)

    @pl.when(tile == 0)
    def _():
        low1[0, PAD : PAD + NY] = blank
        low1[1, PAD : PAD + NY] = blank

    @pl.when(tile == 63)
    def _():
        high1[3, PAD : PAD + NY] = blank
        high1[4, PAD : PAD + NY] = blank

    for copy in edges_in:
        copy.wait()
    sweep(low1, east, north, 1, 2, 3, into(low2, 0))
    sweep(high1, east, north, 1, 9, 3, into(high2, 2))

    @pl.when(tile == 0)
    def _():
        low2[0, PAD : PAD + NY] = blank

    @pl.when(tile == 63)
    def _():
        high2[4, PAD : PAD + NY] = blank

    sweep(low2, east, north, 1, 3, 3, into_snap(snap, 0, scale_ref))
    sweep(high2, east, north, 1, 8, 3, into_snap(snap, 3, scale_ref))
    for copy in send_out(me, snap, singles, stacks, INNER, OUTER, sems):
        copy.wait()


VM = pl.BlockSpec(memory_space=pltpu.VMEM)
SM = pl.BlockSpec(memory_space=pltpu.SMEM)
ANY = pl.BlockSpec(memory_space=pl.ANY)


def half(rows):
    return jax.ShapeDtypeStruct((rows, LANES), jnp.bfloat16)


def planes(count):
    return pltpu.VMEM((count, WIDE, LANES), jnp.float32)


def inner_call(me, weights, own, kp):
    edge = jax.ShapeDtypeStruct((4, WIDE, LANES), jnp.float32)
    return pl.pallas_call(
        inner_rows,
        out_shape=[half(INNER)] * 3 + [half(3 * PIECE), half(2 * PIECE), half(PIECE)] + [edge] * 2,
        in_specs=[SM, SM, ANY, VM],
        out_specs=[ANY] * 8,
        scratch_shapes=[planes(16), planes(16), planes(15), planes(15)]
        + [pltpu.VMEM((WIDE, LANES), jnp.float32), pltpu.VMEM((4, INNER, LANES), jnp.bfloat16)]
        + [pltpu.VMEM((16, NY, LANES), jnp.bfloat16)]
        + [pltpu.SemaphoreType.DMA((12,)), pltpu.SemaphoreType.DMA((4,))],
        compiler_params=pltpu.CompilerParams(vmem_limit_bytes=63 << 20),
        cost_estimate=pl.CostEstimate(flops=400 << 20, bytes_accessed=9 << 20, transcendentals=0),
    )(me, weights, own, kp)


def outer_call(me, tile, weights, own, kp, low, high, edge_one, edge_two, stacks):
    return pl.pallas_call(
        outer_rows,
        out_shape=[half(OUTER)] * 3 + [half(3 * PIECE), half(2 * PIECE), half(PIECE)],
        in_specs=[SM, SM, SM, ANY, VM] + [ANY] * 7,
        out_specs=[ANY] * 6,
        input_output_aliases={9 + n: 3 + n for n in range(3)},
        scratch_shapes=[planes(5)] * 6
        + [planes(13), planes(13), pltpu.VMEM((WIDE, LANES), jnp.float32)]
        + [pltpu.VMEM((4, OUTER, LANES), jnp.bfloat16)]
        + [pltpu.VMEM((3 * NY + 32, LANES), jnp.bfloat16)] * 2
        + [pltpu.VMEM((4, NY, LANES), jnp.bfloat16)]
        + [pltpu.SemaphoreType.DMA((12,)), pltpu.SemaphoreType.DMA((4,))],
        compiler_params=pltpu.CompilerParams(vmem_limit_bytes=63 << 20),
        cost_estimate=pl.CostEstimate(flops=200 << 20, bytes_accessed=9 << 20, transcendentals=0),
    )(me, tile, weights, own, kp, low, high, edge_one, edge_two, *stacks)


def grams(me_ref, core_ref, *refs):
    pieces, own_ref, other_ref, wide, sems = refs[:7], refs[7], refs[8], refs[9], refs[10]
    me, core = me_ref[0], core_ref[0]
    copies = []
    for e in range(4):
        lanes = pl.ds(pl.multiple_of((me ^ e) * 128, 128), 128)
        if e == 0:
            moves = [(pieces[0].at[pl.ds(0, PIECE)], 0, PIECE)]
        else:
            moves = [(pieces[e], 0, INNER), (pieces[3 + e], INNER, OUTER)]
        for source, begin, size in moves:
            target = wide.at[pl.ds(begin, size), lanes]
            copies.append(pltpu.make_async_copy(source, target, sems.at[len(copies)]))
    for copy in copies:
        copy.start()
    for copy in copies:
        copy.wait()
    left, right = wide[:, :256], wide[:, 256:]
    near = lax.dot_general(left, left, ATB, preferred_element_type=jnp.float32)
    far = lax.dot_general(right, right, ATB, preferred_element_type=jnp.float32)
    cross = lax.dot_general(left, right, ATB, preferred_element_type=jnp.float32)
    blocks = [
        near[:128, :128], near[128:, 128:], far[:128, :128], far[128:, 128:], near[:128, 128:],
        far[:128, 128:], cross[:128, :128], cross[:128, 128:], cross[128:, :128], cross[128:, 128:],
    ]
    for side in (0, 1):

        @pl.when(core == side)
        def _(side=side):
            for half, ref in enumerate((own_ref, other_ref) if side == 0 else (other_ref, own_ref)):
                mine = blocks[5 * half : 5 * half + 5]
                ref[:, 0:16] = jnp.concatenate(mine[:4], 0).reshape(32, 16, 128)
                ref[:, 16:24] = jnp.zeros((32, 8, 128), jnp.float32)
                for k in range(32):
                    ref[k, 16:20] = mine[4][4 * k : 4 * k + 4]


def grams_call(me, core, pieces):
    shape = jax.ShapeDtypeStruct((32, 24, 128), jnp.float32)
    return pl.pallas_call(
        grams,
        out_shape=(shape, shape),
        in_specs=[SM, SM] + [ANY] * 7,
        out_specs=(VM, VM),
        scratch_shapes=[pltpu.VMEM((PIECE, 512), jnp.bfloat16), pltpu.SemaphoreType.DMA((7,))],
        compiler_params=pltpu.CompilerParams(vmem_limit_bytes=63 << 20),
        cost_estimate=pl.CostEstimate(flops=2 * 2048 * 512 * 512, bytes_accessed=3 << 20, transcendentals=0),
    )(me, core, *pieces)


def mixing_call(cells, me, core, own, other, start_codes):
    shape = jax.ShapeDtypeStruct((512, 128), jnp.bfloat16)
    vmem = pl.BlockSpec(memory_space=pltpu.VMEM)
    smem = pl.BlockSpec(memory_space=pltpu.SMEM)
    return pl.pallas_call(
        functools.partial(mixing, cells),
        out_shape=(shape, shape),
        in_specs=[smem, smem, ANY, ANY, vmem],
        out_specs=(vmem, vmem),
        scratch_shapes=[pltpu.VMEM((10, 128, 128), jnp.float32)]
        + [pltpu.VMEM((32, 24, 128), jnp.float32)] * 2
        + [pltpu.SemaphoreType.DMA((2,))],
        compiler_params=pltpu.CompilerParams(vmem_limit_bytes=62 << 20),
        cost_estimate=pl.CostEstimate(flops=1 << 30, bytes_accessed=1 << 20, transcendentals=0),
    )(me, core, own, other, start_codes)


def finish(plan, me_ref, high_ref, low_ref, *refs):
    pieces, out_ref = refs[:-5], refs[-5]
    wide, done, in_sems, out_sems = refs[-4:]
    me = me_ref[0]
    loads = []
    for j in range(4):
        group = []
        for e in range(4):
            for index, source, target, size in plan[4 * j + e]:
                group.append(
                    pltpu.make_async_copy(
                        pieces[index].at[pl.ds(source, size)],
                        wide.at[j, pl.ds(target, size), pl.ds(128 * e, 128)],
                        in_sems.at[len(loads), len(group)],
                    )
                )
                group[-1].start()
        loads.append(group)
    mix = jnp.concatenate([high_ref[...], low_ref[...]], 1)
    stores = []
    for j in range(4):
        for copy in loads[j]:
            copy.wait()
        for r in range(16):
            both = jnp.dot(wide[j, 128 * r : 128 * r + 128], mix, preferred_element_type=jnp.float32)
            done[j, r] = (both[:, :128] + both[:, 128:]).astype(jnp.bfloat16)
        columns = pl.ds(pl.multiple_of((me ^ j) * GROUP, GROUP), GROUP)
        for n, (source, target, size) in enumerate(((0, 3, 10), (10, 0, 3), (13, 13, 3))):
            copy = pltpu.make_async_copy(
                done.at[j, pl.ds(source, size)], out_ref.at[pl.ds(target, size), columns], out_sems.at[j, n]
            )
            copy.start()
            stores.append(copy)
    for copy in stores:
        copy.wait()


def finish_call(me, high, low, pieces, plan):
    return pl.pallas_call(
        functools.partial(finish, plan),
        out_shape=jax.ShapeDtypeStruct((16, NY, LANES), jnp.bfloat16),
        in_specs=[SM, VM, VM] + [ANY] * len(pieces),
        out_specs=ANY,
        scratch_shapes=[
            pltpu.VMEM((4, PIECE, 512), jnp.bfloat16),
            pltpu.VMEM((4, 16, GROUP, LANES), jnp.bfloat16),
            pltpu.SemaphoreType.DMA((4, 8)),
            pltpu.SemaphoreType.DMA((4, 3)),
        ],
        compiler_params=pltpu.CompilerParams(vmem_limit_bytes=63 << 20),
        cost_estimate=pl.CostEstimate(flops=2 * 8192 * 512 * 256, bytes_accessed=10 << 20, transcendentals=0),
    )(me, high, low, *pieces)


def packed_edge(cells, perm):
    high = perm.astype(jnp.bfloat16)
    low = (perm - high.astype(jnp.float32)).astype(jnp.bfloat16)
    parts = [cells.reshape(-1, LANES), high.reshape(-1, LANES), low.reshape(-1, LANES)]
    return jnp.concatenate(parts + [jnp.zeros((8, LANES), jnp.bfloat16)], 0)


def merged_bases(forcing, permeability, merge_weights, start_codes):
    me = lax.axis_index("case").astype(jnp.int32).reshape(1)
    tile = lax.axis_index("tile").astype(jnp.int32).reshape(1)
    core = tile & 1
    cells = forcing.shape[1] * lax.axis_size("tile") * forcing.shape[2]
    own, kp = forcing[0], permeability[0]
    up = [(i, i + 1) for i in range(63)]
    down = [(i + 1, i) for i in range(63)]
    low = lax.ppermute(packed_edge(own[-STEPS:], kp[-STEPS:]), "tile", up)
    high = lax.ppermute(packed_edge(own[:STEPS], kp[:STEPS]), "tile", down)
    inner = inner_call(me, merge_weights, own, kp)
    met = [case_swap(inner[e - 1], e) for e in (1, 2, 3)]
    outer = outer_call(me, tile, merge_weights, own, kp, low, high, inner[6], inner[7], inner[3:6])
    one, two, three = outer[3:]
    met = met + [case_swap(outer[e - 1], e) for e in (1, 2, 3)]
    far_one, far_two, far_three = case_swap(one, 1), case_swap(two, 3), case_swap(three, 3)
    via_one = [case_swap(met[2], 1), case_swap(met[5], 1), case_swap(far_three, 1)]
    via_three = [case_swap(met[0], 3), case_swap(met[3], 3)]
    own_part, other_part = grams_call(me, core, [one] + met)
    part = own_part + core_swap(other_part)
    part = plane_exchange(part).sum(0)
    part = part + case_swap(part, 1) + case_swap(part, 2) + case_swap(part, 3)
    mine = plane_exchange(jnp.broadcast_to(part, (32,) + part.shape))
    yours = core_swap(mine)
    high, low = mixing_call(cells, me, core, mine, yours, start_codes)
    pieces = [one, two, three] + met + [far_one, far_two, far_three] + via_one + via_three
    whole = ((0, PIECE),)
    split = ((0, INNER), (INNER, OUTER))
    places = {
        (0, 0): [(0, 0)], (0, 1): [(1, PIECE)], (0, 2): [(0, 2 * PIECE)], (0, 3): [(0, PIECE)],
        (1, 0): [(3, 0), (6, 0)], (2, 0): [(4, 0), (7, 0)], (3, 0): [(5, 0), (8, 0)],
        (1, 1): [(9, 0)], (1, 2): [(9, PIECE)], (1, 3): [(9, 2 * PIECE)],
        (3, 1): [(10, 0)], (3, 2): [(10, PIECE)], (3, 3): [(11, 0)],
        (2, 1): [(12, 0), (13, 0)], (2, 2): [(14, 0)], (2, 3): [(15, 0), (16, 0)],
    }
    plan = []
    for j in range(4):
        for e in range(4):
            sources = places[e, j]
            spans = whole if len(sources) == 1 else split
            plan.append(tuple((i, b, t, n) for (i, b), (t, n) in zip(sources, spans)))
    return finish_call(me, high, low, pieces, tuple(plan)).reshape(1, -1, LANES)


def solution(mesh):
    placed = (P("case", "tile", None, None), P("case", "tile", None), P("case"), P())
    return jax.shard_map(merged_bases, mesh=mesh, in_specs=placed, out_specs=P("case", "tile", None), check_vma=False)
```

```python
import functools
import math

import jax
import jax.numpy as jnp
from jax import lax
from jax.experimental import pallas as pl
from jax.experimental.pallas import tpu as pltpu
from jax.sharding import PartitionSpec as P

STEPS = 3


def at(z, y, core):
    return (z * 4 + y) * 2 + core


LINES = [[at(z, y, core) for z in range(8)] for y in range(4) for core in range(2)]


def case_swap(value, apart):
    return lax.ppermute(value, "case", [(source, source ^ apart) for source in range(4)])


def core_swap(value):
    return lax.ppermute(value, "tile", [(source, source ^ 1) for source in range(64)])


def row_swap(value, apart):
    pairs = [(at(z, y, c), at(z, y ^ apart, c)) for z in range(8) for y in range(4) for c in range(2)]
    return lax.ppermute(value, "tile", pairs)


def line_exchange(value):
    return lax.all_to_all(value, "tile", 0, 0, axis_index_groups=LINES)


AB = (((1,), (0,)), ((), ()))
ATB = (((0,), (0,)), ((), ()))
ABT = (((1,), (1,)), ((), ()))


def parts_of(x, exact=False):
    high = x.astype(jnp.bfloat16)
    if exact:
        return (high,)
    rest = x - high.astype(jnp.float32)
    mid = rest.astype(jnp.bfloat16)
    low = (rest - mid.astype(jnp.float32)).astype(jnp.bfloat16)
    return (high, mid, low)


def product(a, b, dims=AB):
    out = None
    for i in range(len(a) - 1, -1, -1):
        for j in range(len(b) - 1, -1, -1):
            if i + j < 3:
                term = lax.dot_general(a[i], b[j], dims, preferred_element_type=jnp.float32)
                out = term if out is None else out + term
    return out


def spread(x, axis, index, size):
    piece = lax.slice_in_dim(x, index, index + 1, axis=axis)
    shape = (size, x.shape[1]) if axis == 0 else (x.shape[0], size)
    return jnp.broadcast_to(piece, shape)


def inverse_factors(mats):
    lane = lax.broadcasted_iota(jnp.int32, (8, 128), 1)
    sub = lax.broadcasted_iota(jnp.int32, (8, 128), 0)
    tiles = [[m[8 * b : 8 * b + 8] for b in range(16)] for m in mats]
    for big in range(4):
        for a in tiles:
            left, right = [], []
            for k in range(4 * big, 4 * big + 4):
                first = 8 * k
                block = (lane >= first) & (lane < first + 8)
                rows = [spread(a[k], 0, r, 8) for r in range(8)]
                piv = [
                    [spread(rows[r], 1, first + s, 128) if s >= r else None for s in range(8)]
                    for r in range(8)
                ]
                inv = [None] * 8
                mul = [[None] * 8 for _ in range(8)]
                for r in range(8):
                    inv[r] = 1.0 / piv[r][r]
                    for s in range(r + 1, 8):
                        mul[r][s] = piv[r][s] * inv[r]
                    for s in range(r + 1, 8):
                        for t in range(s, 8):
                            piv[s][t] = piv[s][t] - mul[r][s] * piv[r][t]
                for s in range(8):
                    rows[s] = jnp.where(block, jnp.where(lane == first + s, 1.0, 0.0), rows[s])
                for s in range(8):
                    for r in range(s):
                        rows[s] = rows[s] - mul[r][s] * rows[r]
                scaled = [rows[r] * inv[r] for r in range(8)]
                for b in range(k + 1, 4 * big + 4):
                    col = [spread(a[b], 1, first + r, 128) for r in range(8)]
                    for r in range(8):
                        for s in range(r + 1, 8):
                            col[s] = col[s] - col[r] * mul[r][s]
                    new = jnp.where(block, 0.0, a[b])
                    for r in range(8):
                        new = new - col[r] * scaled[r]
                    a[b] = new
                plain, pivots, inverse = rows[0], piv[0][0], inv[0]
                for r in range(1, 8):
                    plain = jnp.where(sub == r, rows[r], plain)
                    pivots = jnp.where(sub == r, piv[r][r], pivots)
                    inverse = jnp.where(sub == r, inv[r], inverse)
                left.append(plain)
                later = (lane >= first + 8) & (lane < 32 * (big + 1))
                right.append(jnp.where(later, 0.0, plain * inverse))
                a[k] = jnp.where(lane < first + 8, plain * lax.rsqrt(pivots), 0.0)
            if big < 3:
                after = 32 * (big + 1)
                x = parts_of(jnp.concatenate(left, 0))
                y = parts_of(jnp.concatenate(right, 0))
                x = jnp.concatenate([x[0], x[0], x[1], x[0], x[2], x[1]], 0)
                y = jnp.concatenate([y[0], y[1], y[0], y[2], y[0], y[1]], 0)
                update = lax.dot_general(x, y, ATB, preferred_element_type=jnp.float32)
                used = (lane >= 32 * big) & (lane < after)
                for b in range(4 * big + 4, 16):
                    a[b] = jnp.where(used, 0.0, a[b]) - update[8 * b : 8 * b + 8]
    return [jnp.concatenate(a, 0) for a in tiles]


def mixing(cells, me_ref, core_ref, y_ref, own_hbm, other_hbm, start_ref, high_ref, low_ref, *scratch):
    gram_ref, own_ref, other_ref, sems = scratch
    me, core = me_ref[0], core_ref[0]
    loads = [
        pltpu.make_async_copy(own_hbm, own_ref, sems.at[0]),
        pltpu.make_async_copy(other_hbm, other_ref, sems.at[1]),
    ]
    for copy in loads:
        copy.start()
    for copy in loads:
        copy.wait()
    for side in (0, 1):

        @pl.when(core == side)
        def _(side=side):
            for half, ref in enumerate((own_ref, other_ref) if side == 0 else (other_ref, own_ref)):
                for y in range(4):
                    slot = y_ref[0] ^ y
                    for z in range(8):
                        k = 4 * z + y
                        row = 16 * (k % 8)
                        gram_ref[5 * half + k // 8, row : row + 16] = ref[slot, z, 0:16]
                        gram_ref[5 * half + 4, 4 * k : 4 * k + 4] = ref[slot, z, 16:20]

    odd = lax.rem(me, 2) == 1
    upper = me // 2

    def side(index, flip):
        x = gram_ref[index]
        return jnp.where(flip, x.T, x)

    def merged(coeff_parts, gram_parts):
        t = product(gram_parts, coeff_parts)
        return product(coeff_parts, parts_of(t), ATB)

    start = parts_of(start_ref[0].astype(jnp.float32), True)
    coeffs, inners = [], []
    for half in (0, 1):
        a, b = me ^ (2 * half), me ^ (2 * half + 1)
        near = side(4 + (upper ^ half), odd)
        gram = jnp.concatenate(
            [jnp.concatenate([gram_ref[a], near], 1), jnp.concatenate([near.T, gram_ref[b]], 1)], 0
        )
        gram = parts_of(gram)
        first = product(gram, start) / cells
        second = product(gram, parts_of(first)) / cells
        coeff = (second.astype(jnp.bfloat16),)
        coeffs.append(coeff)
        inners.append(merged(coeff, gram))
    inverse = inverse_factors(inners)
    scale = math.sqrt(cells)
    maps = [scale * product(c, parts_of(v), ABT) for c, v in zip(coeffs, inverse)]
    maps = [parts_of(m) for m in maps]
    low_group = upper == 0
    rows = []
    for e in (0, 1):
        line = []
        for f in (2, 3):
            a, b = me ^ e, me ^ f
            index = jnp.where(low_group, 6 + 2 * a + (b - 2), 6 + 2 * b + (a - 2))
            line.append(side(index, upper == 1))
        rows.append(jnp.concatenate(line, 1))
    across = parts_of(jnp.concatenate(rows, 0))
    cross = product(maps[0], parts_of(product(across, maps[1])), ATB)
    cross = parts_of(cross / cells)
    start = start_ref[1].astype(jnp.float32)
    top, bottom = start[:128], start[128:]
    exact = True
    for _ in range(2):
        top, bottom = (
            top + product(cross, parts_of(bottom, exact)),
            bottom + product(cross, parts_of(top, exact), ATB),
        )
        exact = False
    top, bottom = (top.astype(jnp.bfloat16),), (bottom.astype(jnp.bfloat16),)
    mixed = product(top, parts_of(product(cross, bottom)), ATB)
    inner = product(top, top, ATB) + product(bottom, bottom, ATB) + mixed + mixed.T
    (last,) = inverse_factors([inner])
    last = parts_of(last)
    for half, coeff in enumerate((top, bottom)):
        step = product(coeff, last, ABT)
        final = product(maps[half], parts_of(step))
        high = final.astype(jnp.bfloat16)
        high_ref[pl.ds(256 * half, 256), :] = high
        low_ref[pl.ds(256 * half, 256), :] = (final - high.astype(jnp.float32)).astype(jnp.bfloat16)


NY, LANES, PAD = 512, 128, 8
WIDE = PAD + NY + PAD
GROUP = 128
INNER, OUTER = 10 * GROUP, 6 * GROUP
PIECE = INNER + OUTER


def spread_faces(perm_ref, east, north, count):
    here = perm_ref[...]
    after = jnp.concatenate([here[1:], here[:1]], 0)
    row = lax.broadcasted_iota(jnp.int32, (256, 256), 0) & 127
    second = lax.broadcasted_iota(jnp.int32, (256, 256), 1) >> 7
    faces = []
    for value in (0.12 * (here + after), 0.12 * (here + pltpu.roll(here, LANES - 1, axis=1))):
        high = value.astype(jnp.bfloat16)
        low = (value - high.astype(jnp.float32)).astype(jnp.bfloat16)
        faces.append(jnp.concatenate([high, low], 1))
    for i in range(0, count, 2):
        pick = jnp.where(row == second + i, 1.0, 0.0).astype(jnp.bfloat16)
        for face, out in zip(faces, (east, north)):
            both = jnp.dot(face, pick, preferred_element_type=jnp.float32)
            out[i] = both[:, :LANES]
            if i + 1 < count:
                out[i + 1] = both[:, LANES:]


def set_perm(perm_ref, rows):
    count = rows.shape[0]
    rows = jnp.concatenate([rows, jnp.zeros((LANES - count, NY), jnp.float32)], 0)
    perm_ref[0:PAD] = jnp.zeros((PAD, LANES), jnp.float32)
    perm_ref[PAD : PAD + NY] = rows.T
    perm_ref[PAD + NY : WIDE] = jnp.zeros((PAD, LANES), jnp.float32)


def clear_pads(buf, count):
    def one(i, _):
        buf[i, 0:PAD] = jnp.zeros((PAD, LANES), jnp.float32)
        buf[i, PAD + NY : WIDE] = jnp.zeros((PAD, LANES), jnp.float32)
        return 0

    lax.fori_loop(0, count, one, 0)


def sweep(source, east, north, begin, face, count, write):
    for g in range(NY // GROUP):
        c = PAD + g * GROUP

        def one(i, carry, c=c, g=g):
            row, plane = begin + i, face + i
            center, south = carry
            above = source[row + 1, c : c + GROUP]
            up = north[plane, c : c + GROUP] * (above - center)
            east_here = east[plane, c : c + GROUP]
            flux = east_here * (source[row, c + 1 : c + GROUP + 1] - center)
            before = source[row, c - PAD : c]
            edge = east[plane, c - PAD : c] * (source[row, c - PAD + 1 : c + 1] - before)
            shifted = jnp.concatenate([edge, flux], 0)[PAD - 1 : PAD - 1 + GROUP]
            write(i, g, center + ((up - south) + (flux - shifted)))
            return above, up

        center = source[begin, c : c + GROUP]
        south = north[face - 1, c : c + GROUP] * (center - source[begin - 1, c : c + GROUP])
        lax.fori_loop(0, count, one, (center, south))


def into(buf, base):
    def write(i, g, value):
        buf[base + i, PAD + g * GROUP : PAD + g * GROUP + GROUP] = value

    return write


def into_snap(snap, base, scale_ref):
    scale = jnp.sqrt(jnp.full((8, LANES), scale_ref[0].astype(jnp.float32)))
    scale = jnp.broadcast_to(scale[0:1], (GROUP, LANES))

    def write(i, g, value):
        at0 = pl.multiple_of((base + i) * GROUP, GROUP)
        snap[g, pl.ds(at0, GROUP)] = (value * scale).astype(jnp.bfloat16)

    return write


def send_out(me, snap, singles, stacks, begin, size, sems):
    one, two, three = stacks
    moves = [(singles[e - 1], e, 0) for e in (1, 2, 3)]
    moves += [(one, j ^ 1, PIECE * (j - 1) + begin) for j in (1, 2, 3)]
    moves += [(two, 2, begin), (two, 1, PIECE + begin), (three, 0, begin)]
    copies = []
    for target, j, at0 in moves:
        copies.append(
            pltpu.make_async_copy(snap.at[me ^ j], target.at[pl.ds(at0, size)], sems.at[len(copies)])
        )
    for copy in copies:
        copy.start()
    return copies


def inner_rows(me_ref, scale_ref, own_ref, kp_ref, *refs):
    singles, stacks, edge_one, edge_two = refs[:3], refs[3:6], refs[6], refs[7]
    first, second, east, north, perm_ref, snap, held, sems, edge_sems = refs[8:]
    me = me_ref[0]
    load = pltpu.make_async_copy(own_ref, held, sems.at[0])
    load.start()
    clear_pads(first, 16)
    clear_pads(second, 16)

    def fill(i, _):
        first[i, PAD : PAD + NY] = held[i].astype(jnp.float32)
        return 0

    set_perm(perm_ref, kp_ref[...])
    spread_faces(perm_ref, east, north, 15)
    load.wait()
    lax.fori_loop(0, 16, fill, 0)
    sweep(first, east, north, 1, 1, 14, into(second, 1))
    sweep(second, east, north, 2, 2, 12, into(first, 2))
    edges_out = [
        pltpu.make_async_copy(second.at[pl.ds(1, 2)], edge_one.at[pl.ds(0, 2)], edge_sems.at[0]),
        pltpu.make_async_copy(second.at[pl.ds(13, 2)], edge_one.at[pl.ds(2, 2)], edge_sems.at[1]),
        pltpu.make_async_copy(first.at[pl.ds(2, 2)], edge_two.at[pl.ds(0, 2)], edge_sems.at[2]),
        pltpu.make_async_copy(first.at[pl.ds(12, 2)], edge_two.at[pl.ds(2, 2)], edge_sems.at[3]),
    ]
    for copy in edges_out:
        copy.start()
    sweep(first, east, north, 3, 3, 10, into_snap(snap, 0, scale_ref))
    for copy in edges_out + send_out(me, snap, singles, stacks, 0, INNER, sems):
        copy.wait()


def outer_rows(me_ref, tile_ref, scale_ref, own_hbm, kp_ref, low_hbm, high_hbm, edge_one, edge_two, *refs):
    singles, stacks = refs[3:6], refs[6:9]
    low0, low1, low2, high0, high1, high2, east, north, perm_ref, snap = refs[9:19]
    low_ref, high_ref, own_ref, sems, edge_sems = refs[19:]
    me, tile = me_ref[0], tile_ref[0]
    loads = [
        pltpu.make_async_copy(low_hbm, low_ref, sems.at[0]),
        pltpu.make_async_copy(high_hbm, high_ref, sems.at[1]),
        pltpu.make_async_copy(own_hbm.at[pl.ds(0, 2)], own_ref.at[pl.ds(0, 2)], sems.at[2]),
        pltpu.make_async_copy(own_hbm.at[pl.ds(14, 2)], own_ref.at[pl.ds(2, 2)], sems.at[3]),
    ]
    for copy in loads:
        copy.start()
    edges_in = [
        pltpu.make_async_copy(edge_one.at[pl.ds(0, 2)], low1.at[pl.ds(3, 2)], edge_sems.at[0]),
        pltpu.make_async_copy(edge_one.at[pl.ds(2, 2)], high1.at[pl.ds(0, 2)], edge_sems.at[1]),
        pltpu.make_async_copy(edge_two.at[pl.ds(0, 2)], low2.at[pl.ds(3, 2)], edge_sems.at[2]),
        pltpu.make_async_copy(edge_two.at[pl.ds(2, 2)], high2.at[pl.ds(0, 2)], edge_sems.at[3]),
    ]
    for copy in edges_in:
        copy.start()
    for buf in (low0, high0):
        clear_pads(buf, 5)
    for buf in (low1, low2):
        clear_pads(buf, 3)
    for buf in (high1, high2):
        clear_pads(buf.at[pl.ds(2, 3)], 3)
    for copy in loads:
        copy.wait()
    for i in range(3):
        low0[i, PAD : PAD + NY] = low_ref[NY * i : NY * i + NY].astype(jnp.float32)
        high0[2 + i, PAD : PAD + NY] = high_ref[NY * i : NY * i + NY].astype(jnp.float32)
    for i in range(2):
        low0[3 + i, PAD : PAD + NY] = own_ref[i].astype(jnp.float32)
        high0[i, PAD : PAD + NY] = own_ref[2 + i].astype(jnp.float32)

    def far_perm(ref):
        both = ref[3 * NY : 3 * NY + 32].astype(jnp.float32)
        packed = both[0:12] + both[12:24]
        return [
            jnp.concatenate([packed[4 * i + q : 4 * i + q + 1] for q in range(4)], 1) for i in range(3)
        ]

    kp = kp_ref[...]
    set_perm(perm_ref, jnp.concatenate(far_perm(low_ref) + [kp[0:4], kp[12:16]] + far_perm(high_ref), 0))
    spread_faces(perm_ref, east, north, 13)
    sweep(low0, east, north, 1, 1, 3, into(low1, 0))
    sweep(high0, east, north, 1, 10, 3, into(high1, 2))
    blank = jnp.zeros((NY, LANES), jnp.float32)

    @pl.when(tile == 0)
    def _():
        low1[0, PAD : PAD + NY] = blank
        low1[1, PAD : PAD + NY] = blank

    @pl.when(tile == 63)
    def _():
        high1[3, PAD : PAD + NY] = blank
        high1[4, PAD : PAD + NY] = blank

    for copy in edges_in:
        copy.wait()
    sweep(low1, east, north, 1, 2, 3, into(low2, 0))
    sweep(high1, east, north, 1, 9, 3, into(high2, 2))

    @pl.when(tile == 0)
    def _():
        low2[0, PAD : PAD + NY] = blank

    @pl.when(tile == 63)
    def _():
        high2[4, PAD : PAD + NY] = blank

    sweep(low2, east, north, 1, 3, 3, into_snap(snap, 0, scale_ref))
    sweep(high2, east, north, 1, 8, 3, into_snap(snap, 3, scale_ref))
    for copy in send_out(me, snap, singles, stacks, INNER, OUTER, sems):
        copy.wait()


VM = pl.BlockSpec(memory_space=pltpu.VMEM)
SM = pl.BlockSpec(memory_space=pltpu.SMEM)
ANY = pl.BlockSpec(memory_space=pl.ANY)


def half(rows):
    return jax.ShapeDtypeStruct((rows, LANES), jnp.bfloat16)


def planes(count):
    return pltpu.VMEM((count, WIDE, LANES), jnp.float32)


def inner_call(me, weights, own, kp):
    edge = jax.ShapeDtypeStruct((4, WIDE, LANES), jnp.float32)
    return pl.pallas_call(
        inner_rows,
        out_shape=[half(INNER)] * 3 + [half(3 * PIECE), half(2 * PIECE), half(PIECE)] + [edge] * 2,
        in_specs=[SM, SM, ANY, VM],
        out_specs=[ANY] * 8,
        scratch_shapes=[planes(16), planes(16), planes(15), planes(15)]
        + [pltpu.VMEM((WIDE, LANES), jnp.float32), pltpu.VMEM((4, INNER, LANES), jnp.bfloat16)]
        + [pltpu.VMEM((16, NY, LANES), jnp.bfloat16)]
        + [pltpu.SemaphoreType.DMA((12,)), pltpu.SemaphoreType.DMA((4,))],
        compiler_params=pltpu.CompilerParams(vmem_limit_bytes=63 << 20),
        cost_estimate=pl.CostEstimate(flops=400 << 20, bytes_accessed=9 << 20, transcendentals=0),
    )(me, weights, own, kp)


def outer_call(me, tile, weights, own, kp, low, high, edge_one, edge_two, stacks):
    return pl.pallas_call(
        outer_rows,
        out_shape=[half(OUTER)] * 3 + [half(3 * PIECE), half(2 * PIECE), half(PIECE)],
        in_specs=[SM, SM, SM, ANY, VM] + [ANY] * 7,
        out_specs=[ANY] * 6,
        input_output_aliases={9 + n: 3 + n for n in range(3)},
        scratch_shapes=[planes(5)] * 6
        + [planes(13), planes(13), pltpu.VMEM((WIDE, LANES), jnp.float32)]
        + [pltpu.VMEM((4, OUTER, LANES), jnp.bfloat16)]
        + [pltpu.VMEM((3 * NY + 32, LANES), jnp.bfloat16)] * 2
        + [pltpu.VMEM((4, NY, LANES), jnp.bfloat16)]
        + [pltpu.SemaphoreType.DMA((12,)), pltpu.SemaphoreType.DMA((4,))],
        compiler_params=pltpu.CompilerParams(vmem_limit_bytes=63 << 20),
        cost_estimate=pl.CostEstimate(flops=200 << 20, bytes_accessed=9 << 20, transcendentals=0),
    )(me, tile, weights, own, kp, low, high, edge_one, edge_two, *stacks)


def grams(me_ref, core_ref, y_ref, *refs):
    pieces, own_ref, other_ref, wide, sems = refs[:7], refs[7], refs[8], refs[9], refs[10]
    me, core = me_ref[0], core_ref[0]
    copies = []
    for e in range(4):
        lanes = pl.ds(pl.multiple_of((me ^ e) * 128, 128), 128)
        if e == 0:
            moves = [(pieces[0].at[pl.ds(0, PIECE)], 0, PIECE)]
        else:
            moves = [(pieces[e], 0, INNER), (pieces[3 + e], INNER, OUTER)]
        for source, begin, size in moves:
            target = wide.at[pl.ds(begin, size), lanes]
            copies.append(pltpu.make_async_copy(source, target, sems.at[len(copies)]))
    for copy in copies:
        copy.start()
    for copy in copies:
        copy.wait()
    left, right = wide[:, :256], wide[:, 256:]
    near = lax.dot_general(left, left, ATB, preferred_element_type=jnp.float32)
    far = lax.dot_general(right, right, ATB, preferred_element_type=jnp.float32)
    cross = lax.dot_general(left, right, ATB, preferred_element_type=jnp.float32)
    blocks = [
        near[:128, :128], near[128:, 128:], far[:128, :128], far[128:, 128:], near[:128, 128:],
        far[:128, 128:], cross[:128, :128], cross[:128, 128:], cross[128:, :128], cross[128:, 128:],
    ]
    for side in (0, 1):

        @pl.when(core == side)
        def _(side=side):
            for half, ref in enumerate((own_ref, other_ref) if side == 0 else (other_ref, own_ref)):
                mine = blocks[5 * half : 5 * half + 5]
                big = jnp.concatenate(mine[:4], 0)
                for y in range(4):
                    slot = y_ref[0] ^ y
                    for z in range(8):
                        k = 4 * z + y
                        ref[slot, z, 0:16] = big[16 * k : 16 * k + 16]
                        ref[slot, z, 16:24] = jnp.zeros((8, 128), jnp.float32)
                        ref[slot, z, 16:20] = mine[4][4 * k : 4 * k + 4]


def grams_call(me, core, row, pieces):
    shape = jax.ShapeDtypeStruct((4, 8, 24, 128), jnp.float32)
    return pl.pallas_call(
        grams,
        out_shape=(shape, shape),
        in_specs=[SM, SM, SM] + [ANY] * 7,
        out_specs=(VM, VM),
        scratch_shapes=[pltpu.VMEM((PIECE, 512), jnp.bfloat16), pltpu.SemaphoreType.DMA((7,))],
        compiler_params=pltpu.CompilerParams(vmem_limit_bytes=63 << 20),
        cost_estimate=pl.CostEstimate(flops=2 * 2048 * 512 * 512, bytes_accessed=3 << 20, transcendentals=0),
    )(me, core, row, *pieces)


def mixing_call(cells, me, core, row, own, other, start_codes):
    shape = jax.ShapeDtypeStruct((512, 128), jnp.bfloat16)
    vmem = pl.BlockSpec(memory_space=pltpu.VMEM)
    smem = pl.BlockSpec(memory_space=pltpu.SMEM)
    return pl.pallas_call(
        functools.partial(mixing, cells),
        out_shape=(shape, shape),
        in_specs=[smem, smem, smem, ANY, ANY, vmem],
        out_specs=(vmem, vmem),
        scratch_shapes=[pltpu.VMEM((10, 128, 128), jnp.float32)]
        + [pltpu.VMEM((4, 8, 24, 128), jnp.float32)] * 2
        + [pltpu.SemaphoreType.DMA((2,))],
        compiler_params=pltpu.CompilerParams(vmem_limit_bytes=62 << 20),
        cost_estimate=pl.CostEstimate(flops=1 << 30, bytes_accessed=1 << 20, transcendentals=0),
    )(me, core, row, own, other, start_codes)


def finish(plan, me_ref, high_ref, low_ref, *refs):
    pieces, out_ref = refs[:-5], refs[-5]
    wide, done, in_sems, out_sems = refs[-4:]
    me = me_ref[0]
    loads = []
    for j in range(4):
        group = []
        for e in range(4):
            for index, source, target, size in plan[4 * j + e]:
                group.append(
                    pltpu.make_async_copy(
                        pieces[index].at[pl.ds(source, size)],
                        wide.at[j, pl.ds(target, size), pl.ds(128 * e, 128)],
                        in_sems.at[len(loads), len(group)],
                    )
                )
                group[-1].start()
        loads.append(group)
    mix = jnp.concatenate([high_ref[...], low_ref[...]], 1)
    stores = []
    for j in range(4):
        for copy in loads[j]:
            copy.wait()
        for r in range(16):
            both = jnp.dot(wide[j, 128 * r : 128 * r + 128], mix, preferred_element_type=jnp.float32)
            done[j, r] = (both[:, :128] + both[:, 128:]).astype(jnp.bfloat16)
        columns = pl.ds(pl.multiple_of((me ^ j) * GROUP, GROUP), GROUP)
        for n, (source, target, size) in enumerate(((0, 3, 10), (10, 0, 3), (13, 13, 3))):
            copy = pltpu.make_async_copy(
                done.at[j, pl.ds(source, size)], out_ref.at[pl.ds(target, size), columns], out_sems.at[j, n]
            )
            copy.start()
            stores.append(copy)
    for copy in stores:
        copy.wait()


def finish_call(me, high, low, pieces, plan):
    return pl.pallas_call(
        functools.partial(finish, plan),
        out_shape=jax.ShapeDtypeStruct((16, NY, LANES), jnp.bfloat16),
        in_specs=[SM, VM, VM] + [ANY] * len(pieces),
        out_specs=ANY,
        scratch_shapes=[
            pltpu.VMEM((4, PIECE, 512), jnp.bfloat16),
            pltpu.VMEM((4, 16, GROUP, LANES), jnp.bfloat16),
            pltpu.SemaphoreType.DMA((4, 8)),
            pltpu.SemaphoreType.DMA((4, 3)),
        ],
        compiler_params=pltpu.CompilerParams(vmem_limit_bytes=63 << 20),
        cost_estimate=pl.CostEstimate(flops=2 * 8192 * 512 * 256, bytes_accessed=10 << 20, transcendentals=0),
    )(me, high, low, *pieces)


def packed_edge(cells, perm):
    high = perm.astype(jnp.bfloat16)
    low = (perm - high.astype(jnp.float32)).astype(jnp.bfloat16)
    parts = [cells.reshape(-1, LANES), high.reshape(-1, LANES), low.reshape(-1, LANES)]
    return jnp.concatenate(parts + [jnp.zeros((8, LANES), jnp.bfloat16)], 0)


def merged_bases(forcing, permeability, merge_weights, start_codes):
    me = lax.axis_index("case").astype(jnp.int32).reshape(1)
    tile = lax.axis_index("tile").astype(jnp.int32).reshape(1)
    core = tile & 1
    row = (tile >> 1) & 3
    cells = forcing.shape[1] * lax.axis_size("tile") * forcing.shape[2]
    own, kp = forcing[0], permeability[0]
    up = [(i, i + 1) for i in range(63)]
    down = [(i + 1, i) for i in range(63)]
    low = lax.ppermute(packed_edge(own[-STEPS:], kp[-STEPS:]), "tile", up)
    high = lax.ppermute(packed_edge(own[:STEPS], kp[:STEPS]), "tile", down)
    inner = inner_call(me, merge_weights, own, kp)
    met = [case_swap(inner[e - 1], e) for e in (1, 2, 3)]
    outer = outer_call(me, tile, merge_weights, own, kp, low, high, inner[6], inner[7], inner[3:6])
    one, two, three = outer[3:]
    met = met + [case_swap(outer[e - 1], e) for e in (1, 2, 3)]
    far_one, far_two, far_three = case_swap(one, 1), case_swap(two, 3), case_swap(three, 3)
    via_one = [case_swap(met[2], 1), case_swap(met[5], 1), case_swap(far_three, 1)]
    via_three = [case_swap(met[0], 3), case_swap(met[3], 3)]
    own_part, other_part = grams_call(me, core, row, [one] + met)
    part = own_part + core_swap(other_part)
    part = part[0] + row_swap(part[1], 1) + row_swap(part[2], 2) + row_swap(part[3], 3)
    part = line_exchange(part).sum(0)
    part = part + case_swap(part, 1) + case_swap(part, 2) + case_swap(part, 3)
    mine = line_exchange(jnp.broadcast_to(part, (8,) + part.shape))
    mine = jnp.stack([mine, row_swap(mine, 1), row_swap(mine, 2), row_swap(mine, 3)])
    yours = core_swap(mine)
    high, low = mixing_call(cells, me, core, row, mine, yours, start_codes)
    pieces = [one, two, three] + met + [far_one, far_two, far_three] + via_one + via_three
    whole = ((0, PIECE),)
    split = ((0, INNER), (INNER, OUTER))
    places = {
        (0, 0): [(0, 0)], (0, 1): [(1, PIECE)], (0, 2): [(0, 2 * PIECE)], (0, 3): [(0, PIECE)],
        (1, 0): [(3, 0), (6, 0)], (2, 0): [(4, 0), (7, 0)], (3, 0): [(5, 0), (8, 0)],
        (1, 1): [(9, 0)], (1, 2): [(9, PIECE)], (1, 3): [(9, 2 * PIECE)],
        (3, 1): [(10, 0)], (3, 2): [(10, PIECE)], (3, 3): [(11, 0)],
        (2, 1): [(12, 0), (13, 0)], (2, 2): [(14, 0)], (2, 3): [(15, 0), (16, 0)],
    }
    plan = []
    for j in range(4):
        for e in range(4):
            sources = places[e, j]
            spans = whole if len(sources) == 1 else split
            plan.append(tuple((i, b, t, n) for (i, b), (t, n) in zip(sources, spans)))
    return finish_call(me, high, low, pieces, tuple(plan)).reshape(1, -1, LANES)


def solution(mesh):
    placed = (P("case", "tile", None, None), P("case", "tile", None), P("case"), P())
    return jax.shard_map(merged_bases, mesh=mesh, in_specs=placed, out_specs=P("case", "tile", None), check_vma=False)
```

```python
import functools
import math

import jax
import jax.numpy as jnp
from jax import lax
from jax.experimental import pallas as pl
from jax.experimental.pallas import tpu as pltpu
from jax.sharding import PartitionSpec as P

STEPS = 3


def at(z, y, core):
    return (z * 4 + y) * 2 + core


PLANES = [[at(z, y, core) for z in range(8) for y in range(4)] for core in range(2)]


def case_swap(value, apart):
    return lax.ppermute(value, "case", [(source, source ^ apart) for source in range(4)])


def core_swap(value):
    return lax.ppermute(value, "tile", [(source, source ^ 1) for source in range(64)])


def plane_exchange(value):
    return lax.all_to_all(value, "tile", 0, 0, axis_index_groups=PLANES)


AB = (((1,), (0,)), ((), ()))
ATB = (((0,), (0,)), ((), ()))
ABT = (((1,), (1,)), ((), ()))


def parts_of(x, exact=False):
    high = x.astype(jnp.bfloat16)
    if exact:
        return (high,)
    rest = x - high.astype(jnp.float32)
    mid = rest.astype(jnp.bfloat16)
    low = (rest - mid.astype(jnp.float32)).astype(jnp.bfloat16)
    return (high, mid, low)


def product(a, b, dims=AB):
    out = None
    for i in range(len(a) - 1, -1, -1):
        for j in range(len(b) - 1, -1, -1):
            if i + j < 3:
                term = lax.dot_general(a[i], b[j], dims, preferred_element_type=jnp.float32)
                out = term if out is None else out + term
    return out


def spread(x, axis, index, size):
    piece = lax.slice_in_dim(x, index, index + 1, axis=axis)
    shape = (size, x.shape[1]) if axis == 0 else (x.shape[0], size)
    return jnp.broadcast_to(piece, shape)


def inverse_factors(mats):
    lane = lax.broadcasted_iota(jnp.int32, (8, 128), 1)
    sub = lax.broadcasted_iota(jnp.int32, (8, 128), 0)
    tiles = [[m[8 * b : 8 * b + 8] for b in range(16)] for m in mats]
    for big in range(4):
        for a in tiles:
            left, right = [], []
            for k in range(4 * big, 4 * big + 4):
                first = 8 * k
                block = (lane >= first) & (lane < first + 8)
                rows = [spread(a[k], 0, r, 8) for r in range(8)]
                piv = [
                    [spread(rows[r], 1, first + s, 128) if s >= r else None for s in range(8)]
                    for r in range(8)
                ]
                inv = [None] * 8
                mul = [[None] * 8 for _ in range(8)]
                for r in range(8):
                    inv[r] = 1.0 / piv[r][r]
                    for s in range(r + 1, 8):
                        mul[r][s] = piv[r][s] * inv[r]
                    for s in range(r + 1, 8):
                        for t in range(s, 8):
                            piv[s][t] = piv[s][t] - mul[r][s] * piv[r][t]
                for s in range(8):
                    rows[s] = jnp.where(block, jnp.where(lane == first + s, 1.0, 0.0), rows[s])
                for s in range(8):
                    for r in range(s):
                        rows[s] = rows[s] - mul[r][s] * rows[r]
                scaled = [rows[r] * inv[r] for r in range(8)]
                for b in range(k + 1, 4 * big + 4):
                    col = [spread(a[b], 1, first + r, 128) for r in range(8)]
                    for r in range(8):
                        for s in range(r + 1, 8):
                            col[s] = col[s] - col[r] * mul[r][s]
                    new = jnp.where(block, 0.0, a[b])
                    for r in range(8):
                        new = new - col[r] * scaled[r]
                    a[b] = new
                plain, pivots, inverse = rows[0], piv[0][0], inv[0]
                for r in range(1, 8):
                    plain = jnp.where(sub == r, rows[r], plain)
                    pivots = jnp.where(sub == r, piv[r][r], pivots)
                    inverse = jnp.where(sub == r, inv[r], inverse)
                left.append(plain)
                later = (lane >= first + 8) & (lane < 32 * (big + 1))
                right.append(jnp.where(later, 0.0, plain * inverse))
                a[k] = jnp.where(lane < first + 8, plain * lax.rsqrt(pivots), 0.0)
            if big < 3:
                after = 32 * (big + 1)
                x = parts_of(jnp.concatenate(left, 0))
                y = parts_of(jnp.concatenate(right, 0))
                x = jnp.concatenate([x[0], x[0], x[1], x[0], x[2], x[1]], 0)
                y = jnp.concatenate([y[0], y[1], y[0], y[2], y[0], y[1]], 0)
                update = lax.dot_general(x, y, ATB, preferred_element_type=jnp.float32)
                used = (lane >= 32 * big) & (lane < after)
                for b in range(4 * big + 4, 16):
                    a[b] = jnp.where(used, 0.0, a[b]) - update[8 * b : 8 * b + 8]
    return [jnp.concatenate(a, 0) for a in tiles]


def mixing(cells, me_ref, core_ref, own_hbm, other_hbm, start_ref, high_ref, low_ref, *scratch):
    gram_ref, own_ref, other_ref, sems = scratch
    me, core = me_ref[0], core_ref[0]
    loads = [
        pltpu.make_async_copy(own_hbm, own_ref, sems.at[0]),
        pltpu.make_async_copy(other_hbm, other_ref, sems.at[1]),
    ]
    for copy in loads:
        copy.start()
    for copy in loads:
        copy.wait()
    for side in (0, 1):

        @pl.when(core == side)
        def _(side=side):
            for half, ref in enumerate((own_ref, other_ref) if side == 0 else (other_ref, own_ref)):
                rows = ref[:, 0:16].reshape(4, 128, 128)
                for i in range(4):
                    gram_ref[5 * half + i] = rows[i]
                for k in range(32):
                    gram_ref[5 * half + 4, 4 * k : 4 * k + 4] = ref[k, 16:20]

    odd = lax.rem(me, 2) == 1
    upper = me // 2

    def side(index, flip):
        x = gram_ref[index]
        return jnp.where(flip, x.T, x)

    def merged(coeff_parts, gram_parts):
        t = product(gram_parts, coeff_parts)
        return product(coeff_parts, parts_of(t), ATB)

    start = parts_of(start_ref[0].astype(jnp.float32), True)
    coeffs, inners = [], []
    for half in (0, 1):
        a, b = me ^ (2 * half), me ^ (2 * half + 1)
        near = side(4 + (upper ^ half), odd)
        gram = jnp.concatenate(
            [jnp.concatenate([gram_ref[a], near], 1), jnp.concatenate([near.T, gram_ref[b]], 1)], 0
        )
        gram = parts_of(gram)
        first = product(gram, start) / cells
        second = product(gram, parts_of(first)) / cells
        coeff = (second.astype(jnp.bfloat16),)
        coeffs.append(coeff)
        inners.append(merged(coeff, gram))
    inverse = inverse_factors(inners)
    scale = math.sqrt(cells)
    maps = [scale * product(c, parts_of(v), ABT) for c, v in zip(coeffs, inverse)]
    maps = [parts_of(m) for m in maps]
    low_group = upper == 0
    rows = []
    for e in (0, 1):
        line = []
        for f in (2, 3):
            a, b = me ^ e, me ^ f
            index = jnp.where(low_group, 6 + 2 * a + (b - 2), 6 + 2 * b + (a - 2))
            line.append(side(index, upper == 1))
        rows.append(jnp.concatenate(line, 1))
    across = parts_of(jnp.concatenate(rows, 0))
    cross = product(maps[0], parts_of(product(across, maps[1])), ATB)
    cross = parts_of(cross / cells)
    start = start_ref[1].astype(jnp.float32)
    top, bottom = start[:128], start[128:]
    exact = True
    for _ in range(2):
        top, bottom = (
            top + product(cross, parts_of(bottom, exact)),
            bottom + product(cross, parts_of(top, exact), ATB),
        )
        exact = False
    top, bottom = (top.astype(jnp.bfloat16),), (bottom.astype(jnp.bfloat16),)
    mixed = product(top, parts_of(product(cross, bottom)), ATB)
    inner = product(top, top, ATB) + product(bottom, bottom, ATB) + mixed + mixed.T
    (last,) = inverse_factors([inner])
    last = parts_of(last)
    for half, coeff in enumerate((top, bottom)):
        step = product(coeff, last, ABT)
        final = product(maps[half], parts_of(step))
        high = final.astype(jnp.bfloat16)
        high_ref[pl.ds(256 * half, 256), :] = high
        low_ref[pl.ds(256 * half, 256), :] = (final - high.astype(jnp.float32)).astype(jnp.bfloat16)


NY, LANES, PAD = 512, 128, 8
WIDE = PAD + NY + PAD
GROUP = 128
INNER, OUTER = 10 * GROUP, 6 * GROUP
PIECE = INNER + OUTER


def spread_faces(perm_ref, east, north, count):
    here = perm_ref[...]
    after = jnp.concatenate([here[1:], here[:1]], 0)
    row = lax.broadcasted_iota(jnp.int32, (256, 256), 0) & 127
    second = lax.broadcasted_iota(jnp.int32, (256, 256), 1) >> 7
    faces = []
    for value in (0.12 * (here + after), 0.12 * (here + pltpu.roll(here, LANES - 1, axis=1))):
        high = value.astype(jnp.bfloat16)
        low = (value - high.astype(jnp.float32)).astype(jnp.bfloat16)
        faces.append(jnp.concatenate([high, low], 1))
    for i in range(0, count, 2):
        pick = jnp.where(row == second + i, 1.0, 0.0).astype(jnp.bfloat16)
        for face, out in zip(faces, (east, north)):
            both = jnp.dot(face, pick, preferred_element_type=jnp.float32)
            out[i] = both[:, :LANES]
            if i + 1 < count:
                out[i + 1] = both[:, LANES:]


def set_perm(perm_ref, rows):
    count = rows.shape[0]
    rows = jnp.concatenate([rows, jnp.zeros((LANES - count, NY), jnp.float32)], 0)
    perm_ref[0:PAD] = jnp.zeros((PAD, LANES), jnp.float32)
    perm_ref[PAD : PAD + NY] = rows.T
    perm_ref[PAD + NY : WIDE] = jnp.zeros((PAD, LANES), jnp.float32)


def clear_pads(buf, count):
    def one(i, _):
        buf[i, 0:PAD] = jnp.zeros((PAD, LANES), jnp.float32)
        buf[i, PAD + NY : WIDE] = jnp.zeros((PAD, LANES), jnp.float32)
        return 0

    lax.fori_loop(0, count, one, 0)


def sweep(source, east, north, begin, face, count, write):
    for g in range(NY // GROUP):
        c = PAD + g * GROUP

        def one(i, carry, c=c, g=g):
            row, plane = begin + i, face + i
            center, south = carry
            above = source[row + 1, c : c + GROUP]
            up = north[plane, c : c + GROUP] * (above - center)
            east_here = east[plane, c : c + GROUP]
            flux = east_here * (source[row, c + 1 : c + GROUP + 1] - center)
            before = source[row, c - PAD : c]
            edge = east[plane, c - PAD : c] * (source[row, c - PAD + 1 : c + 1] - before)
            shifted = jnp.concatenate([edge, flux], 0)[PAD - 1 : PAD - 1 + GROUP]
            write(i, g, center + ((up - south) + (flux - shifted)))
            return above, up

        center = source[begin, c : c + GROUP]
        south = north[face - 1, c : c + GROUP] * (center - source[begin - 1, c : c + GROUP])
        lax.fori_loop(0, count, one, (center, south))


def into(buf, base):
    def write(i, g, value):
        buf[base + i, PAD + g * GROUP : PAD + g * GROUP + GROUP] = value

    return write


def into_snap(snap, base, scale_ref):
    scale = jnp.sqrt(jnp.full((8, LANES), scale_ref[0].astype(jnp.float32)))
    scale = jnp.broadcast_to(scale[0:1], (GROUP, LANES))

    def write(i, g, value):
        at0 = pl.multiple_of((base + i) * GROUP, GROUP)
        snap[g, pl.ds(at0, GROUP)] = (value * scale).astype(jnp.bfloat16)

    return write


def send_out(me, snap, singles, stacks, begin, size, sems):
    one, two, three = stacks
    moves = [(singles[e - 1], e, 0) for e in (1, 2, 3)]
    moves += [(one, j ^ 1, PIECE * (j - 1) + begin) for j in (1, 2, 3)]
    moves += [(two, 2, begin), (two, 1, PIECE + begin), (three, 0, begin)]
    copies = []
    for target, j, at0 in moves:
        copies.append(
            pltpu.make_async_copy(snap.at[me ^ j], target.at[pl.ds(at0, size)], sems.at[len(copies)])
        )
    for copy in copies:
        copy.start()
    return copies


def inner_rows(me_ref, scale_ref, own_ref, kp_ref, *refs):
    singles, stacks, edge_one, edge_two = refs[:3], refs[3:6], refs[6], refs[7]
    first, second, east, north, perm_ref, snap, held, sems, edge_sems = refs[8:]
    me = me_ref[0]
    load = pltpu.make_async_copy(own_ref, held, sems.at[0])
    load.start()
    clear_pads(first, 16)
    clear_pads(second, 16)

    def fill(i, _):
        first[i, PAD : PAD + NY] = held[i].astype(jnp.float32)
        return 0

    set_perm(perm_ref, kp_ref[...])
    spread_faces(perm_ref, east, north, 15)
    load.wait()
    lax.fori_loop(0, 16, fill, 0)
    sweep(first, east, north, 1, 1, 14, into(second, 1))
    sweep(second, east, north, 2, 2, 12, into(first, 2))
    edges_out = [
        pltpu.make_async_copy(second.at[pl.ds(1, 2)], edge_one.at[pl.ds(0, 2)], edge_sems.at[0]),
        pltpu.make_async_copy(second.at[pl.ds(13, 2)], edge_one.at[pl.ds(2, 2)], edge_sems.at[1]),
        pltpu.make_async_copy(first.at[pl.ds(2, 2)], edge_two.at[pl.ds(0, 2)], edge_sems.at[2]),
        pltpu.make_async_copy(first.at[pl.ds(12, 2)], edge_two.at[pl.ds(2, 2)], edge_sems.at[3]),
    ]
    for copy in edges_out:
        copy.start()
    sweep(first, east, north, 3, 3, 10, into_snap(snap, 0, scale_ref))
    for copy in edges_out + send_out(me, snap, singles, stacks, 0, INNER, sems):
        copy.wait()


def outer_rows(me_ref, tile_ref, scale_ref, own_hbm, kp_ref, low_hbm, high_hbm, edge_one, edge_two, *refs):
    singles, stacks = refs[3:6], refs[6:9]
    low0, low1, low2, high0, high1, high2, east, north, perm_ref, snap = refs[9:19]
    low_ref, high_ref, own_ref, sems, edge_sems = refs[19:]
    me, tile = me_ref[0], tile_ref[0]
    loads = [
        pltpu.make_async_copy(low_hbm, low_ref, sems.at[0]),
        pltpu.make_async_copy(high_hbm, high_ref, sems.at[1]),
        pltpu.make_async_copy(own_hbm.at[pl.ds(0, 2)], own_ref.at[pl.ds(0, 2)], sems.at[2]),
        pltpu.make_async_copy(own_hbm.at[pl.ds(14, 2)], own_ref.at[pl.ds(2, 2)], sems.at[3]),
    ]
    for copy in loads:
        copy.start()
    edges_in = [
        pltpu.make_async_copy(edge_one.at[pl.ds(0, 2)], low1.at[pl.ds(3, 2)], edge_sems.at[0]),
        pltpu.make_async_copy(edge_one.at[pl.ds(2, 2)], high1.at[pl.ds(0, 2)], edge_sems.at[1]),
        pltpu.make_async_copy(edge_two.at[pl.ds(0, 2)], low2.at[pl.ds(3, 2)], edge_sems.at[2]),
        pltpu.make_async_copy(edge_two.at[pl.ds(2, 2)], high2.at[pl.ds(0, 2)], edge_sems.at[3]),
    ]
    for copy in edges_in:
        copy.start()
    for buf in (low0, high0):
        clear_pads(buf, 5)
    for buf in (low1, low2):
        clear_pads(buf, 3)
    for buf in (high1, high2):
        clear_pads(buf.at[pl.ds(2, 3)], 3)
    for copy in loads:
        copy.wait()
    for i in range(3):
        low0[i, PAD : PAD + NY] = low_ref[NY * i : NY * i + NY].astype(jnp.float32)
        high0[2 + i, PAD : PAD + NY] = high_ref[NY * i : NY * i + NY].astype(jnp.float32)
    for i in range(2):
        low0[3 + i, PAD : PAD + NY] = own_ref[i].astype(jnp.float32)
        high0[i, PAD : PAD + NY] = own_ref[2 + i].astype(jnp.float32)

    def far_perm(ref):
        both = ref[3 * NY : 3 * NY + 32].astype(jnp.float32)
        packed = both[0:12] + both[12:24]
        return [
            jnp.concatenate([packed[4 * i + q : 4 * i + q + 1] for q in range(4)], 1) for i in range(3)
        ]

    kp = kp_ref[...]
    set_perm(perm_ref, jnp.concatenate(far_perm(low_ref) + [kp[0:4], kp[12:16]] + far_perm(high_ref), 0))
    spread_faces(perm_ref, east, north, 13)
    sweep(low0, east, north, 1, 1, 3, into(low1, 0))
    sweep(high0, east, north, 1, 10, 3, into(high1, 2))
    blank = jnp.zeros((NY, LANES), jnp.float32)

    @pl.when(tile == 0)
    def _():
        low1[0, PAD : PAD + NY] = blank
        low1[1, PAD : PAD + NY] = blank

    @pl.when(tile == 63)
    def _():
        high1[3, PAD : PAD + NY] = blank
        high1[4, PAD : PAD + NY] = blank

    for copy in edges_in:
        copy.wait()
    sweep(low1, east, north, 1, 2, 3, into(low2, 0))
    sweep(high1, east, north, 1, 9, 3, into(high2, 2))

    @pl.when(tile == 0)
    def _():
        low2[0, PAD : PAD + NY] = blank

    @pl.when(tile == 63)
    def _():
        high2[4, PAD : PAD + NY] = blank

    sweep(low2, east, north, 1, 3, 3, into_snap(snap, 0, scale_ref))
    sweep(high2, east, north, 1, 8, 3, into_snap(snap, 3, scale_ref))
    for copy in send_out(me, snap, singles, stacks, INNER, OUTER, sems):
        copy.wait()


VM = pl.BlockSpec(memory_space=pltpu.VMEM)
SM = pl.BlockSpec(memory_space=pltpu.SMEM)
ANY = pl.BlockSpec(memory_space=pl.ANY)


def half(rows):
    return jax.ShapeDtypeStruct((rows, LANES), jnp.bfloat16)


def planes(count):
    return pltpu.VMEM((count, WIDE, LANES), jnp.float32)


def inner_call(me, weights, own, kp):
    edge = jax.ShapeDtypeStruct((4, WIDE, LANES), jnp.float32)
    return pl.pallas_call(
        inner_rows,
        out_shape=[half(INNER)] * 3 + [half(3 * PIECE), half(2 * PIECE), half(PIECE)] + [edge] * 2,
        in_specs=[SM, SM, ANY, VM],
        out_specs=[ANY] * 8,
        scratch_shapes=[planes(16), planes(16), planes(15), planes(15)]
        + [pltpu.VMEM((WIDE, LANES), jnp.float32), pltpu.VMEM((4, INNER, LANES), jnp.bfloat16)]
        + [pltpu.VMEM((16, NY, LANES), jnp.bfloat16)]
        + [pltpu.SemaphoreType.DMA((12,)), pltpu.SemaphoreType.DMA((4,))],
        compiler_params=pltpu.CompilerParams(vmem_limit_bytes=63 << 20),
        cost_estimate=pl.CostEstimate(flops=400 << 20, bytes_accessed=9 << 20, transcendentals=0),
    )(me, weights, own, kp)


def outer_call(me, tile, weights, own, kp, low, high, edge_one, edge_two, stacks):
    return pl.pallas_call(
        outer_rows,
        out_shape=[half(OUTER)] * 3 + [half(3 * PIECE), half(2 * PIECE), half(PIECE)],
        in_specs=[SM, SM, SM, ANY, VM] + [ANY] * 7,
        out_specs=[ANY] * 6,
        input_output_aliases={9 + n: 3 + n for n in range(3)},
        scratch_shapes=[planes(5)] * 6
        + [planes(13), planes(13), pltpu.VMEM((WIDE, LANES), jnp.float32)]
        + [pltpu.VMEM((4, OUTER, LANES), jnp.bfloat16)]
        + [pltpu.VMEM((3 * NY + 32, LANES), jnp.bfloat16)] * 2
        + [pltpu.VMEM((4, NY, LANES), jnp.bfloat16)]
        + [pltpu.SemaphoreType.DMA((12,)), pltpu.SemaphoreType.DMA((4,))],
        compiler_params=pltpu.CompilerParams(vmem_limit_bytes=63 << 20),
        cost_estimate=pl.CostEstimate(flops=200 << 20, bytes_accessed=9 << 20, transcendentals=0),
    )(me, tile, weights, own, kp, low, high, edge_one, edge_two, *stacks)


def grams(me_ref, core_ref, *refs):
    pieces, own_ref, other_ref, wide, sems = refs[:7], refs[7], refs[8], refs[9], refs[10]
    me, core = me_ref[0], core_ref[0]
    copies = []
    for e in range(4):
        lanes = pl.ds(pl.multiple_of((me ^ e) * 128, 128), 128)
        if e == 0:
            moves = [(pieces[0].at[pl.ds(0, PIECE)], 0, PIECE)]
        else:
            moves = [(pieces[e], 0, INNER), (pieces[3 + e], INNER, OUTER)]
        for source, begin, size in moves:
            target = wide.at[pl.ds(begin, size), lanes]
            copies.append(pltpu.make_async_copy(source, target, sems.at[len(copies)]))
    for copy in copies:
        copy.start()
    for copy in copies:
        copy.wait()
    left, right = wide[:, :256], wide[:, 256:]
    near = lax.dot_general(left, left, ATB, preferred_element_type=jnp.float32)
    far = lax.dot_general(right, right, ATB, preferred_element_type=jnp.float32)
    cross = lax.dot_general(left, right, ATB, preferred_element_type=jnp.float32)
    blocks = [
        near[:128, :128], near[128:, 128:], far[:128, :128], far[128:, 128:], near[:128, 128:],
        far[:128, 128:], cross[:128, :128], cross[:128, 128:], cross[128:, :128], cross[128:, 128:],
    ]
    for side in (0, 1):

        @pl.when(core == side)
        def _(side=side):
            for half, ref in enumerate((own_ref, other_ref) if side == 0 else (other_ref, own_ref)):
                mine = blocks[5 * half : 5 * half + 5]
                ref[:, 0:16] = jnp.concatenate(mine[:4], 0).reshape(32, 16, 128)
                ref[:, 16:24] = jnp.zeros((32, 8, 128), jnp.float32)
                for k in range(32):
                    ref[k, 16:20] = mine[4][4 * k : 4 * k + 4]


def grams_call(me, core, pieces):
    shape = jax.ShapeDtypeStruct((32, 24, 128), jnp.float32)
    return pl.pallas_call(
        grams,
        out_shape=(shape, shape),
        in_specs=[SM, SM] + [ANY] * 7,
        out_specs=(VM, VM),
        scratch_shapes=[pltpu.VMEM((PIECE, 512), jnp.bfloat16), pltpu.SemaphoreType.DMA((7,))],
        compiler_params=pltpu.CompilerParams(vmem_limit_bytes=63 << 20),
        cost_estimate=pl.CostEstimate(flops=2 * 2048 * 512 * 512, bytes_accessed=3 << 20, transcendentals=0),
    )(me, core, *pieces)


def mixing_call(cells, me, core, own, other, start_codes):
    shape = jax.ShapeDtypeStruct((512, 128), jnp.bfloat16)
    vmem = pl.BlockSpec(memory_space=pltpu.VMEM)
    smem = pl.BlockSpec(memory_space=pltpu.SMEM)
    return pl.pallas_call(
        functools.partial(mixing, cells),
        out_shape=(shape, shape),
        in_specs=[smem, smem, ANY, ANY, vmem],
        out_specs=(vmem, vmem),
        scratch_shapes=[pltpu.VMEM((10, 128, 128), jnp.float32)]
        + [pltpu.VMEM((32, 24, 128), jnp.float32)] * 2
        + [pltpu.SemaphoreType.DMA((2,))],
        compiler_params=pltpu.CompilerParams(vmem_limit_bytes=62 << 20),
        cost_estimate=pl.CostEstimate(flops=1 << 30, bytes_accessed=1 << 20, transcendentals=0),
    )(me, core, own, other, start_codes)


def finish(plan, me_ref, high_ref, low_ref, *refs):
    pieces, out_ref = refs[:-5], refs[-5]
    wide, done, in_sems, out_sems = refs[-4:]
    me = me_ref[0]
    loads = []
    for j in range(4):
        group = []
        for e in range(4):
            for index, source, target, size in plan[4 * j + e]:
                group.append(
                    pltpu.make_async_copy(
                        pieces[index].at[pl.ds(source, size)],
                        wide.at[j, pl.ds(target, size), pl.ds(128 * e, 128)],
                        in_sems.at[len(loads), len(group)],
                    )
                )
                group[-1].start()
        loads.append(group)
    mix = jnp.concatenate([high_ref[...], low_ref[...]], 1)
    stores = []
    for j in range(4):
        for copy in loads[j]:
            copy.wait()
        for r in range(0, 16, 4):
            both = jnp.dot(wide[j, 128 * r : 128 * r + 512], mix, preferred_element_type=jnp.float32)
            done[j, r : r + 4] = (both[:, :128] + both[:, 128:]).astype(jnp.bfloat16).reshape(4, GROUP, LANES)
        columns = pl.ds(pl.multiple_of((me ^ j) * GROUP, GROUP), GROUP)
        for n, (source, target, size) in enumerate(((0, 3, 10), (10, 0, 3), (13, 13, 3))):
            copy = pltpu.make_async_copy(
                done.at[j, pl.ds(source, size)], out_ref.at[pl.ds(target, size), columns], out_sems.at[j, n]
            )
            copy.start()
            stores.append(copy)
    for copy in stores:
        copy.wait()


def finish_call(me, high, low, pieces, plan):
    return pl.pallas_call(
        functools.partial(finish, plan),
        out_shape=jax.ShapeDtypeStruct((16, NY, LANES), jnp.bfloat16),
        in_specs=[SM, VM, VM] + [ANY] * len(pieces),
        out_specs=ANY,
        scratch_shapes=[
            pltpu.VMEM((4, PIECE, 512), jnp.bfloat16),
            pltpu.VMEM((4, 16, GROUP, LANES), jnp.bfloat16),
            pltpu.SemaphoreType.DMA((4, 8)),
            pltpu.SemaphoreType.DMA((4, 3)),
        ],
        compiler_params=pltpu.CompilerParams(vmem_limit_bytes=63 << 20),
        cost_estimate=pl.CostEstimate(flops=2 * 8192 * 512 * 256, bytes_accessed=10 << 20, transcendentals=0),
    )(me, high, low, *pieces)


def packed_edge(cells, perm):
    high = perm.astype(jnp.bfloat16)
    low = (perm - high.astype(jnp.float32)).astype(jnp.bfloat16)
    parts = [cells.reshape(-1, LANES), high.reshape(-1, LANES), low.reshape(-1, LANES)]
    return jnp.concatenate(parts + [jnp.zeros((8, LANES), jnp.bfloat16)], 0)


def merged_bases(forcing, permeability, merge_weights, start_codes):
    me = lax.axis_index("case").astype(jnp.int32).reshape(1)
    tile = lax.axis_index("tile").astype(jnp.int32).reshape(1)
    core = tile & 1
    cells = forcing.shape[1] * lax.axis_size("tile") * forcing.shape[2]
    own, kp = forcing[0], permeability[0]
    up = [(i, i + 1) for i in range(63)]
    down = [(i + 1, i) for i in range(63)]
    low = lax.ppermute(packed_edge(own[-STEPS:], kp[-STEPS:]), "tile", up)
    high = lax.ppermute(packed_edge(own[:STEPS], kp[:STEPS]), "tile", down)
    inner = inner_call(me, merge_weights, own, kp)
    met = [case_swap(inner[e - 1], e) for e in (1, 2, 3)]
    outer = outer_call(me, tile, merge_weights, own, kp, low, high, inner[6], inner[7], inner[3:6])
    one, two, three = outer[3:]
    met = met + [case_swap(outer[e - 1], e) for e in (1, 2, 3)]
    far_one, far_two, far_three = case_swap(one, 1), case_swap(two, 3), case_swap(three, 3)
    via_one = [case_swap(met[2], 1), case_swap(met[5], 1), case_swap(far_three, 1)]
    via_three = [case_swap(met[0], 3), case_swap(met[3], 3)]
    own_part, other_part = grams_call(me, core, [one] + met)
    part = own_part + core_swap(other_part)
    part = plane_exchange(part).sum(0)
    part = part + case_swap(part, 1) + case_swap(part, 2) + case_swap(part, 3)
    mine = plane_exchange(jnp.broadcast_to(part, (32,) + part.shape))
    yours = core_swap(mine)
    high, low = mixing_call(cells, me, core, mine, yours, start_codes)
    pieces = [one, two, three] + met + [far_one, far_two, far_three] + via_one + via_three
    whole = ((0, PIECE),)
    split = ((0, INNER), (INNER, OUTER))
    places = {
        (0, 0): [(0, 0)], (0, 1): [(1, PIECE)], (0, 2): [(0, 2 * PIECE)], (0, 3): [(0, PIECE)],
        (1, 0): [(3, 0), (6, 0)], (2, 0): [(4, 0), (7, 0)], (3, 0): [(5, 0), (8, 0)],
        (1, 1): [(9, 0)], (1, 2): [(9, PIECE)], (1, 3): [(9, 2 * PIECE)],
        (3, 1): [(10, 0)], (3, 2): [(10, PIECE)], (3, 3): [(11, 0)],
        (2, 1): [(12, 0), (13, 0)], (2, 2): [(14, 0)], (2, 3): [(15, 0), (16, 0)],
    }
    plan = []
    for j in range(4):
        for e in range(4):
            sources = places[e, j]
            spans = whole if len(sources) == 1 else split
            plan.append(tuple((i, b, t, n) for (i, b), (t, n) in zip(sources, spans)))
    return finish_call(me, high, low, pieces, tuple(plan)).reshape(1, -1, LANES)


def solution(mesh):
    placed = (P("case", "tile", None, None), P("case", "tile", None), P("case"), P())
    return jax.shard_map(merged_bases, mesh=mesh, in_specs=placed, out_specs=P("case", "tile", None), check_vma=False)
```
